32 devices in a mesh: dp: 8 (over y, x, core), tensor: 4 (over z).
Axes of the slice: x: 2, y: 2, z: 4, core: 2. Of those that a mesh axis runs over, the one named last changes fastest.
Arguments:
- inputs: bfloat16 [32768, 768], P('dp'), may hold values from -6 to 6
- segments: int32 [64, 512], P('dp'), may hold values from 0 to 7, never falling along the last dimension, each value on 1 to 128 neighbouring positions
- w_query: bfloat16 [768, 768], P(None, 'tensor'), may hold values from -0.21875 to 0.21875
- w_key: bfloat16 [768, 768], P(None, 'tensor'), may hold values from -0.21875 to 0.21875
- w_value: bfloat16 [768, 768], P(None, 'tensor'), may hold values from -0.21875 to 0.21875
- b_query: bfloat16 [768], P('tensor'), may hold values from -3 to 3
- b_value: bfloat16 [768], P('tensor'), may hold values from -3 to 3
- w_output: bfloat16 [768, 768], P('tensor'), may hold values from -0.875 to 0.875
- b_output: bfloat16 [768], replicated, may hold values from -3 to 3
- gain_attn: bfloat16 [768], replicated, may hold values from 0.5 to 1.5
- shift_attn: bfloat16 [768], replicated, may hold values from -3 to 3
- w_hidden: bfloat16 [768, 3072], P(None, 'tensor'), may hold values from -0.21875 to 0.21875
- b_hidden: bfloat16 [3072], P('tensor'), may hold values from -3 to 3
- w_project: bfloat16 [3072, 768], P('tensor'), may hold values from -0.109375 to 0.109375
- b_project: bfloat16 [768], replicated, may hold values from -3 to 3
- gain_ffn: bfloat16 [768], replicated, may hold values from 0.5 to 1.5
- shift_ffn: bfloat16 [768], replicated, may hold values from -3 to 3
- cotangent: bfloat16 [32768, 768], P(('dp', 'tensor')), may hold values from -6 to 6
Outputs:
- output: bfloat16 [32768, 768], P(('dp', 'tensor'))
- grad_input: float32 [32768, 768], P(('dp', 'tensor'))
- grad_w_query: float32 [768, 768], P('dp', 'tensor')
- grad_w_key: float32 [768, 768], P('dp', 'tensor')
- grad_w_value: float32 [768, 768], P('dp', 'tensor')
- grad_w_output: float32 [768, 768], P('tensor', 'dp')
- grad_w_hidden: float32 [768, 3072], P('dp', 'tensor')
- grad_w_project: float32 [3072, 768], P('tensor', 'dp')
- grad_bias_qv: float32 [2, 12, 64], P(None, 'tensor', 'dp')
- grad_b_hidden: float32 [48, 64], P('tensor', 'dp')
- grad_vectors: float32 [6, 768], P(None, ('dp', 'tensor'))
The draws below stay inside these ranges and needn't reach their ends.
Inputs may be any that keep to these rules, and one draw needn't show every extreme that they name: `segments`: within each row of 512 tokens segment numbers never fall; each text holds 1 to 128 tokens, and some text holds exactly 128.
All inputs are finite; a program needn't handle non-finite values.
Results may differ from the reference program's by a relative error of at most 0.014.
Values may be sent and summed in bfloat16 or wider, within the bound.
A program may use at most 192 MiB of HBM per device.

```python
import math
import jax
import jax.numpy as jnp
import numpy as np
from jax import lax

D = 768
HEADS = 12
HD = 64
FF = 3072
SEQ = 512
SEGS = 8
ROWS_DEV = 8
ROWS = 64
TOKENS = 32768


def steps_of(key, shape, split, low, top_value):
    loudness = 1.0
    for position, parts in split:
        steps = jax.random.uniform(jax.random.fold_in(jax.random.fold_in(key, 6), position), (parts,), jnp.float32, low / len(split), top_value / len(split))
        loudness = loudness * jnp.repeat(jnp.exp(steps), shape[position] // parts).reshape((-1,) + (1,) * (len(shape) - 1 - position))
    return loudness


def length_profile(number_of, total, most, lean):
    loads = [(1 << 20) // math.isqrt(rank ** lean) + 1 for rank in range(2, number_of + 1)]
    rest, holding = total - most - (number_of - 1), [1] * (number_of - 1)
    while rest > 0:
        candidates = [i for i in range(number_of - 1) if holding[i] < most]
        pool, left = sum([loads[i] for i in candidates]), rest
        for i in candidates:
            extra = min(most - holding[i], max(1, left * loads[i] // pool), rest)
            holding[i] = holding[i] + extra
            rest = rest - extra
    return np.array([most] + holding)


def uneven_parts(key, number_of, total, reach, slope):
    if number_of == 2:
        one = jax.random.randint(key, (), max(1, total - reach), min(reach, total - 1) + 1)
        return jnp.stack([one, total - one])
    lengths = jnp.asarray(length_profile(number_of, total, reach, slope), jnp.int32)
    pairs = (number_of - 1) // 2
    giver, receiver = lengths[1:1 + 2 * pairs:2], lengths[2:2 + 2 * pairs:2]
    room = jnp.minimum(giver - 1, reach - receiver)
    moved = jax.random.randint(jax.random.fold_in(key, 1), (pairs,), 0, 1 << 20) % (room + 1)
    lengths = lengths.at[1:1 + 2 * pairs:2].set(giver - moved).at[2:2 + 2 * pairs:2].set(receiver + moved)
    return lengths[jax.random.permutation(jax.random.fold_in(key, 2), number_of)]


def scatter_about(key, shape, deviation, reach, split=(), kind=jnp.bfloat16):
    result = jax.random.normal(key, shape, jnp.float32) * deviation
    if len(split) > 0:
        result = steps_of(key, shape, split, -0.22, 0.18) * result
    return jnp.clip(result, min=-reach, max=reach).astype(kind)


def setup_inputs(seed: int = 0) -> dict:
    splits = jax.random.split(jax.random.key(seed), 19)
    inputs = scatter_about(splits[0], (TOKENS, D), 1.0, 6.0, ((0, 8),))
    segments = jax.vmap(lambda own: jnp.searchsorted(jnp.cumsum(uneven_parts(own, SEGS, SEQ, SEQ // 4, 0)), jnp.arange(SEQ), side="right"))(jax.random.split(splits[1], ROWS)).reshape((ROWS, SEQ)).astype(jnp.int32)
    w_query = scatter_about(splits[2], (D, D), D ** -0.5, 0.21875, ((1, 4),))
    w_key = scatter_about(splits[3], (D, D), D ** -0.5, 0.21875, ((1, 4),))
    w_value = scatter_about(splits[4], (D, D), D ** -0.5, 0.21875, ((1, 4),))
    b_query = scatter_about(splits[5], (D,), 0.5, 3.0, ((0, 4),))
    b_value = scatter_about(splits[6], (D,), 0.5, 3.0, ((0, 4),))
    w_output = scatter_about(splits[7], (D, D), (D // 16) ** -0.5, 0.875, ((0, 4),))
    b_output = scatter_about(splits[8], (D,), 0.5, 3.0)
    gain_attn = jnp.clip(1.0 + 0.1 * jax.random.normal(splits[9], (D,), jnp.float32), 0.5, 1.5).astype(jnp.bfloat16)
    shift_attn = scatter_about(splits[10], (D,), 0.5, 3.0)
    w_hidden = scatter_about(splits[11], (D, FF), D ** -0.5, 0.21875, ((1, 4),))
    b_hidden = scatter_about(splits[12], (FF,), 0.5, 3.0, ((0, 4),))
    w_project = scatter_about(splits[13], (FF, D), FF ** -0.5, 0.109375, ((0, 4),))
    b_project = scatter_about(splits[14], (D,), 0.5, 3.0)
    gain_ffn = jnp.clip(1.0 + 0.1 * jax.random.normal(splits[15], (D,), jnp.float32), 0.5, 1.5).astype(jnp.bfloat16)
    shift_ffn = scatter_about(splits[16], (D,), 0.5, 3.0)
    cotangent = scatter_about(splits[17], (TOKENS, D), 1.0, 6.0, ((0, 32),))
    return {"inputs": inputs, "segments": segments, "w_query": w_query, "w_key": w_key, "w_value": w_value, "b_query": b_query, "b_value": b_value, "w_output": w_output, "b_output": b_output, "gain_attn": gain_attn, "shift_attn": shift_attn, "w_hidden": w_hidden, "b_hidden": b_hidden, "w_project": w_project, "b_project": b_project, "gain_ffn": gain_ffn, "shift_ffn": shift_ffn, "cotangent": cotangent}


@jax.custom_vjp
def low(v):
    return lax.optimization_barrier(v.astype(jnp.bfloat16)).astype(jnp.float32)

@jax.custom_vjp
def low_back(v):
    return v

def low_keep(v):
    return (low(v), None)

def low_pass(kept, grad):
    return (grad,)

def back_keep(v):
    return (v, None)

def back_low(kept, grad):
    return (low(grad),)
low.defvjp(low_keep, low_pass)
low_back.defvjp(back_keep, back_low)
highest_precision = lax.Precision.HIGHEST
norm_epsilon = 1e-12
root_half = 0.7071067811865476

def layer_norm(values, norm_gain, norm_shift):
    average = lax.optimization_barrier(jnp.mean(values, axis=-1, keepdims=True))
    centered = values - average
    variance = lax.optimization_barrier(jnp.mean(centered * centered, axis=-1, keepdims=True))
    return centered * lax.rsqrt(variance + norm_epsilon) * norm_gain + norm_shift

def gelu_exact(values):
    return 0.5 * values * (1.0 + lax.erf(values * root_half))

def attend(queries, keys_in, values, segment_row):
    same_text = segment_row[:, None] == segment_row[None, :]
    scores = jnp.einsum('qhd,khd->hqk', queries, keys_in, precision=highest_precision) * HD ** (-0.5)
    scores = low_back(scores)
    scores = jnp.where(same_text[None], scores, -1000000000.0)
    row_max = lax.optimization_barrier(jnp.max(scores, axis=-1, keepdims=True))
    exponent = jnp.exp(scores - row_max)
    attn_probs = low(exponent / lax.optimization_barrier(jnp.sum(exponent, axis=-1, keepdims=True)))
    return jnp.einsum('hqk,khd->qhd', attn_probs, values, precision=highest_precision)

def block_forward(params, inputs, segment_block):
    w_query, w_key, w_value, b_query, b_value, w_output, b_output, gain_attn, shift_attn, w_hidden, b_hidden, w_project, b_project, gain_ffn, shift_ffn = params
    row_total = inputs.shape[0]
    head_shape = (row_total // SEQ, SEQ, HEADS, HD)
    queries = low_back(low(jnp.dot(inputs, w_query, precision=highest_precision) + b_query))
    keys_in = low_back(low(jnp.dot(inputs, w_key, precision=highest_precision)))
    values = low_back(low(jnp.dot(inputs, w_value, precision=highest_precision) + b_value))
    mixed_heads = jax.vmap(attend)(queries.reshape(head_shape), keys_in.reshape(head_shape), values.reshape(head_shape), segment_block)
    mixed_heads = low_back(low(mixed_heads.reshape(row_total, D)))
    branch = low_back(jnp.dot(mixed_heads, w_output, precision=highest_precision) + b_output)
    normed = layer_norm(inputs + branch, gain_attn, shift_attn)
    hidden_pre = low_back(jnp.dot(low(normed), w_hidden, precision=highest_precision) + b_hidden)
    active = low(gelu_exact(hidden_pre))
    second = low_back(jnp.dot(active, w_project, precision=highest_precision) + b_project)
    return layer_norm(normed + second, gain_ffn, shift_ffn)

def reference(inputs, segments, w_query, w_key, w_value, b_query, b_value, w_output, b_output, gain_attn, shift_attn, w_hidden, b_hidden, w_project, b_project, gain_ffn, shift_ffn, cotangent):
    given = (w_query, w_key, w_value, b_query, b_value, w_output, b_output, gain_attn, shift_attn, w_hidden, b_hidden, w_project, b_project, gain_ffn, shift_ffn)
    params = tuple((matrix.astype(jnp.float32) for matrix in given))
    block_rows = ROWS_DEV * SEQ
    input_blocks = inputs.astype(jnp.float32).reshape(-1, block_rows, D)
    segment_blocks = segments.reshape(-1, ROWS_DEV, SEQ)
    checked = jax.checkpoint(block_forward)

    def forward(all_inputs, *all_params):

        def one_block(carry, pair):
            return (carry, checked(all_params, pair[0], pair[1]))
        carry_out, results = lax.scan(one_block, jnp.zeros((), jnp.float32), (all_inputs, segment_blocks))
        return results
    primal, pullback = jax.vjp(forward, input_blocks, *params)
    grads = pullback(cotangent.astype(jnp.float32).reshape(-1, block_rows, D))
    output = primal.reshape(TOKENS, D).astype(jnp.bfloat16)
    grad_input = grads[0].reshape(TOKENS, D)
    grad_bias_qv = jnp.stack([grads[4], grads[5]]).reshape(2, HEADS, HD)
    grad_b_hidden = grads[11].reshape(FF // HD, HD)
    grad_vectors = jnp.stack([grads[8], grads[9], grads[7], grads[14], grads[15], grads[13]])
    return (output, grad_input, grads[1], grads[2], grads[3], grads[6], grads[10], grads[12], grad_bias_qv, grad_b_hidden, grad_vectors)
```

```python
import jax
import jax.numpy as jnp
from jax import lax
from jax.sharding import PartitionSpec as P

HD = 64


norm_epsilon = 1e-12
root_half = 0.7071067811865476


def norm_forward(values, norm_gain, norm_shift):
    average = jnp.mean(values, axis=-1, keepdims=True)
    centered = values - average
    variance = jnp.mean(centered * centered, axis=-1, keepdims=True)
    inverse = lax.rsqrt(variance + norm_epsilon)
    scaled = centered * inverse
    return (scaled * norm_gain + norm_shift, scaled, inverse)


def norm_backward(grad_out, scaled, inverse, norm_gain):
    weighted = grad_out * norm_gain
    mean_grad = jnp.mean(weighted, axis=-1, keepdims=True)
    mean_proj = jnp.mean(weighted * scaled, axis=-1, keepdims=True)
    return inverse * (weighted - mean_grad - scaled * mean_proj)


def gelu_exact(values):
    return 0.5 * values * (1.0 + lax.erf(values * root_half))


def cross_rows(left, right):
    return lax.dot_general(
        left, right, (((0,), (0,)), ((), ())), preferred_element_type=jnp.float32
    )


def times_transposed(left, right):
    return lax.dot_general(
        left, right, (((1,), (1,)), ((), ())), preferred_element_type=jnp.float32
    )


def masked_scores(queries, keys_in, segment_row):
    same_text = segment_row[:, None] == segment_row[None, :]
    scores = jnp.einsum("qhd,khd->hqk", queries, keys_in, preferred_element_type=jnp.float32)
    scores = scores * queries.shape[2] ** (-0.5)
    return jnp.where(same_text[None], scores, -1000000000.0)


def attend_forward(packed):
    queries, keys_in, values, segment_row = packed
    scores = masked_scores(queries, keys_in, segment_row)
    row_max = jnp.max(scores, axis=-1, keepdims=True)
    exponent = jnp.exp(scores - row_max)
    row_total = jnp.sum(exponent, axis=-1, keepdims=True)
    attn_probs = (exponent / row_total).astype(jnp.bfloat16)
    mixed_heads = jnp.einsum("hqk,khd->qhd", attn_probs, values, preferred_element_type=jnp.float32)
    return (mixed_heads.astype(jnp.bfloat16), row_max + jnp.log(row_total))


def attend_backward(packed):
    queries, keys_in, values, segment_row, logsum, grad_mixed = packed
    score_scale = queries.shape[2] ** (-0.5)
    scores = masked_scores(queries, keys_in, segment_row)
    attn_probs = jnp.exp(scores - logsum)
    grad_probs = jnp.einsum("qhd,khd->hqk", grad_mixed, values, preferred_element_type=jnp.float32)
    grad_values = jnp.einsum(
        "hqk,qhd->khd",
        attn_probs.astype(jnp.bfloat16),
        grad_mixed,
        preferred_element_type=jnp.float32,
    )
    inner_sum = jnp.sum(attn_probs * grad_probs, axis=-1, keepdims=True)
    grad_scores = (attn_probs * (grad_probs - inner_sum)).astype(jnp.bfloat16)
    grad_queries = (
        jnp.einsum("hqk,khd->qhd", grad_scores, keys_in, preferred_element_type=jnp.float32)
        * score_scale
    )
    grad_keys = (
        jnp.einsum("hqk,qhd->khd", grad_scores, queries, preferred_element_type=jnp.float32)
        * score_scale
    )
    return (
        grad_queries.astype(jnp.bfloat16),
        grad_keys.astype(jnp.bfloat16),
        grad_values.astype(jnp.bfloat16),
    )


def per_device(
    inputs,
    segments,
    w_query,
    w_key,
    w_value,
    b_query,
    b_value,
    w_output,
    b_output,
    gain_attn,
    shift_attn,
    w_hidden,
    b_hidden,
    w_project,
    b_project,
    gain_ffn,
    shift_ffn,
    cotangent,
):
    seq_len = segments.shape[1]
    share_tokens = cotangent.shape[0]
    share_rows = share_tokens // seq_len
    width = inputs.shape[1]
    groups, parts = lax.axis_size("tensor"), lax.axis_size("dp")
    place, part = lax.axis_index("tensor"), lax.axis_index("dp")
    everyone = ("tensor", "dp")
    low = jnp.bfloat16
    wide = jnp.float32

    def gathered(shard):
        rows = shard.shape[0] // parts
        piece = lax.dynamic_slice_in_dim(shard, part * rows, rows, 0)
        return lax.all_gather(piece, everyone, axis=0, tiled=True)

    def bias_of(shard):
        return lax.all_gather(shard, "tensor", axis=0, tiled=True).astype(wide)

    tokens = lax.dynamic_slice_in_dim(inputs, place * share_tokens, share_tokens, 0)
    rows_segments = lax.dynamic_slice_in_dim(segments, place * share_rows, share_rows, 0)
    split = w_query.shape[1]
    w_in = gathered(jnp.concatenate([w_query, w_key, w_value], axis=1))
    w_in = w_in.reshape(groups, width, 3, split).transpose(1, 2, 0, 3).reshape(width, 3 * groups * split)
    w_out = gathered(w_output)
    w_up = gathered(w_hidden).reshape(groups, width, -1).transpose(1, 0, 2).reshape(width, -1)
    w_down = gathered(w_project)
    small = bias_of(jnp.concatenate([b_query, b_value, b_hidden])).reshape(groups, -1)
    bias_query = small[:, :split].reshape(-1)
    bias_value = small[:, split : 2 * split].reshape(-1)
    bias_hidden = small[:, 2 * split :].reshape(-1)
    full = groups * split
    head_shape = (share_rows, seq_len, full // HD, HD)

    attn_gain = gain_attn.astype(wide)
    attn_shift = shift_attn.astype(wide)
    attn_bias = b_output.astype(wide)
    ffn_gain = gain_ffn.astype(wide)
    ffn_shift = shift_ffn.astype(wide)
    ffn_bias = b_project.astype(wide)
    grad_out = cotangent.astype(wide)

    projected = jnp.dot(tokens, w_in, preferred_element_type=wide)
    queries = (projected[:, :full] + bias_query).astype(low)
    keys_in = projected[:, full : 2 * full].astype(low)
    values = (projected[:, 2 * full :] + bias_value).astype(low)
    query_heads = queries.reshape(head_shape)
    key_heads = keys_in.reshape(head_shape)
    value_heads = values.reshape(head_shape)
    mixed_heads, logsum = lax.map(attend_forward, (query_heads, key_heads, value_heads, rows_segments))
    mixed = mixed_heads.reshape(share_tokens, full)
    hidden = tokens.astype(wide) + (jnp.dot(mixed, w_out, preferred_element_type=wide) + attn_bias)
    normed, scaled, inverse = norm_forward(hidden, attn_gain, attn_shift)
    normed_low = normed.astype(low)
    hidden_pre = jnp.dot(normed_low, w_up, preferred_element_type=wide) + bias_hidden
    active, gelu_pull = jax.vjp(gelu_exact, hidden_pre)
    active_low = active.astype(low)
    block_sum = normed + (jnp.dot(active_low, w_down, preferred_element_type=wide) + ffn_bias)
    output, scaled_out, inverse_out = norm_forward(block_sum, ffn_gain, ffn_shift)
    grad_sum = norm_backward(grad_out, scaled_out, inverse_out, ffn_gain)
    grad_ffn_gain = jnp.sum(grad_out * scaled_out, axis=0)
    grad_ffn_shift = jnp.sum(grad_out, axis=0)
    grad_sum_low = grad_sum.astype(low)
    grad_ffn_bias = jnp.sum(grad_sum_low.astype(wide), axis=0)
    grad_active = times_transposed(grad_sum_low, w_down)
    grad_w_down = cross_rows(grad_sum_low, active_low)
    grad_hidden_pre = gelu_pull(grad_active)[0].astype(low)
    grad_b_hidden = jnp.sum(grad_hidden_pre.astype(wide), axis=0)
    grad_w_up = cross_rows(normed_low, grad_hidden_pre)
    grad_normed = grad_sum + times_transposed(grad_hidden_pre, w_up)
    grad_hidden = norm_backward(grad_normed, scaled, inverse, attn_gain)
    grad_hidden_low = grad_hidden.astype(low)
    grad_attn_gain = jnp.sum(grad_normed * scaled, axis=0)
    grad_attn_shift = jnp.sum(grad_normed, axis=0)
    grad_attn_bias = jnp.sum(grad_hidden_low.astype(wide), axis=0)
    grad_w_out = cross_rows(grad_hidden_low, mixed)
    grad_mixed = times_transposed(grad_hidden_low, w_out).astype(low).reshape(head_shape)
    grad_q, grad_k, grad_v = lax.map(
        attend_backward, (query_heads, key_heads, value_heads, rows_segments, logsum, grad_mixed)
    )
    grad_q = grad_q.reshape(share_tokens, full)
    grad_k = grad_k.reshape(share_tokens, full)
    grad_v = grad_v.reshape(share_tokens, full)
    grad_projected = jnp.concatenate([grad_q, grad_k, grad_v], axis=1)
    grad_w_in = cross_rows(tokens, grad_projected)
    grad_b_query = jnp.sum(grad_q.astype(wide), axis=0)
    grad_b_value = jnp.sum(grad_v.astype(wide), axis=0)
    grad_input = grad_hidden + times_transposed(grad_projected, w_in)

    def scattered(grad):
        rows = grad.shape[0]
        grad = grad.reshape(rows, groups, -1).transpose(1, 0, 2).reshape(groups * rows, -1)
        return lax.psum_scatter(grad, everyone, scatter_dimension=0, tiled=True)

    sum_down = scattered(grad_w_down).T
    sum_up = scattered(grad_w_up)
    sum_out = scattered(grad_w_out).T
    sum_in = scattered(
        grad_w_in.reshape(width, 3, groups, split).transpose(0, 2, 1, 3).reshape(width, -1)
    )
    vectors = jnp.concatenate(
        [
            jnp.stack([grad_b_query, grad_b_value]).reshape(2 * groups, split),
            grad_b_hidden.reshape(-1, split),
            jnp.stack(
                [
                    grad_attn_gain,
                    grad_attn_shift,
                    grad_attn_bias,
                    grad_ffn_gain,
                    grad_ffn_shift,
                    grad_ffn_bias,
                ]
            ).reshape(-1, split),
        ],
        axis=0,
    )
    vectors = lax.psum(vectors, ("dp", "tensor"))
    bias_qv = vectors[: 2 * groups].reshape(2, groups, split // HD, HD)
    rest = vectors[2 * groups :]
    hid = bias_hidden.shape[0] // split
    bias_h = rest[:hid].reshape(groups, -1, HD)
    vec = rest[hid:].reshape(6, -1)
    piece = HD // parts
    bias_qv = lax.dynamic_slice_in_dim(bias_qv, place, 1, 1)[:, 0]
    bias_qv = lax.dynamic_slice_in_dim(bias_qv, part * piece, piece, 2)
    bias_h = lax.dynamic_slice_in_dim(bias_h, place, 1, 0)[0]
    bias_h = lax.dynamic_slice_in_dim(bias_h, part * piece, piece, 1)
    piece = width // (parts * groups)
    vec = lax.dynamic_slice_in_dim(vec, (part * groups + place) * piece, piece, 1)
    return (
        output.astype(low),
        grad_input,
        sum_in[:, :split],
        sum_in[:, split : 2 * split],
        sum_in[:, 2 * split :],
        sum_out,
        sum_up,
        sum_down,
        bias_qv,
        bias_h,
        vec,
    )


def solution(mesh):
    in_specs = (
        P("dp", None),
        P("dp", None),
        P(None, "tensor"),
        P(None, "tensor"),
        P(None, "tensor"),
        P("tensor"),
        P("tensor"),
        P("tensor", None),
        P(),
        P(),
        P(),
        P(None, "tensor"),
        P("tensor"),
        P("tensor", None),
        P(),
        P(),
        P(),
        P(("dp", "tensor"), None),
    )
    out_specs = (
        P(("dp", "tensor"), None),
        P(("dp", "tensor"), None),
        P("dp", "tensor"),
        P("dp", "tensor"),
        P("dp", "tensor"),
        P("tensor", "dp"),
        P("dp", "tensor"),
        P("tensor", "dp"),
        P(None, "tensor", "dp"),
        P("tensor", "dp"),
        P(None, ("dp", "tensor")),
    )
    return jax.shard_map(
        per_device, mesh=mesh, in_specs=in_specs, out_specs=out_specs, check_vma=False
    )
```

```python
import functools
import jax
import jax.numpy as jnp
from jax import lax
from jax.experimental import pallas as pl
from jax.experimental.pallas import tpu as pltpu
from jax.sharding import PartitionSpec as P

HD = 64
MESH = pl.DeviceIdType.MESH
LOW = jnp.bfloat16


class Place:
    def __init__(self, groups, parts):
        self.groups, self.parts = groups, parts
        self.t, self.d = lax.axis_index("tensor"), lax.axis_index("dp")
        self.count = parts.bit_length() - 1
        self.bits = [(self.d // (1 << i)) % 2 for i in range(self.count)]

    def partner(self, bit):
        return (self.d + (1 - 2 * self.bits[bit]) * (1 << bit), self.t)

    def along(self, step):
        return (self.d, (self.t + step) % self.groups)

    def enter(self):
        barrier = pltpu.get_barrier_semaphore()
        peers = [self.partner(b) for b in range(self.count)]
        peers += [self.along(j) for j in range(1, self.groups)]
        for peer in peers:
            pl.semaphore_signal(barrier, inc=1, device_id=peer, device_id_type=MESH)
        pl.semaphore_wait(barrier, len(peers))

    def pieces(self, open_bits, flipped=None):
        index = []
        for bit in reversed(range(self.count)):
            own = self.bits[bit]
            index.append(slice(None) if bit in open_bits else 1 - own if bit == flipped else own)
        return tuple(index)


def send(src, dst, sems, slot, peer):
    return pltpu.make_async_remote_copy(
        src_ref=src,
        dst_ref=dst,
        send_sem=sems[0].at[slot],
        recv_sem=sems[1].at[slot],
        device_id=peer,
        device_id_type=MESH,
    )


def orders(count):
    rest = list(range(1, count))
    return [rest, rest[::-1]]


def gather_kernel(groups, parts, arrays, *refs):
    shards, small = refs[:arrays], refs[arrays]
    outs, small_out = refs[arrays + 1 : 2 * arrays + 1], refs[2 * arrays + 1]
    held, small_held = refs[2 * arrays + 2 : 3 * arrays + 2], refs[3 * arrays + 2]
    load_sem, store_sem, z_send, z_recv, x_send, x_recv, s_send, s_recv = refs[3 * arrays + 3 :]
    me = Place(groups, parts)
    n = me.count
    half = shards[0].shape[-1] // 2
    bits_order = orders(n)
    me.enter()
    own = [me.t] + list(me.pieces(()))
    hops, doubles, tiny = {}, {}, []
    for j in range(1, groups):
        tiny.append(send(small, small_held.at[j - 1], (s_send, s_recv), j - 1, me.along(j)))
        tiny[-1].start()
    for a in range(arrays):
        for j in range(1, groups):
            u = a * (groups - 1) + j - 1
            hops[u] = send(
                shards[a].at[tuple(me.pieces(()))], held[a].at[tuple(own)], (z_send, z_recv), u, me.along(j)
            )
            hops[u].start()
    loads = []
    for a in range(arrays):
        loads.append(pltpu.make_async_copy(shards[a], held[a].at[me.t], load_sem.at[a]))
        loads[-1].start()

    units = arrays * (groups - 1)
    stores = []

    def advance(u, stage):
        a, j = divmod(u, groups - 1)
        source = (me.t + groups - 1 - j) % groups
        if stage == 0:
            hops[u].wait_recv()
        else:
            for h in range(2):
                if stage < n or h == 0:
                    doubles[u, stage - 1, h].wait_recv()
        if stage == n:
            out = pltpu.make_async_copy(held[a].at[source], outs[a].at[source], store_sem.at[u])
            out.start()
            stores.append(out)
            return
        for h in range(2):
            if stage == n - 1:
                if h == 1:
                    continue
                bit, done, cols = 0, set(range(1, n)), slice(None)
            else:
                bit, done = bits_order[h][stage], set(bits_order[h][:stage])
                cols = pl.ds(h * half, half)
            view = (source,) + me.pieces(done) + (slice(None), cols)
            slot = (u * n + stage) * 2 + h
            copy = send(held[a].at[view], held[a].at[view], (x_send, x_recv), slot, me.partner(bit))
            copy.start()
            doubles[u, stage, h] = copy

    for tick in range(units + n):
        for stage in range(n + 1):
            u = tick - stage
            if 0 <= u < units:
                advance(u, stage)
    for a in range(arrays):
        loads[a].wait()
        out = pltpu.make_async_copy(held[a].at[me.t], outs[a].at[me.t], store_sem.at[units + a])
        out.start()
        stores.append(out)
    small_out[me.t] = small[...]
    for j in range(1, groups):
        tiny[j - 1].wait()
        small_out[(me.t + groups - j) % groups] = small_held[j - 1]
    for copy in hops.values():
        copy.wait_send()
    for copy in doubles.values():
        copy.wait_send()
    for copy in stores:
        copy.wait()


def gather(shards, small, groups, parts):
    arrays, n = len(shards), parts.bit_length() - 1
    rows, cols = shards[0].shape[0] // parts, shards[0].shape[1]
    shape = (2,) * n + (rows, cols)
    units = arrays * (groups - 1)
    any_space = pl.BlockSpec(memory_space=pl.ANY)
    vmem = pl.BlockSpec(memory_space=pltpu.VMEM)
    *outs, small = pl.pallas_call(
        functools.partial(gather_kernel, groups, parts, arrays),
        out_shape=[jax.ShapeDtypeStruct((groups,) + shape, LOW)] * arrays
        + [jax.ShapeDtypeStruct((groups,) + small.shape, LOW)],
        in_specs=[any_space] * arrays + [vmem],
        out_specs=[any_space] * arrays + [vmem],
        scratch_shapes=[pltpu.VMEM((groups,) + shape, LOW)] * arrays
        + [
            pltpu.VMEM((groups - 1,) + small.shape, LOW),
            pltpu.SemaphoreType.DMA((arrays,)),
            pltpu.SemaphoreType.DMA((units + arrays,)),
            pltpu.SemaphoreType.DMA((units,)),
            pltpu.SemaphoreType.DMA((units,)),
            pltpu.SemaphoreType.DMA((units * n * 2,)),
            pltpu.SemaphoreType.DMA((units * n * 2,)),
            pltpu.SemaphoreType.DMA((groups - 1,)),
            pltpu.SemaphoreType.DMA((groups - 1,)),
        ],
        compiler_params=pltpu.CompilerParams(
            collective_id=0, has_side_effects=True, vmem_limit_bytes=60 << 20
        ),
        name="gather_weights",
    )(*[s.reshape(shape) for s in shards], small)
    return [o.reshape(groups, parts * rows, cols) for o in outs], small


def add_into(dst, src, lead):
    def one(i, carry):
        index = []
        for size in reversed(lead):
            index.append(i % size)
            i = i // size
        index = tuple(reversed(index))
        total = dst[index].astype(jnp.float32) + src[index].astype(jnp.float32)
        dst[index] = total.astype(LOW)
        return carry

    total = 1
    for size in lead:
        total *= size
    lax.fori_loop(0, total, one, 0)


def scatter_kernel(groups, parts, arrays, *refs):
    parted, vec = refs[:arrays], refs[arrays]
    outs, vec_out = refs[arrays + 1 : 2 * arrays + 1], refs[2 * arrays + 1]
    p = 2 * arrays + 2
    held = refs[p : p + arrays]
    n = parts.bit_length() - 1
    p += arrays
    landing = refs[p]
    halves = refs[p + 1 : p + n]
    final = refs[p + n]
    load_sem, x_send, x_recv, z_send, z_recv, vec_sum, vec_land, v_send, v_recv = refs[p + n + 1 :]
    me = Place(groups, parts)
    half = parted[0].shape[-1] // 2
    bits_order = orders(n)
    units = arrays * groups
    loads = []
    turn = [(u // groups, (me.t + 1 + u % groups) % groups) for u in range(units)]
    for u in range(units):
        a, target = turn[u]
        copy = pltpu.make_async_copy(parted[a].at[target], held[a].at[target], load_sem.at[u])
        copy.start()
        loads.append(copy)
    me.enter()
    copies, hops, tiny = {}, {}, {}

    def advance_vectors(stage):
        source = vec if stage == 0 else vec_sum.at[stage - 1]
        if stage:
            tiny[stage - 1].wait_recv()
            before = vec[...] if stage == 1 else vec_sum[stage - 2]
            vec_sum[stage - 1] = before + vec_land[stage - 1]
        peers = [me.partner(stage)] if stage < n else [me.along(j) for j in range(1, groups)]
        for k, peer in enumerate(peers):
            copy = send(source, vec_land.at[stage + k], (v_send, v_recv), stage + k, peer)
            copy.start()
            tiny[stage + k] = copy

    def advance(u, stage):
        a, target = turn[u]
        if stage == 0:
            loads[u].wait()
            copy = send(
                held[a].at[(target,) + me.pieces(set(range(1, n)), 0)],
                landing.at[u],
                (x_send, x_recv),
                u * 2 * n,
                me.partner(0),
            )
            copy.start()
            copies[u, 0, 0] = copy
            return
        for h in range(2):
            if stage == 1:
                if h == 1:
                    continue
                left, cols, source = set(range(1, n)), slice(None), landing.at[u]
            else:
                bits = bits_order[h]
                left, cols = set(bits[stage - 1 :]), pl.ds(h * half, half)
                source = halves[stage - 2].at[u, h]
            copies[u, stage - 1, h].wait_recv()
            view = (target,) + me.pieces(left) + (slice(None), cols)
            add_into(held[a].at[view], source, [2] * len(left))
        if stage == n:
            if u % groups < groups - 1:
                j = u % groups + 1
                slot = a * (groups - 1) + j - 1
                hops[slot] = send(
                    held[a].at[(target,) + me.pieces(())], final.at[slot], (z_send, z_recv), slot, me.along(j)
                )
                hops[slot].start()
            return
        for h in range(2):
            bits = bits_order[h]
            bit, left = bits[stage - 1], set(bits[stage:])
            view = (target,) + me.pieces(left, bit) + (slice(None), pl.ds(h * half, half))
            copy = send(
                held[a].at[view],
                halves[stage - 1].at[u, h],
                (x_send, x_recv),
                u * 2 * n + stage * 2 + h,
                me.partner(bit),
            )
            copy.start()
            copies[u, stage, h] = copy

    for tick in range(units + n):
        if tick <= n:
            advance_vectors(tick)
        for stage in reversed(range(n + 1)):
            u = tick - stage
            if 0 <= u < units:
                advance(u, stage)
    total = vec_sum[n - 1]
    for j in range(groups - 1):
        tiny[n + j].wait_recv()
        total = total + vec_land[n + j]
    vec_out[...] = total
    for a in range(arrays):
        total = held[a][(me.t,) + me.pieces(())].astype(jnp.float32)
        for j in range(groups - 1):
            slot = a * (groups - 1) + j
            hops[slot].wait_recv()
            total = total + final[slot].astype(jnp.float32)
        outs[a][...] = total
    for copy in tiny.values():
        copy.wait_send()
    for copy in copies.values():
        copy.wait_send()
    for copy in hops.values():
        copy.wait_send()


def scatter(parted, vec, groups, parts):
    arrays, n = len(parted), parts.bit_length() - 1
    rows, cols = parted[0].shape[1] // parts, parted[0].shape[2]
    shape = (groups,) + (2,) * n + (rows, cols)
    units = arrays * groups
    vmem = pl.BlockSpec(memory_space=pltpu.VMEM)
    return pl.pallas_call(
        functools.partial(scatter_kernel, groups, parts, arrays),
        out_shape=[jax.ShapeDtypeStruct((rows, cols), jnp.float32)] * arrays
        + [jax.ShapeDtypeStruct(vec.shape, jnp.float32)],
        in_specs=[pl.BlockSpec(memory_space=pl.ANY)] * arrays + [vmem],
        out_specs=[vmem] * (arrays + 1),
        scratch_shapes=[pltpu.VMEM(shape, LOW)] * arrays
        + [pltpu.VMEM((units,) + (2,) * (n - 1) + (rows, cols), LOW)]
        + [pltpu.VMEM((units, 2) + (2,) * (n - 1 - s) + (rows, cols // 2), LOW) for s in range(1, n)]
        + [
            pltpu.VMEM((arrays * (groups - 1), rows, cols), LOW),
            pltpu.SemaphoreType.DMA((units,)),
            pltpu.SemaphoreType.DMA((units * 2 * n,)),
            pltpu.SemaphoreType.DMA((units * 2 * n,)),
            pltpu.SemaphoreType.DMA((arrays * (groups - 1),)),
            pltpu.SemaphoreType.DMA((arrays * (groups - 1),)),
            pltpu.VMEM((n,) + vec.shape, jnp.float32),
            pltpu.VMEM((n + groups - 1,) + vec.shape, jnp.float32),
            pltpu.SemaphoreType.DMA((n + groups - 1,)),
            pltpu.SemaphoreType.DMA((n + groups - 1,)),
        ],
        compiler_params=pltpu.CompilerParams(
            collective_id=1, has_side_effects=True, vmem_limit_bytes=60 << 20
        ),
        name="scatter_gradients",
    )(*[g.reshape(shape) for g in parted], vec)


norm_epsilon = 1e-12
root_half = 0.7071067811865476


def norm_forward(values, norm_gain, norm_shift):
    average = jnp.mean(values, axis=-1, keepdims=True)
    centered = values - average
    variance = jnp.mean(centered * centered, axis=-1, keepdims=True)
    inverse = lax.rsqrt(variance + norm_epsilon)
    scaled = centered * inverse
    return (scaled * norm_gain + norm_shift, scaled, inverse)


def norm_backward(grad_out, scaled, inverse, norm_gain):
    weighted = grad_out * norm_gain
    mean_grad = jnp.mean(weighted, axis=-1, keepdims=True)
    mean_proj = jnp.mean(weighted * scaled, axis=-1, keepdims=True)
    return inverse * (weighted - mean_grad - scaled * mean_proj)


def gelu_exact(values):
    return 0.5 * values * (1.0 + lax.erf(values * root_half))


def cross_rows(left, right):
    return lax.dot_general(
        left, right, (((0,), (0,)), ((), ())), preferred_element_type=jnp.float32
    )


def times_transposed(left, right):
    return lax.dot_general(
        left, right, (((1,), (1,)), ((), ())), preferred_element_type=jnp.float32
    )


def masked_scores(queries, keys_in, segment_row):
    same_text = segment_row[:, None] == segment_row[None, :]
    scores = jnp.einsum("qhd,khd->hqk", queries, keys_in, preferred_element_type=jnp.float32)
    scores = scores * queries.shape[2] ** (-0.5)
    return jnp.where(same_text[None], scores, -1000000000.0)


def attend_forward(packed):
    queries, keys_in, values, segment_row = packed
    scores = masked_scores(queries, keys_in, segment_row)
    row_max = jnp.max(scores, axis=-1, keepdims=True)
    exponent = jnp.exp(scores - row_max)
    row_total = jnp.sum(exponent, axis=-1, keepdims=True)
    attn_probs = (exponent / row_total).astype(jnp.bfloat16)
    mixed_heads = jnp.einsum("hqk,khd->qhd", attn_probs, values, preferred_element_type=jnp.float32)
    return (mixed_heads.astype(jnp.bfloat16), row_max + jnp.log(row_total))


def attend_backward(packed):
    queries, keys_in, values, segment_row, logsum, grad_mixed = packed
    score_scale = queries.shape[2] ** (-0.5)
    scores = masked_scores(queries, keys_in, segment_row)
    attn_probs = jnp.exp(scores - logsum)
    grad_probs = jnp.einsum("qhd,khd->hqk", grad_mixed, values, preferred_element_type=jnp.float32)
    grad_values = jnp.einsum(
        "hqk,qhd->khd",
        attn_probs.astype(jnp.bfloat16),
        grad_mixed,
        preferred_element_type=jnp.float32,
    )
    inner_sum = jnp.sum(attn_probs * grad_probs, axis=-1, keepdims=True)
    grad_scores = (attn_probs * (grad_probs - inner_sum)).astype(jnp.bfloat16)
    grad_queries = (
        jnp.einsum("hqk,khd->qhd", grad_scores, keys_in, preferred_element_type=jnp.float32)
        * score_scale
    )
    grad_keys = (
        jnp.einsum("hqk,qhd->khd", grad_scores, queries, preferred_element_type=jnp.float32)
        * score_scale
    )
    return (
        grad_queries.astype(jnp.bfloat16),
        grad_keys.astype(jnp.bfloat16),
        grad_values.astype(jnp.bfloat16),
    )


def per_device(
    inputs,
    segments,
    w_query,
    w_key,
    w_value,
    b_query,
    b_value,
    w_output,
    b_output,
    gain_attn,
    shift_attn,
    w_hidden,
    b_hidden,
    w_project,
    b_project,
    gain_ffn,
    shift_ffn,
    cotangent,
):
    seq_len = segments.shape[1]
    share_tokens = cotangent.shape[0]
    share_rows = share_tokens // seq_len
    width = inputs.shape[1]
    groups, parts = lax.axis_size("tensor"), lax.axis_size("dp")
    place, part = lax.axis_index("tensor"), lax.axis_index("dp")
    low = jnp.bfloat16
    wide = jnp.float32

    tokens = lax.dynamic_slice_in_dim(inputs, place * share_tokens, share_tokens, 0)
    rows_segments = lax.dynamic_slice_in_dim(segments, place * share_rows, share_rows, 0)
    split = w_query.shape[1]
    small = jnp.concatenate([b_query, b_value, b_hidden]).reshape(-1, 128)
    small_rows = small.shape[0]
    small = jnp.pad(small, ((0, -small_rows % 16), (0, 0)))
    first = jnp.concatenate([w_query, w_key, w_value, w_output.T], axis=1)
    (first, w_up, w_down), small = gather([first, w_hidden, w_project], small, groups, parts)
    w_in = first[:, :, : 3 * split].reshape(groups, width, 3, split).transpose(1, 2, 0, 3)
    w_in = w_in.reshape(width, 3 * groups * split)
    w_out = first[:, :, 3 * split :].transpose(0, 2, 1).reshape(groups * split, width)
    w_up = w_up.transpose(1, 0, 2).reshape(width, -1)
    w_down = w_down.reshape(-1, width)
    small = small[:, :small_rows].reshape(groups, -1).astype(wide)
    bias_query = small[:, :split].reshape(-1)
    bias_value = small[:, split : 2 * split].reshape(-1)
    bias_hidden = small[:, 2 * split :].reshape(-1)
    full = groups * split
    head_shape = (share_rows, seq_len, full // HD, HD)

    attn_gain = gain_attn.astype(wide)
    attn_shift = shift_attn.astype(wide)
    attn_bias = b_output.astype(wide)
    ffn_gain = gain_ffn.astype(wide)
    ffn_shift = shift_ffn.astype(wide)
    ffn_bias = b_project.astype(wide)
    grad_out = cotangent.astype(wide)

    projected = jnp.dot(tokens, w_in, preferred_element_type=wide)
    queries = (projected[:, :full] + bias_query).astype(low)
    keys_in = projected[:, full : 2 * full].astype(low)
    values = (projected[:, 2 * full :] + bias_value).astype(low)
    query_heads = queries.reshape(head_shape)
    key_heads = keys_in.reshape(head_shape)
    value_heads = values.reshape(head_shape)
    mixed_heads, logsum = lax.map(attend_forward, (query_heads, key_heads, value_heads, rows_segments))
    mixed = mixed_heads.reshape(share_tokens, full)
    hidden = tokens.astype(wide) + (jnp.dot(mixed, w_out, preferred_element_type=wide) + attn_bias)
    normed, scaled, inverse = norm_forward(hidden, attn_gain, attn_shift)
    normed_low = normed.astype(low)
    hidden_pre = jnp.dot(normed_low, w_up, preferred_element_type=wide) + bias_hidden
    active, gelu_pull = jax.vjp(gelu_exact, hidden_pre)
    active_low = active.astype(low)
    block_sum = normed + (jnp.dot(active_low, w_down, preferred_element_type=wide) + ffn_bias)
    output, scaled_out, inverse_out = norm_forward(block_sum, ffn_gain, ffn_shift)
    grad_sum = norm_backward(grad_out, scaled_out, inverse_out, ffn_gain)
    grad_ffn_gain = jnp.sum(grad_out * scaled_out, axis=0)
    grad_ffn_shift = jnp.sum(grad_out, axis=0)
    grad_sum_low = grad_sum.astype(low)
    grad_ffn_bias = jnp.sum(grad_sum_low.astype(wide), axis=0)
    grad_active = times_transposed(grad_sum_low, w_down)
    grad_w_down = cross_rows(grad_sum_low, active_low)
    grad_hidden_pre = gelu_pull(grad_active)[0].astype(low)
    grad_b_hidden = jnp.sum(grad_hidden_pre.astype(wide), axis=0)
    grad_w_up = cross_rows(normed_low, grad_hidden_pre)
    grad_normed = grad_sum + times_transposed(grad_hidden_pre, w_up)
    grad_hidden = norm_backward(grad_normed, scaled, inverse, attn_gain)
    grad_hidden_low = grad_hidden.astype(low)
    grad_attn_gain = jnp.sum(grad_normed * scaled, axis=0)
    grad_attn_shift = jnp.sum(grad_normed, axis=0)
    grad_attn_bias = jnp.sum(grad_hidden_low.astype(wide), axis=0)
    grad_w_out = cross_rows(grad_hidden_low, mixed)
    grad_mixed = times_transposed(grad_hidden_low, w_out).astype(low).reshape(head_shape)
    grad_q, grad_k, grad_v = lax.map(
        attend_backward, (query_heads, key_heads, value_heads, rows_segments, logsum, grad_mixed)
    )
    grad_q = grad_q.reshape(share_tokens, full)
    grad_k = grad_k.reshape(share_tokens, full)
    grad_v = grad_v.reshape(share_tokens, full)
    grad_projected = jnp.concatenate([grad_q, grad_k, grad_v], axis=1)
    grad_w_in = cross_rows(tokens, grad_projected)
    grad_b_query = jnp.sum(grad_q.astype(wide), axis=0)
    grad_b_value = jnp.sum(grad_v.astype(wide), axis=0)
    grad_input = grad_hidden + times_transposed(grad_projected, w_in)

    def parted(grad):
        return grad.astype(low).reshape(width, groups, -1).transpose(1, 0, 2)

    first = jnp.concatenate(
        [parted(grad_w_in[:, i * full : (i + 1) * full]) for i in range(3)] + [parted(grad_w_out)], axis=2
    )
    vectors = jnp.concatenate(
        [
            jnp.stack([grad_b_query, grad_b_value]).reshape(2 * groups, split),
            grad_b_hidden.reshape(-1, split),
            jnp.stack(
                [
                    grad_attn_gain,
                    grad_attn_shift,
                    grad_attn_bias,
                    grad_ffn_gain,
                    grad_ffn_shift,
                    grad_ffn_bias,
                ]
            ).reshape(-1, split),
        ],
        axis=0,
    )
    count = vectors.size // split
    vectors = vectors.reshape(-1, 128)
    (sum_first, sum_up, sum_down, vectors) = scatter(
        [first, parted(grad_w_up), parted(grad_w_down)], vectors, groups, parts
    )
    vectors = vectors.reshape(count, split)
    bias_qv = vectors[: 2 * groups].reshape(2, groups, split // HD, HD)
    rest = vectors[2 * groups :]
    hid = bias_hidden.shape[0] // split
    bias_h = rest[:hid].reshape(groups, -1, HD)
    vec = rest[hid:].reshape(6, -1)
    piece = HD // parts
    bias_qv = lax.dynamic_slice_in_dim(bias_qv, place, 1, 1)[:, 0]
    bias_qv = lax.dynamic_slice_in_dim(bias_qv, part * piece, piece, 2)
    bias_h = lax.dynamic_slice_in_dim(bias_h, place, 1, 0)[0]
    bias_h = lax.dynamic_slice_in_dim(bias_h, part * piece, piece, 1)
    piece = width // (parts * groups)
    vec = lax.dynamic_slice_in_dim(vec, (part * groups + place) * piece, piece, 1)
    return (
        output.astype(low),
        grad_input,
        sum_first[:, :split],
        sum_first[:, split : 2 * split],
        sum_first[:, 2 * split : 3 * split],
        sum_first[:, 3 * split :].T,
        sum_up,
        sum_down.T,
        bias_qv,
        bias_h,
        vec,
    )


def solution(mesh):
    in_specs = (
        P("dp", None),
        P("dp", None),
        P(None, "tensor"),
        P(None, "tensor"),
        P(None, "tensor"),
        P("tensor"),
        P("tensor"),
        P("tensor", None),
        P(),
        P(),
        P(),
        P(None, "tensor"),
        P("tensor"),
        P("tensor", None),
        P(),
        P(),
        P(),
        P(("dp", "tensor"), None),
    )
    out_specs = (
        P(("dp", "tensor"), None),
        P(("dp", "tensor"), None),
        P("dp", "tensor"),
        P("dp", "tensor"),
        P("dp", "tensor"),
        P("tensor", "dp"),
        P("dp", "tensor"),
        P("tensor", "dp"),
        P(None, "tensor", "dp"),
        P("tensor", "dp"),
        P(None, ("dp", "tensor")),
    )
    return jax.shard_map(
        per_device, mesh=mesh, in_specs=in_specs, out_specs=out_specs, check_vma=False
    )
```

```python
import functools
import jax
import jax.numpy as jnp
from jax import lax
from jax.experimental import pallas as pl
from jax.experimental.pallas import tpu as pltpu
from jax.sharding import PartitionSpec as P

HD = 64
MESH = pl.DeviceIdType.MESH
LOW = jnp.bfloat16


class Place:
    def __init__(self, groups, parts):
        self.groups, self.parts = groups, parts
        self.t, self.d = lax.axis_index("tensor"), lax.axis_index("dp")
        self.count = parts.bit_length() - 1
        self.bits = [(self.d // (1 << i)) % 2 for i in range(self.count)]

    def partner(self, bit):
        return (self.d + (1 - 2 * self.bits[bit]) * (1 << bit), self.t)

    def along(self, step):
        return (self.d, (self.t + step) % self.groups)

    def enter(self):
        barrier = pltpu.get_barrier_semaphore()
        peers = [self.partner(b) for b in range(self.count)]
        peers += [self.along(j) for j in range(1, self.groups)]
        for peer in peers:
            pl.semaphore_signal(barrier, inc=1, device_id=peer, device_id_type=MESH)
        pl.semaphore_wait(barrier, len(peers))

    def pieces(self, open_bits, flipped=None):
        index = []
        for bit in reversed(range(self.count)):
            own = self.bits[bit]
            index.append(slice(None) if bit in open_bits else 1 - own if bit == flipped else own)
        return tuple(index)


def send(src, dst, sems, slot, peer):
    return pltpu.make_async_remote_copy(
        src_ref=src,
        dst_ref=dst,
        send_sem=sems[0].at[slot],
        recv_sem=sems[1].at[slot],
        device_id=peer,
        device_id_type=MESH,
    )


def orders(count):
    rest = list(range(1, count))
    return [rest, rest[::-1]]


def gather_kernel(groups, parts, arrays, *refs):
    shards, small = refs[:arrays], refs[arrays]
    outs, small_out = refs[arrays + 1 : 2 * arrays + 1], refs[2 * arrays + 1]
    held, small_held = refs[2 * arrays + 2 : 3 * arrays + 2], refs[3 * arrays + 2]
    load_sem, store_sem, z_send, z_recv, x_send, x_recv, s_send, s_recv = refs[3 * arrays + 3 :]
    me = Place(groups, parts)
    n = me.count
    half = shards[0].shape[-1] // 2
    bits_order = orders(n)
    me.enter()
    own = [me.t] + list(me.pieces(()))
    hops, doubles, tiny = {}, {}, []
    for j in range(1, groups):
        tiny.append(send(small, small_held.at[j - 1], (s_send, s_recv), j - 1, me.along(j)))
        tiny[-1].start()
    for a in range(arrays):
        for j in range(1, groups):
            u = a * (groups - 1) + j - 1
            hops[u] = send(
                shards[a].at[tuple(me.pieces(()))], held[a].at[tuple(own)], (z_send, z_recv), u, me.along(j)
            )
            hops[u].start()
    loads = []
    for a in range(arrays):
        loads.append(pltpu.make_async_copy(shards[a], held[a].at[me.t], load_sem.at[a]))
        loads[-1].start()

    units = arrays * (groups - 1)
    stores = []

    def advance(u, stage):
        a, j = divmod(u, groups - 1)
        source = (me.t + groups - 1 - j) % groups
        if stage == 0:
            hops[u].wait_recv()
        else:
            for h in range(2):
                if stage < n or h == 0:
                    doubles[u, stage - 1, h].wait_recv()
        if stage == n:
            out = pltpu.make_async_copy(held[a].at[source], outs[a].at[source], store_sem.at[u])
            out.start()
            stores.append(out)
            return
        for h in range(2):
            if stage == n - 1:
                if h == 1:
                    continue
                bit, done, cols = 0, set(range(1, n)), slice(None)
            else:
                bit, done = bits_order[h][stage], set(bits_order[h][:stage])
                cols = pl.ds(h * half, half)
            view = (source,) + me.pieces(done) + (slice(None), cols)
            slot = (u * n + stage) * 2 + h
            copy = send(held[a].at[view], held[a].at[view], (x_send, x_recv), slot, me.partner(bit))
            copy.start()
            doubles[u, stage, h] = copy

    for tick in range(units + n):
        for stage in range(n + 1):
            u = tick - stage
            if 0 <= u < units:
                advance(u, stage)
    for a in range(arrays):
        loads[a].wait()
        out = pltpu.make_async_copy(held[a].at[me.t], outs[a].at[me.t], store_sem.at[units + a])
        out.start()
        stores.append(out)
    small_out[me.t] = small[...]
    for j in range(1, groups):
        tiny[j - 1].wait()
        small_out[(me.t + groups - j) % groups] = small_held[j - 1]
    for copy in hops.values():
        copy.wait_send()
    for copy in doubles.values():
        copy.wait_send()
    for copy in stores:
        copy.wait()


def gather(shards, small, groups, parts):
    arrays, n = len(shards), parts.bit_length() - 1
    rows, cols = shards[0].shape[0] // parts, shards[0].shape[1]
    shape = (2,) * n + (rows, cols)
    units = arrays * (groups - 1)
    any_space = pl.BlockSpec(memory_space=pl.ANY)
    vmem = pl.BlockSpec(memory_space=pltpu.VMEM)
    *outs, small = pl.pallas_call(
        functools.partial(gather_kernel, groups, parts, arrays),
        out_shape=[jax.ShapeDtypeStruct((groups,) + shape, LOW)] * arrays
        + [jax.ShapeDtypeStruct((groups,) + small.shape, LOW)],
        in_specs=[any_space] * arrays + [vmem],
        out_specs=[any_space] * arrays + [vmem],
        scratch_shapes=[pltpu.VMEM((groups,) + shape, LOW)] * arrays
        + [
            pltpu.VMEM((groups - 1,) + small.shape, LOW),
            pltpu.SemaphoreType.DMA((arrays,)),
            pltpu.SemaphoreType.DMA((units + arrays,)),
            pltpu.SemaphoreType.DMA((units,)),
            pltpu.SemaphoreType.DMA((units,)),
            pltpu.SemaphoreType.DMA((units * n * 2,)),
            pltpu.SemaphoreType.DMA((units * n * 2,)),
            pltpu.SemaphoreType.DMA((groups - 1,)),
            pltpu.SemaphoreType.DMA((groups - 1,)),
        ],
        compiler_params=pltpu.CompilerParams(
            collective_id=0, has_side_effects=True, vmem_limit_bytes=60 << 20
        ),
        name="gather_weights",
    )(*[s.reshape(shape) for s in shards], small)
    return [o.reshape(groups, parts * rows, cols) for o in outs], small


def add_into(dst, src, lead):
    def one(i, carry):
        index = []
        for size in reversed(lead):
            index.append(i % size)
            i = i // size
        index = tuple(reversed(index))
        total = dst[index].astype(jnp.float32) + src[index].astype(jnp.float32)
        dst[index] = total.astype(LOW)
        return carry

    total = 1
    for size in lead:
        total *= size
    lax.fori_loop(0, total, one, 0)


def scatter_kernel(groups, parts, arrays, *refs):
    parted, vec = refs[:arrays], refs[arrays]
    outs, vec_out = refs[arrays + 1 : 2 * arrays + 1], refs[2 * arrays + 1]
    p = 2 * arrays + 2
    held = refs[p : p + arrays]
    n = parts.bit_length() - 1
    p += arrays
    landing = refs[p]
    halves = refs[p + 1 : p + n]
    final = refs[p + n]
    load_sem, x_send, x_recv, z_send, z_recv, vec_sum, vec_land, v_send, v_recv = refs[p + n + 1 :]
    me = Place(groups, parts)
    half = parted[0].shape[-1] // 2
    bits_order = orders(n)
    units = arrays * groups
    loads = []
    turn = [(u // groups, (me.t + 1 + u % groups) % groups) for u in range(units)]
    for u in range(units):
        a, target = turn[u]
        copy = pltpu.make_async_copy(parted[a].at[target], held[a].at[target], load_sem.at[u])
        copy.start()
        loads.append(copy)
    me.enter()
    copies, hops, tiny = {}, {}, {}

    def advance_vectors(stage):
        source = vec if stage == 0 else vec_sum.at[stage - 1]
        if stage:
            tiny[stage - 1].wait_recv()
            before = vec[...] if stage == 1 else vec_sum[stage - 2]
            vec_sum[stage - 1] = before + vec_land[stage - 1]
        peers = [me.partner(stage)] if stage < n else [me.along(j) for j in range(1, groups)]
        for k, peer in enumerate(peers):
            copy = send(source, vec_land.at[stage + k], (v_send, v_recv), stage + k, peer)
            copy.start()
            tiny[stage + k] = copy

    def advance(u, stage):
        a, target = turn[u]
        if stage == 0:
            loads[u].wait()
            copy = send(
                held[a].at[(target,) + me.pieces(set(range(1, n)), 0)],
                landing.at[u],
                (x_send, x_recv),
                u * 2 * n,
                me.partner(0),
            )
            copy.start()
            copies[u, 0, 0] = copy
            return
        for h in range(2):
            if stage == 1:
                if h == 1:
                    continue
                left, cols, source = set(range(1, n)), slice(None), landing.at[u]
            else:
                bits = bits_order[h]
                left, cols = set(bits[stage - 1 :]), pl.ds(h * half, half)
                source = halves[stage - 2].at[u, h]
            copies[u, stage - 1, h].wait_recv()
            view = (target,) + me.pieces(left) + (slice(None), cols)
            add_into(held[a].at[view], source, [2] * len(left))
        if stage == n:
            if u % groups < groups - 1:
                j = u % groups + 1
                slot = a * (groups - 1) + j - 1
                hops[slot] = send(
                    held[a].at[(target,) + me.pieces(())], final.at[slot], (z_send, z_recv), slot, me.along(j)
                )
                hops[slot].start()
            return
        for h in range(2):
            bits = bits_order[h]
            bit, left = bits[stage - 1], set(bits[stage:])
            view = (target,) + me.pieces(left, bit) + (slice(None), pl.ds(h * half, half))
            copy = send(
                held[a].at[view],
                halves[stage - 1].at[u, h],
                (x_send, x_recv),
                u * 2 * n + stage * 2 + h,
                me.partner(bit),
            )
            copy.start()
            copies[u, stage, h] = copy

    for tick in range(units + n):
        if tick <= n:
            advance_vectors(tick)
        for stage in reversed(range(n + 1)):
            u = tick - stage
            if 0 <= u < units:
                advance(u, stage)
    total = vec_sum[n - 1]
    for j in range(groups - 1):
        tiny[n + j].wait_recv()
        total = total + vec_land[n + j]
    vec_out[...] = total
    for a in range(arrays):
        total = held[a][(me.t,) + me.pieces(())].astype(jnp.float32)
        for j in range(groups - 1):
            slot = a * (groups - 1) + j
            hops[slot].wait_recv()
            total = total + final[slot].astype(jnp.float32)
        outs[a][...] = total
    for copy in tiny.values():
        copy.wait_send()
    for copy in copies.values():
        copy.wait_send()
    for copy in hops.values():
        copy.wait_send()


def scatter(parted, vec, groups, parts):
    arrays, n = len(parted), parts.bit_length() - 1
    rows, cols = parted[0].shape[1] // parts, parted[0].shape[2]
    shape = (groups,) + (2,) * n + (rows, cols)
    units = arrays * groups
    vmem = pl.BlockSpec(memory_space=pltpu.VMEM)
    return pl.pallas_call(
        functools.partial(scatter_kernel, groups, parts, arrays),
        out_shape=[jax.ShapeDtypeStruct((rows, cols), jnp.float32)] * arrays
        + [jax.ShapeDtypeStruct(vec.shape, jnp.float32)],
        in_specs=[pl.BlockSpec(memory_space=pl.ANY)] * arrays + [vmem],
        out_specs=[vmem] * (arrays + 1),
        scratch_shapes=[pltpu.VMEM(shape, LOW)] * arrays
        + [pltpu.VMEM((units,) + (2,) * (n - 1) + (rows, cols), LOW)]
        + [pltpu.VMEM((units, 2) + (2,) * (n - 1 - s) + (rows, cols // 2), LOW) for s in range(1, n)]
        + [
            pltpu.VMEM((arrays * (groups - 1), rows, cols), LOW),
            pltpu.SemaphoreType.DMA((units,)),
            pltpu.SemaphoreType.DMA((units * 2 * n,)),
            pltpu.SemaphoreType.DMA((units * 2 * n,)),
            pltpu.SemaphoreType.DMA((arrays * (groups - 1),)),
            pltpu.SemaphoreType.DMA((arrays * (groups - 1),)),
            pltpu.VMEM((n,) + vec.shape, jnp.float32),
            pltpu.VMEM((n + groups - 1,) + vec.shape, jnp.float32),
            pltpu.SemaphoreType.DMA((n + groups - 1,)),
            pltpu.SemaphoreType.DMA((n + groups - 1,)),
        ],
        compiler_params=pltpu.CompilerParams(
            collective_id=1, has_side_effects=True, vmem_limit_bytes=60 << 20
        ),
        name="scatter_gradients",
    )(*[g.reshape(shape) for g in parted], vec)


norm_epsilon = 1e-12
root_half = 0.7071067811865476


def norm_forward(values, norm_gain, norm_shift):
    average = jnp.mean(values, axis=-1, keepdims=True)
    centered = values - average
    variance = jnp.mean(centered * centered, axis=-1, keepdims=True)
    inverse = lax.rsqrt(variance + norm_epsilon)
    scaled = centered * inverse
    return (scaled * norm_gain + norm_shift, scaled, inverse)


def norm_backward(grad_out, scaled, inverse, norm_gain):
    weighted = grad_out * norm_gain
    mean_grad = jnp.mean(weighted, axis=-1, keepdims=True)
    mean_proj = jnp.mean(weighted * scaled, axis=-1, keepdims=True)
    return inverse * (weighted - mean_grad - scaled * mean_proj)


def gelu_exact(values):
    return 0.5 * values * (1.0 + lax.erf(values * root_half))


def cross_rows(left, right):
    return lax.dot_general(
        left, right, (((0,), (0,)), ((), ())), preferred_element_type=jnp.float32
    )


def times_transposed(left, right):
    return lax.dot_general(
        left, right, (((1,), (1,)), ((), ())), preferred_element_type=jnp.float32
    )


def masked_scores(queries, keys_in, segment_row):
    same_text = segment_row[:, None] == segment_row[None, :]
    scores = jnp.einsum("qhd,khd->hqk", queries, keys_in, preferred_element_type=jnp.float32)
    scores = scores * queries.shape[2] ** (-0.5)
    return jnp.where(same_text[None], scores, -1000000000.0)


def attend_forward(packed):
    queries, keys_in, values, segment_row = packed
    scores = masked_scores(queries, keys_in, segment_row)
    row_max = jnp.max(scores, axis=-1, keepdims=True)
    exponent = jnp.exp(scores - row_max)
    row_total = jnp.sum(exponent, axis=-1, keepdims=True)
    attn_probs = (exponent / row_total).astype(jnp.bfloat16)
    mixed_heads = jnp.einsum("hqk,khd->qhd", attn_probs, values, preferred_element_type=jnp.float32)
    return (mixed_heads.astype(jnp.bfloat16), row_max + jnp.log(row_total))


def attend_backward(packed):
    queries, keys_in, values, segment_row, logsum, grad_mixed = packed
    score_scale = queries.shape[2] ** (-0.5)
    scores = masked_scores(queries, keys_in, segment_row)
    attn_probs = jnp.exp(scores - logsum)
    grad_probs = jnp.einsum("qhd,khd->hqk", grad_mixed, values, preferred_element_type=jnp.float32)
    grad_values = jnp.einsum(
        "hqk,qhd->khd",
        attn_probs.astype(jnp.bfloat16),
        grad_mixed,
        preferred_element_type=jnp.float32,
    )
    inner_sum = jnp.sum(attn_probs * grad_probs, axis=-1, keepdims=True)
    grad_scores = (attn_probs * (grad_probs - inner_sum)).astype(jnp.bfloat16)
    grad_queries = (
        jnp.einsum("hqk,khd->qhd", grad_scores, keys_in, preferred_element_type=jnp.float32)
        * score_scale
    )
    grad_keys = (
        jnp.einsum("hqk,qhd->khd", grad_scores, queries, preferred_element_type=jnp.float32)
        * score_scale
    )
    return (
        grad_queries.astype(jnp.bfloat16),
        grad_keys.astype(jnp.bfloat16),
        grad_values.astype(jnp.bfloat16),
    )


def matmul_t(left, right):
    return lax.dot_general(left, right, (((1,), (1,)), ((), ())), preferred_element_type=jnp.float32)


TILE = 256
SCORE = 1.4426950408889634


def row_tiles(count, size, body):
    def step(i, carry):
        body(pl.ds(pl.multiple_of(i * size, size), size))
        return carry

    lax.fori_loop(0, count // size, step, 0)


def key_window(block, blocks, span):
    return max(0, block - 1) * span, min(blocks, block + 2) * span


def fold(values):
    return jnp.sum(values.reshape(-1, 8, values.shape[-1]), axis=0)


def make_mask(mask, seg_col, seg_row):
    def step(r, carry):
        mask[r] = jnp.where(seg_col[r] == seg_row[r], 0.0, -1.0e9)
        return carry

    lax.fori_loop(0, mask.shape[0], step, 0)


def forward_kernel(groups, parts, *refs):
    (first, w_hidden, w_project, inputs, cot_in, small, rows, seg_row, seg_col) = refs[:9]
    (out, dz_out, h_out, qkv_out, mixed_out, g_out, gp_out, lse_out, w0_out, w1_out, w2_out, sums) = refs[9:21]
    (held0, held1, held2, small_all, tok, mask, hacc, facc, yb, qkv, mixed, act, slope, lse, cot) = refs[21:36]
    (load_sem, store_sem, z_send, z_recv, x_send, x_recv, s_send, s_recv) = refs[36:]
    me = Place(groups, parts)
    n = me.count
    wide, width = jnp.float32, tok.shape[1]
    count, seq = tok.shape[0], mask.shape[1]
    split = mixed.shape[2]
    heads = split // HD
    shards, held, weights = (first, w_hidden, w_project), (held0, held1, held2), (w0_out, w1_out, w2_out)
    half = width // 2
    bits_order = orders(n)
    loads, stores = [], []

    def load(src, dst):
        loads.append(pltpu.make_async_copy(src, dst, load_sem.at[len(loads)]))
        loads[-1].start()

    def store(src, dst):
        stores.append(pltpu.make_async_copy(src, dst, store_sem.at[len(stores)]))
        stores[-1].start()

    load(first, held0.at[me.t])
    load(inputs.at[pl.ds(me.t * count, count)], tok)
    load(w_hidden, held1.at[me.t])
    load(w_project, held2.at[me.t])
    load(cot_in, cot)
    me.enter()
    mine = me.pieces(())
    turn = [(0, j) for j in range(1, groups)]
    turn += [(a, j) for j in range(1, groups) for a in (1, 2)]
    units = len(turn)
    hops, doubles, tiny = {}, {}, []
    for j in range(1, groups):
        tiny.append(send(small, small_all.at[me.t], (s_send, s_recv), j - 1, me.along(j)))
        tiny[-1].start()
    for u, (a, j) in enumerate(turn):
        hops[u] = send(shards[a].at[mine], held[a].at[(me.t,) + mine], (z_send, z_recv), u, me.along(j))
        hops[u].start()

    def advance(u, stage):
        a, j = turn[u]
        source = (me.t + groups - j) % groups
        if stage == 0:
            hops[u].wait_recv()
        else:
            for h in range(2):
                if stage < n or h == 0:
                    doubles[u, stage - 1, h].wait_recv()
        if stage == n:
            store(held[a].at[source], weights[a].at[source])
            return
        for h in range(2):
            if stage == n - 1:
                if h == 1:
                    continue
                bit, done, cols = 0, set(range(1, n)), slice(None)
            else:
                bit, done = bits_order[h][stage], set(bits_order[h][:stage])
                cols = pl.ds(h * half, half)
            view = (source,) + me.pieces(done) + (slice(None), cols)
            slot = (u * n + stage) * 2 + h
            copy = send(held[a].at[view], held[a].at[view], (x_send, x_recv), slot, me.partner(bit))
            copy.start()
            doubles[u, stage, h] = copy

    ticks = [0]

    def tick(upto):
        while ticks[0] <= upto:
            for stage in range(n + 1):
                u = ticks[0] - stage
                if 0 <= u < units:
                    advance(u, stage)
            ticks[0] += 1

    def ready(a, j):
        if j:
            tick(turn.index((a, j)) + n)

    def group(j):
        return (me.t + groups - j) % groups

    def weight(a, g):
        return held[a][g].reshape(width, width)

    def project(g):
        bias = small_all[g, 0:1, : 3 * split].astype(wide)

        def body(r):
            total = jnp.dot(tok[r, :], weight(0, g)[:, : 3 * split], preferred_element_type=wide)
            qkv[g, r, :] = (total + bias).astype(LOW)

        row_tiles(count, TILE, body)

    span = 128
    blocks = seq // span
    factor = SCORE * HD ** (-0.5)

    def attend(g):
        def packed_row(p, carry):
            base = p * seq
            for b in range(blocks):
                lo, hi = key_window(b, blocks, span)
                rq = pl.ds(pl.multiple_of(base + b * span, span), span)
                rk = pl.ds(pl.multiple_of(base + lo, span), hi - lo)
                bias = mask[p, b * span : (b + 1) * span, lo:hi]
                parts_o, lane = [], lax.broadcasted_iota(jnp.int32, (span, 128), 1)
                kept = jnp.zeros((span, 128), wide)
                for h in range(heads):
                    q = qkv[g, rq, h * HD : (h + 1) * HD]
                    k = qkv[g, rk, split + h * HD : split + (h + 1) * HD]
                    v = qkv[g, rk, 2 * split + h * HD : 2 * split + (h + 1) * HD]
                    s = matmul_t(q, k) * factor + bias
                    top = jnp.max(s, axis=1, keepdims=True)
                    e = jnp.exp2(s - top)
                    total = jnp.sum(e, axis=1, keepdims=True)
                    o = jnp.dot(e.astype(LOW), v, preferred_element_type=wide)
                    parts_o.append(o * (1.0 / total))
                    kept = jnp.where(lane == h, top + jnp.log(total) * SCORE, kept)
                mixed[g, rq, :] = jnp.concatenate(parts_o, axis=1).astype(LOW)
                lse[g, rq, :] = kept
            return carry

        lax.fori_loop(0, count // seq, packed_row, 0)

    def combine(g, start):
        def body(r):
            total = matmul_t(mixed[g, r, :], weight(0, g)[:, 3 * split :])
            if start:
                hacc[r, :] = total + (tok[r, :].astype(wide) + rows[0:1])
            else:
                hacc[r, :] = hacc[r, :] + total

        row_tiles(count, TILE, body)
        store(qkv.at[g], qkv_out.at[g])
        store(mixed.at[g], mixed_out.at[g])
        store(lse.at[g], lse_out.at[g])

    def first_norm():
        def body(r):
            y, _, _ = norm_forward(hacc[r, :], rows[1:2], rows[2:3])
            yb[r, :] = y.astype(LOW)
            facc[r, :] = y + rows[5:6]

        row_tiles(count, 64, body)
        store(hacc, h_out)

    def ffn_up(g):
        bias = small_all[g, 1:2, :].astype(wide)

        def body(r):
            u = jnp.dot(yb[r, :], weight(1, g), preferred_element_type=wide) + bias
            below = 0.5 + 0.5 * lax.erf(u * root_half)
            act[g, r, :] = (u * below).astype(LOW)
            bell = jnp.exp2(u * u * (-0.5 * SCORE)) * 0.3989422804014327
            slope[g, r, :] = (below + u * bell).astype(LOW)

        row_tiles(count, TILE, body)
        store(act.at[g], g_out.at[g])
        store(slope.at[g], gp_out.at[g])

    def ffn_down(g):
        def body(r):
            facc[r, :] = facc[r, :] + jnp.dot(act[g, r, :], weight(2, g), preferred_element_type=wide)

        row_tiles(count, TILE, body)

    def last_norm():
        def step(i, carry):
            r = pl.ds(pl.multiple_of(i * 64, 64), 64)
            y, scaled, inverse = norm_forward(facc[r, :], rows[3:4], rows[4:5])
            tok[r, :] = y.astype(LOW)
            grad = cot[r, :].astype(wide)
            dz = norm_backward(grad, scaled, inverse, rows[3:4])
            facc[r, :] = dz
            return (
                carry[0] + fold(grad * scaled),
                carry[1] + fold(grad),
                carry[2] + fold(dz.astype(LOW).astype(wide)),
            )

        zero = jnp.zeros((8, width), wide)
        found = lax.fori_loop(0, count // 64, step, (zero, zero, zero))
        for i in range(3):
            sums[i : i + 1, :] = jnp.sum(found[i], axis=0, keepdims=True)

    small_all[me.t] = small[...]
    make_mask(mask, seg_col, seg_row)
    loads[0].wait()
    loads[1].wait()
    for j in range(groups):
        if j == 1:
            for t in tiny:
                t.wait()
        g = group(j)
        ready(0, j)
        project(g)
        if j == 0:
            tick(0)
        attend(g)
        tick(n + j if j else 1)
        combine(g, j == 0)
    loads[2].wait()
    loads[3].wait()
    loads[4].wait()
    first_norm()
    tick(turn.index((1, 1)) + n)
    for j in range(groups):
        g = group(j)
        ready(1, j)
        ffn_up(g)
        if j == 0:
            tick(turn.index((2, 1)) + n)
        ready(2, j)
        ffn_down(g)
        if j == 0:
            tick(turn.index((1, 2)) + n)
    last_norm()
    store(tok, out)
    store(facc, dz_out)
    for a in range(3):
        store(held[a].at[me.t], weights[a].at[me.t])
    for copy in hops.values():
        copy.wait_send()
    for copy in doubles.values():
        copy.wait_send()
    for copy in stores:
        copy.wait()


def forward(shards, inputs, cotangent, small, rows, segments, groups, parts):
    n = parts.bit_length() - 1
    width, count = inputs.shape[1], cotangent.shape[0]
    split = width // groups
    shape = (2,) * n + (width // parts, width)
    packed, seq = segments.shape
    units = 3 * (groups - 1)
    anywhere, vmem = pl.BlockSpec(memory_space=pl.ANY), pl.BlockSpec(memory_space=pltpu.VMEM)
    wide = jnp.float32

    def made(*dims):
        return lambda kind, dtype: kind(dims, dtype)

    tokens, grouped = made(count, width), made(groups, count, width)
    layout = [
        (tokens, LOW),
        (tokens, wide),
        (tokens, wide),
        (made(groups, count, 3 * split), LOW),
        (made(groups, count, split), LOW),
        (grouped, LOW),
        (grouped, LOW),
        (made(groups, count, 128), wide),
    ] + [(made(groups, *shape), LOW)] * 3 + [(made(8, width), wide)]
    dma = pltpu.SemaphoreType.DMA
    outs = pl.pallas_call(
        functools.partial(forward_kernel, groups, parts),
        out_shape=[f(jax.ShapeDtypeStruct, dtype) for f, dtype in layout],
        in_specs=[anywhere] * 5 + [vmem] * 4,
        out_specs=[anywhere] * (len(layout) - 1) + [vmem],
        scratch_shapes=[pltpu.VMEM((groups,) + shape, LOW)] * 3
        + [
            pltpu.VMEM((groups,) + small.shape, LOW),
            pltpu.VMEM((count, width), LOW),
            pltpu.VMEM((packed, seq, seq), wide),
            pltpu.VMEM((count, width), wide),
            pltpu.VMEM((count, width), wide),
            pltpu.VMEM((count, width), LOW),
            pltpu.VMEM((groups, count, 3 * split), LOW),
            pltpu.VMEM((groups, count, split), LOW),
            pltpu.VMEM((groups, count, width), LOW),
            pltpu.VMEM((groups, count, width), LOW),
            pltpu.VMEM((groups, count, 128), wide),
            pltpu.VMEM((count, width), LOW),
            dma((5,)),
            dma((5 * groups + 3 * groups + 3,)),
            dma((units,)),
            dma((units,)),
            dma((units * n * 2,)),
            dma((units * n * 2,)),
            dma((groups - 1,)),
            dma((groups - 1,)),
        ],
        compiler_params=pltpu.CompilerParams(
            collective_id=2, has_side_effects=True, vmem_limit_bytes=63 << 20
        ),
        name="gather_and_forward",
    )(
        *[s.reshape(shape) for s in shards],
        inputs,
        cotangent,
        small,
        rows,
        segments[:, None, :],
        segments[:, :, None],
    )
    weights = [w.reshape(groups, width, width) for w in outs[8:11]]
    return outs[:8], weights, outs[11]


def per_device_small(
    inputs,
    segments,
    w_query,
    w_key,
    w_value,
    b_query,
    b_value,
    w_output,
    b_output,
    gain_attn,
    shift_attn,
    w_hidden,
    b_hidden,
    w_project,
    b_project,
    gain_ffn,
    shift_ffn,
    cotangent,
):
    seq_len = segments.shape[1]
    share_tokens = cotangent.shape[0]
    share_rows = share_tokens // seq_len
    width = inputs.shape[1]
    groups, parts = lax.axis_size("tensor"), lax.axis_size("dp")
    place, part = lax.axis_index("tensor"), lax.axis_index("dp")
    low = jnp.bfloat16
    wide = jnp.float32

    tokens = lax.dynamic_slice_in_dim(inputs, place * share_tokens, share_tokens, 0)
    rows_segments = lax.dynamic_slice_in_dim(segments, place * share_rows, share_rows, 0)
    split = w_query.shape[1]
    small = jnp.concatenate([b_query, b_value, b_hidden]).reshape(-1, 128)
    small_rows = small.shape[0]
    small = jnp.pad(small, ((0, -small_rows % 16), (0, 0)))
    first = jnp.concatenate([w_query, w_key, w_value, w_output.T], axis=1)
    (first, w_up, w_down), small = gather([first, w_hidden, w_project], small, groups, parts)
    w_in = first[:, :, : 3 * split].reshape(groups, width, 3, split).transpose(1, 2, 0, 3)
    w_in = w_in.reshape(width, 3 * groups * split)
    w_out = first[:, :, 3 * split :].transpose(0, 2, 1).reshape(groups * split, width)
    w_up = w_up.transpose(1, 0, 2).reshape(width, -1)
    w_down = w_down.reshape(-1, width)
    small = small[:, :small_rows].reshape(groups, -1).astype(wide)
    bias_query = small[:, :split].reshape(-1)
    bias_value = small[:, split : 2 * split].reshape(-1)
    bias_hidden = small[:, 2 * split :].reshape(-1)
    full = groups * split
    head_shape = (share_rows, seq_len, full // HD, HD)

    attn_gain = gain_attn.astype(wide)
    attn_shift = shift_attn.astype(wide)
    attn_bias = b_output.astype(wide)
    ffn_gain = gain_ffn.astype(wide)
    ffn_shift = shift_ffn.astype(wide)
    ffn_bias = b_project.astype(wide)
    grad_out = cotangent.astype(wide)

    projected = jnp.dot(tokens, w_in, preferred_element_type=wide)
    queries = (projected[:, :full] + bias_query).astype(low)
    keys_in = projected[:, full : 2 * full].astype(low)
    values = (projected[:, 2 * full :] + bias_value).astype(low)
    query_heads = queries.reshape(head_shape)
    key_heads = keys_in.reshape(head_shape)
    value_heads = values.reshape(head_shape)
    mixed_heads, logsum = lax.map(attend_forward, (query_heads, key_heads, value_heads, rows_segments))
    mixed = mixed_heads.reshape(share_tokens, full)
    hidden = tokens.astype(wide) + (jnp.dot(mixed, w_out, preferred_element_type=wide) + attn_bias)
    normed, scaled, inverse = norm_forward(hidden, attn_gain, attn_shift)
    normed_low = normed.astype(low)
    hidden_pre = jnp.dot(normed_low, w_up, preferred_element_type=wide) + bias_hidden
    active, gelu_pull = jax.vjp(gelu_exact, hidden_pre)
    active_low = active.astype(low)
    block_sum = normed + (jnp.dot(active_low, w_down, preferred_element_type=wide) + ffn_bias)
    output, scaled_out, inverse_out = norm_forward(block_sum, ffn_gain, ffn_shift)
    grad_sum = norm_backward(grad_out, scaled_out, inverse_out, ffn_gain)
    grad_ffn_gain = jnp.sum(grad_out * scaled_out, axis=0)
    grad_ffn_shift = jnp.sum(grad_out, axis=0)
    grad_sum_low = grad_sum.astype(low)
    grad_ffn_bias = jnp.sum(grad_sum_low.astype(wide), axis=0)
    grad_active = times_transposed(grad_sum_low, w_down)
    grad_w_down = cross_rows(grad_sum_low, active_low)
    grad_hidden_pre = gelu_pull(grad_active)[0].astype(low)
    grad_b_hidden = jnp.sum(grad_hidden_pre.astype(wide), axis=0)
    grad_w_up = cross_rows(normed_low, grad_hidden_pre)
    grad_normed = grad_sum + times_transposed(grad_hidden_pre, w_up)
    grad_hidden = norm_backward(grad_normed, scaled, inverse, attn_gain)
    grad_hidden_low = grad_hidden.astype(low)
    grad_attn_gain = jnp.sum(grad_normed * scaled, axis=0)
    grad_attn_shift = jnp.sum(grad_normed, axis=0)
    grad_attn_bias = jnp.sum(grad_hidden_low.astype(wide), axis=0)
    grad_w_out = cross_rows(grad_hidden_low, mixed)
    grad_mixed = times_transposed(grad_hidden_low, w_out).astype(low).reshape(head_shape)
    grad_q, grad_k, grad_v = lax.map(
        attend_backward, (query_heads, key_heads, value_heads, rows_segments, logsum, grad_mixed)
    )
    grad_q = grad_q.reshape(share_tokens, full)
    grad_k = grad_k.reshape(share_tokens, full)
    grad_v = grad_v.reshape(share_tokens, full)
    grad_projected = jnp.concatenate([grad_q, grad_k, grad_v], axis=1)
    grad_w_in = cross_rows(tokens, grad_projected)
    grad_b_query = jnp.sum(grad_q.astype(wide), axis=0)
    grad_b_value = jnp.sum(grad_v.astype(wide), axis=0)
    grad_input = grad_hidden + times_transposed(grad_projected, w_in)

    def parted(grad):
        return grad.astype(low).reshape(width, groups, -1).transpose(1, 0, 2)

    first = jnp.concatenate(
        [parted(grad_w_in[:, i * full : (i + 1) * full]) for i in range(3)] + [parted(grad_w_out)], axis=2
    )
    vectors = jnp.concatenate(
        [
            jnp.stack([grad_b_query, grad_b_value]).reshape(2 * groups, split),
            grad_b_hidden.reshape(-1, split),
            jnp.stack(
                [
                    grad_attn_gain,
                    grad_attn_shift,
                    grad_attn_bias,
                    grad_ffn_gain,
                    grad_ffn_shift,
                    grad_ffn_bias,
                ]
            ).reshape(-1, split),
        ],
        axis=0,
    )
    count = vectors.size // split
    vectors = vectors.reshape(-1, 128)
    (sum_first, sum_up, sum_down, vectors) = scatter(
        [first, parted(grad_w_up), parted(grad_w_down)], vectors, groups, parts
    )
    vectors = vectors.reshape(count, split)
    bias_qv = vectors[: 2 * groups].reshape(2, groups, split // HD, HD)
    rest = vectors[2 * groups :]
    hid = bias_hidden.shape[0] // split
    bias_h = rest[:hid].reshape(groups, -1, HD)
    vec = rest[hid:].reshape(6, -1)
    piece = HD // parts
    bias_qv = lax.dynamic_slice_in_dim(bias_qv, place, 1, 1)[:, 0]
    bias_qv = lax.dynamic_slice_in_dim(bias_qv, part * piece, piece, 2)
    bias_h = lax.dynamic_slice_in_dim(bias_h, place, 1, 0)[0]
    bias_h = lax.dynamic_slice_in_dim(bias_h, part * piece, piece, 1)
    piece = width // (parts * groups)
    vec = lax.dynamic_slice_in_dim(vec, (part * groups + place) * piece, piece, 1)
    return (
        output.astype(low),
        grad_input,
        sum_first[:, :split],
        sum_first[:, split : 2 * split],
        sum_first[:, 2 * split : 3 * split],
        sum_first[:, 3 * split :].T,
        sum_up,
        sum_down.T,
        bias_qv,
        bias_h,
        vec,
    )


def per_device(
    inputs,
    segments,
    w_query,
    w_key,
    w_value,
    b_query,
    b_value,
    w_output,
    b_output,
    gain_attn,
    shift_attn,
    w_hidden,
    b_hidden,
    w_project,
    b_project,
    gain_ffn,
    shift_ffn,
    cotangent,
):

    if (inputs.shape[1] // lax.axis_size("dp")) % 16:
        return per_device_small(
            inputs, segments, w_query, w_key, w_value, b_query, b_value, w_output, b_output, gain_attn, shift_attn,
            w_hidden, b_hidden, w_project, b_project, gain_ffn, shift_ffn, cotangent,
        )
    seq_len = segments.shape[1]
    share_tokens = cotangent.shape[0]
    share_rows = share_tokens // seq_len
    width = inputs.shape[1]
    groups, parts = lax.axis_size("tensor"), lax.axis_size("dp")
    place, part = lax.axis_index("tensor"), lax.axis_index("dp")
    low, wide = jnp.bfloat16, jnp.float32
    split = w_query.shape[1]
    nothing = jnp.zeros((split,), low)
    small = jnp.concatenate([b_query, nothing, b_value, nothing, b_hidden]).reshape(2, width)
    small = jnp.pad(small, ((0, 14), (0, 0)))
    nothing = jnp.zeros((width,), low)
    rows = [b_output, gain_attn, shift_attn, gain_ffn, shift_ffn, b_project, nothing, nothing]
    rows = jnp.concatenate(rows).reshape(8, width).astype(wide)
    rows_segments = lax.dynamic_slice_in_dim(segments, place * share_rows, share_rows, 0)
    first = jnp.concatenate([w_query, w_key, w_value, w_output.T], axis=1)
    saved, weights, sums = forward(
        [first, w_hidden, w_project], inputs, cotangent, small, rows, rows_segments, groups, parts
    )
    output, grad_sum, hidden, qkv, mixed, active, slope, lse = saved
    first, w_up, w_down = weights
    tokens = lax.dynamic_slice_in_dim(inputs, place * share_tokens, share_tokens, 0)

    def ein(spec, *terms):
        return jnp.einsum(spec, *terms, preferred_element_type=wide)

    normed, scaled, inverse = norm_forward(hidden, rows[1], rows[2])
    normed_low = normed.astype(low)
    grad_sum_low = grad_sum.astype(low)
    grad_active = ein("td,ghd->gth", grad_sum_low, w_down)
    grad_hidden_pre = (grad_active * slope.astype(wide)).astype(low)
    grad_w_down = ein("td,gth->gdh", grad_sum_low, active)
    grad_b_hidden = jnp.sum(grad_hidden_pre.astype(wide), axis=1)
    grad_w_up = ein("td,gth->gdh", normed_low, grad_hidden_pre)
    grad_normed = grad_sum + ein("gth,gdh->td", grad_hidden_pre, w_up)
    grad_hidden = norm_backward(grad_normed, scaled, inverse, rows[1])
    grad_hidden_low = grad_hidden.astype(low)
    grad_attn_gain = jnp.sum(grad_normed * scaled, axis=0)
    grad_attn_shift = jnp.sum(grad_normed, axis=0)
    grad_attn_bias = jnp.sum(grad_hidden_low.astype(wide), axis=0)
    grad_w_out = ein("td,gth->gdh", grad_hidden_low, mixed)
    grad_mixed = ein("td,gdh->gth", grad_hidden_low, first[:, :, 3 * split :]).astype(low)
    heads = width // HD

    def by_row(x):
        return x.reshape(groups, share_rows, seq_len, -1, HD).transpose(1, 2, 0, 3, 4).reshape(share_rows, seq_len, heads, HD)

    logsum = lse[:, :, : heads // groups].reshape(groups, share_rows, seq_len, -1) / SCORE
    logsum = logsum.transpose(1, 0, 3, 2).reshape(share_rows, heads, seq_len, 1)
    grads = lax.map(
        attend_backward,
        (by_row(qkv[:, :, :split]), by_row(qkv[:, :, split : 2 * split]), by_row(qkv[:, :, 2 * split :]), rows_segments, logsum, by_row(grad_mixed)),
    )
    grads = [g.reshape(share_tokens, groups, split).transpose(1, 0, 2) for g in grads]
    grad_b_query = jnp.sum(grads[0].astype(wide), axis=1)
    grad_b_value = jnp.sum(grads[2].astype(wide), axis=1)
    grads = jnp.concatenate(grads, axis=2)
    grad_w_in = ein("td,gth->gdh", tokens, grads)
    grad_input = grad_hidden + ein("gth,gdh->td", grads, first[:, :, : 3 * split])
    first = jnp.concatenate([grad_w_in, grad_w_out], axis=2)
    vectors = jnp.concatenate(
        [v.reshape(-1) for v in (grad_b_query, grad_b_value, grad_b_hidden, grad_attn_gain, grad_attn_shift, grad_attn_bias)]
        + [sums[:3].reshape(-1)]
    ).reshape(-1, 128)
    (sum_first, sum_up, sum_down, vectors) = scatter(
        [g.astype(low) for g in (first, grad_w_up, grad_w_down)], vectors, groups, parts
    )
    vectors = vectors.reshape(-1, split)

    bias_qv = vectors[: 2 * groups].reshape(2, groups, split // HD, HD)
    rest = vectors[2 * groups :]
    hid = width // split * groups
    bias_h = rest[:hid].reshape(groups, -1, HD)
    vec = rest[hid:].reshape(6, -1)
    piece = HD // parts
    bias_qv = lax.dynamic_slice_in_dim(bias_qv, place, 1, 1)[:, 0]
    bias_qv = lax.dynamic_slice_in_dim(bias_qv, part * piece, piece, 2)
    bias_h = lax.dynamic_slice_in_dim(bias_h, place, 1, 0)[0]
    bias_h = lax.dynamic_slice_in_dim(bias_h, part * piece, piece, 1)
    piece = width // (parts * groups)
    vec = lax.dynamic_slice_in_dim(vec, (part * groups + place) * piece, piece, 1)
    return (
        output.astype(low),
        grad_input,
        sum_first[:, :split],
        sum_first[:, split : 2 * split],
        sum_first[:, 2 * split : 3 * split],
        sum_first[:, 3 * split :].T,
        sum_up,
        sum_down.T,
        bias_qv,
        bias_h,
        vec,
    )


def solution(mesh):
    in_specs = (
        P("dp", None),
        P("dp", None),
        P(None, "tensor"),
        P(None, "tensor"),
        P(None, "tensor"),
        P("tensor"),
        P("tensor"),
        P("tensor", None),
        P(),
        P(),
        P(),
        P(None, "tensor"),
        P("tensor"),
        P("tensor", None),
        P(),
        P(),
        P(),
        P(("dp", "tensor"), None),
    )
    out_specs = (
        P(("dp", "tensor"), None),
        P(("dp", "tensor"), None),
        P("dp", "tensor"),
        P("dp", "tensor"),
        P("dp", "tensor"),
        P("tensor", "dp"),
        P("dp", "tensor"),
        P("tensor", "dp"),
        P(None, "tensor", "dp"),
        P("tensor", "dp"),
        P(None, ("dp", "tensor")),
    )
    return jax.shard_map(
        per_device, mesh=mesh, in_specs=in_specs, out_specs=out_specs, check_vma=False
    )
```

```python
import functools
import jax
import jax.numpy as jnp
from jax import lax
from jax.experimental import pallas as pl
from jax.experimental.pallas import tpu as pltpu
from jax.sharding import PartitionSpec as P

HD = 64
MESH = pl.DeviceIdType.MESH
LOW = jnp.bfloat16


class Place:
    def __init__(self, groups, parts):
        self.groups, self.parts = groups, parts
        self.t, self.d = lax.axis_index("tensor"), lax.axis_index("dp")
        self.count = parts.bit_length() - 1
        self.bits = [(self.d // (1 << i)) % 2 for i in range(self.count)]

    def partner(self, bit):
        return (self.d + (1 - 2 * self.bits[bit]) * (1 << bit), self.t)

    def along(self, step):
        return (self.d, (self.t + step) % self.groups)

    def enter(self):
        barrier = pltpu.get_barrier_semaphore()
        peers = [self.partner(b) for b in range(self.count)]
        peers += [self.along(j) for j in range(1, self.groups)]
        for peer in peers:
            pl.semaphore_signal(barrier, inc=1, device_id=peer, device_id_type=MESH)
        pl.semaphore_wait(barrier, len(peers))

    def pieces(self, open_bits, flipped=None):
        index = []
        for bit in reversed(range(self.count)):
            own = self.bits[bit]
            index.append(slice(None) if bit in open_bits else 1 - own if bit == flipped else own)
        return tuple(index)


def send(src, dst, sems, slot, peer):
    return pltpu.make_async_remote_copy(
        src_ref=src,
        dst_ref=dst,
        send_sem=sems[0].at[slot],
        recv_sem=sems[1].at[slot],
        device_id=peer,
        device_id_type=MESH,
    )


def orders(count):
    rest = list(range(1, count))
    return [rest, rest[::-1]]


def gather_kernel(groups, parts, arrays, *refs):
    shards, small = refs[:arrays], refs[arrays]
    outs, small_out = refs[arrays + 1 : 2 * arrays + 1], refs[2 * arrays + 1]
    held, small_held = refs[2 * arrays + 2 : 3 * arrays + 2], refs[3 * arrays + 2]
    load_sem, store_sem, z_send, z_recv, x_send, x_recv, s_send, s_recv = refs[3 * arrays + 3 :]
    me = Place(groups, parts)
    n = me.count
    half = shards[0].shape[-1] // 2
    bits_order = orders(n)
    me.enter()
    own = [me.t] + list(me.pieces(()))
    hops, doubles, tiny = {}, {}, []
    for j in range(1, groups):
        tiny.append(send(small, small_held.at[j - 1], (s_send, s_recv), j - 1, me.along(j)))
        tiny[-1].start()
    for a in range(arrays):
        for j in range(1, groups):
            u = a * (groups - 1) + j - 1
            hops[u] = send(
                shards[a].at[tuple(me.pieces(()))], held[a].at[tuple(own)], (z_send, z_recv), u, me.along(j)
            )
            hops[u].start()
    loads = []
    for a in range(arrays):
        loads.append(pltpu.make_async_copy(shards[a], held[a].at[me.t], load_sem.at[a]))
        loads[-1].start()

    units = arrays * (groups - 1)
    stores = []

    def advance(u, stage):
        a, j = divmod(u, groups - 1)
        source = (me.t + groups - 1 - j) % groups
        if stage == 0:
            hops[u].wait_recv()
        else:
            for h in range(2):
                if stage < n or h == 0:
                    doubles[u, stage - 1, h].wait_recv()
        if stage == n:
            out = pltpu.make_async_copy(held[a].at[source], outs[a].at[source], store_sem.at[u])
            out.start()
            stores.append(out)
            return
        for h in range(2):
            if stage == n - 1:
                if h == 1:
                    continue
                bit, done, cols = 0, set(range(1, n)), slice(None)
            else:
                bit, done = bits_order[h][stage], set(bits_order[h][:stage])
                cols = pl.ds(h * half, half)
            view = (source,) + me.pieces(done) + (slice(None), cols)
            slot = (u * n + stage) * 2 + h
            copy = send(held[a].at[view], held[a].at[view], (x_send, x_recv), slot, me.partner(bit))
            copy.start()
            doubles[u, stage, h] = copy

    for tick in range(units + n):
        for stage in range(n + 1):
            u = tick - stage
            if 0 <= u < units:
                advance(u, stage)
    for a in range(arrays):
        loads[a].wait()
        out = pltpu.make_async_copy(held[a].at[me.t], outs[a].at[me.t], store_sem.at[units + a])
        out.start()
        stores.append(out)
    small_out[me.t] = small[...]
    for j in range(1, groups):
        tiny[j - 1].wait()
        small_out[(me.t + groups - j) % groups] = small_held[j - 1]
    for copy in hops.values():
        copy.wait_send()
    for copy in doubles.values():
        copy.wait_send()
    for copy in stores:
        copy.wait()


def gather(shards, small, groups, parts):
    arrays, n = len(shards), parts.bit_length() - 1
    rows, cols = shards[0].shape[0] // parts, shards[0].shape[1]
    shape = (2,) * n + (rows, cols)
    units = arrays * (groups - 1)
    any_space = pl.BlockSpec(memory_space=pl.ANY)
    vmem = pl.BlockSpec(memory_space=pltpu.VMEM)
    *outs, small = pl.pallas_call(
        functools.partial(gather_kernel, groups, parts, arrays),
        out_shape=[jax.ShapeDtypeStruct((groups,) + shape, LOW)] * arrays
        + [jax.ShapeDtypeStruct((groups,) + small.shape, LOW)],
        in_specs=[any_space] * arrays + [vmem],
        out_specs=[any_space] * arrays + [vmem],
        scratch_shapes=[pltpu.VMEM((groups,) + shape, LOW)] * arrays
        + [
            pltpu.VMEM((groups - 1,) + small.shape, LOW),
            pltpu.SemaphoreType.DMA((arrays,)),
            pltpu.SemaphoreType.DMA((units + arrays,)),
            pltpu.SemaphoreType.DMA((units,)),
            pltpu.SemaphoreType.DMA((units,)),
            pltpu.SemaphoreType.DMA((units * n * 2,)),
            pltpu.SemaphoreType.DMA((units * n * 2,)),
            pltpu.SemaphoreType.DMA((groups - 1,)),
            pltpu.SemaphoreType.DMA((groups - 1,)),
        ],
        compiler_params=pltpu.CompilerParams(
            collective_id=0, has_side_effects=True, vmem_limit_bytes=60 << 20
        ),
        name="gather_weights",
    )(*[s.reshape(shape) for s in shards], small)
    return [o.reshape(groups, parts * rows, cols) for o in outs], small


def add_into(dst, src, lead):
    def one(i, carry):
        index = []
        for size in reversed(lead):
            index.append(i % size)
            i = i // size
        index = tuple(reversed(index))
        total = dst[index].astype(jnp.float32) + src[index].astype(jnp.float32)
        dst[index] = total.astype(LOW)
        return carry

    total = 1
    for size in lead:
        total *= size
    lax.fori_loop(0, total, one, 0)


def scatter_kernel(groups, parts, arrays, *refs):
    parted, vec = refs[:arrays], refs[arrays]
    outs, vec_out = refs[arrays + 1 : 2 * arrays + 1], refs[2 * arrays + 1]
    p = 2 * arrays + 2
    held = refs[p : p + arrays]
    n = parts.bit_length() - 1
    p += arrays
    landing = refs[p]
    halves = refs[p + 1 : p + n]
    final = refs[p + n]
    load_sem, x_send, x_recv, z_send, z_recv, vec_sum, vec_land, v_send, v_recv = refs[p + n + 1 :]
    me = Place(groups, parts)
    half = parted[0].shape[-1] // 2
    bits_order = orders(n)
    units = arrays * groups
    loads = []
    turn = [(u // groups, (me.t + 1 + u % groups) % groups) for u in range(units)]
    for u in range(units):
        a, target = turn[u]
        copy = pltpu.make_async_copy(parted[a].at[target], held[a].at[target], load_sem.at[u])
        copy.start()
        loads.append(copy)
    me.enter()
    copies, hops, tiny = {}, {}, {}

    def advance_vectors(stage):
        source = vec if stage == 0 else vec_sum.at[stage - 1]
        if stage:
            tiny[stage - 1].wait_recv()
            before = vec[...] if stage == 1 else vec_sum[stage - 2]
            vec_sum[stage - 1] = before + vec_land[stage - 1]
        peers = [me.partner(stage)] if stage < n else [me.along(j) for j in range(1, groups)]
        for k, peer in enumerate(peers):
            copy = send(source, vec_land.at[stage + k], (v_send, v_recv), stage + k, peer)
            copy.start()
            tiny[stage + k] = copy

    def advance(u, stage):
        a, target = turn[u]
        if stage == 0:
            loads[u].wait()
            copy = send(
                held[a].at[(target,) + me.pieces(set(range(1, n)), 0)],
                landing.at[u],
                (x_send, x_recv),
                u * 2 * n,
                me.partner(0),
            )
            copy.start()
            copies[u, 0, 0] = copy
            return
        for h in range(2):
            if stage == 1:
                if h == 1:
                    continue
                left, cols, source = set(range(1, n)), slice(None), landing.at[u]
            else:
                bits = bits_order[h]
                left, cols = set(bits[stage - 1 :]), pl.ds(h * half, half)
                source = halves[stage - 2].at[u, h]
            copies[u, stage - 1, h].wait_recv()
            view = (target,) + me.pieces(left) + (slice(None), cols)
            add_into(held[a].at[view], source, [2] * len(left))
        if stage == n:
            if u % groups < groups - 1:
                j = u % groups + 1
                slot = a * (groups - 1) + j - 1
                hops[slot] = send(
                    held[a].at[(target,) + me.pieces(())], final.at[slot], (z_send, z_recv), slot, me.along(j)
                )
                hops[slot].start()
            return
        for h in range(2):
            bits = bits_order[h]
            bit, left = bits[stage - 1], set(bits[stage:])
            view = (target,) + me.pieces(left, bit) + (slice(None), pl.ds(h * half, half))
            copy = send(
                held[a].at[view],
                halves[stage - 1].at[u, h],
                (x_send, x_recv),
                u * 2 * n + stage * 2 + h,
                me.partner(bit),
            )
            copy.start()
            copies[u, stage, h] = copy

    for tick in range(units + n):
        if tick <= n:
            advance_vectors(tick)
        for stage in reversed(range(n + 1)):
            u = tick - stage
            if 0 <= u < units:
                advance(u, stage)
    total = vec_sum[n - 1]
    for j in range(groups - 1):
        tiny[n + j].wait_recv()
        total = total + vec_land[n + j]
    vec_out[...] = total
    for a in range(arrays):
        total = held[a][(me.t,) + me.pieces(())].astype(jnp.float32)
        for j in range(groups - 1):
            slot = a * (groups - 1) + j
            hops[slot].wait_recv()
            total = total + final[slot].astype(jnp.float32)
        outs[a][...] = total
    for copy in tiny.values():
        copy.wait_send()
    for copy in copies.values():
        copy.wait_send()
    for copy in hops.values():
        copy.wait_send()


def scatter(parted, vec, groups, parts):
    arrays, n = len(parted), parts.bit_length() - 1
    rows, cols = parted[0].shape[1] // parts, parted[0].shape[2]
    shape = (groups,) + (2,) * n + (rows, cols)
    units = arrays * groups
    vmem = pl.BlockSpec(memory_space=pltpu.VMEM)
    return pl.pallas_call(
        functools.partial(scatter_kernel, groups, parts, arrays),
        out_shape=[jax.ShapeDtypeStruct((rows, cols), jnp.float32)] * arrays
        + [jax.ShapeDtypeStruct(vec.shape, jnp.float32)],
        in_specs=[pl.BlockSpec(memory_space=pl.ANY)] * arrays + [vmem],
        out_specs=[vmem] * (arrays + 1),
        scratch_shapes=[pltpu.VMEM(shape, LOW)] * arrays
        + [pltpu.VMEM((units,) + (2,) * (n - 1) + (rows, cols), LOW)]
        + [pltpu.VMEM((units, 2) + (2,) * (n - 1 - s) + (rows, cols // 2), LOW) for s in range(1, n)]
        + [
            pltpu.VMEM((arrays * (groups - 1), rows, cols), LOW),
            pltpu.SemaphoreType.DMA((units,)),
            pltpu.SemaphoreType.DMA((units * 2 * n,)),
            pltpu.SemaphoreType.DMA((units * 2 * n,)),
            pltpu.SemaphoreType.DMA((arrays * (groups - 1),)),
            pltpu.SemaphoreType.DMA((arrays * (groups - 1),)),
            pltpu.VMEM((n,) + vec.shape, jnp.float32),
            pltpu.VMEM((n + groups - 1,) + vec.shape, jnp.float32),
            pltpu.SemaphoreType.DMA((n + groups - 1,)),
            pltpu.SemaphoreType.DMA((n + groups - 1,)),
        ],
        compiler_params=pltpu.CompilerParams(
            collective_id=1, has_side_effects=True, vmem_limit_bytes=60 << 20
        ),
        name="scatter_gradients",
    )(*[g.reshape(shape) for g in parted], vec)


norm_epsilon = 1e-12
root_half = 0.7071067811865476


def norm_forward(values, norm_gain, norm_shift):
    average = jnp.mean(values, axis=-1, keepdims=True)
    centered = values - average
    variance = jnp.mean(centered * centered, axis=-1, keepdims=True)
    inverse = lax.rsqrt(variance + norm_epsilon)
    scaled = centered * inverse
    return (scaled * norm_gain + norm_shift, scaled, inverse)


def norm_backward(grad_out, scaled, inverse, norm_gain):
    weighted = grad_out * norm_gain
    mean_grad = jnp.mean(weighted, axis=-1, keepdims=True)
    mean_proj = jnp.mean(weighted * scaled, axis=-1, keepdims=True)
    return inverse * (weighted - mean_grad - scaled * mean_proj)


def gelu_exact(values):
    return 0.5 * values * (1.0 + lax.erf(values * root_half))


def cross_rows(left, right):
    return lax.dot_general(
        left, right, (((0,), (0,)), ((), ())), preferred_element_type=jnp.float32
    )


def times_transposed(left, right):
    return lax.dot_general(
        left, right, (((1,), (1,)), ((), ())), preferred_element_type=jnp.float32
    )


def masked_scores(queries, keys_in, segment_row):
    same_text = segment_row[:, None] == segment_row[None, :]
    scores = jnp.einsum("qhd,khd->hqk", queries, keys_in, preferred_element_type=jnp.float32)
    scores = scores * queries.shape[2] ** (-0.5)
    return jnp.where(same_text[None], scores, -1000000000.0)


def attend_forward(packed):
    queries, keys_in, values, segment_row = packed
    scores = masked_scores(queries, keys_in, segment_row)
    row_max = jnp.max(scores, axis=-1, keepdims=True)
    exponent = jnp.exp(scores - row_max)
    row_total = jnp.sum(exponent, axis=-1, keepdims=True)
    attn_probs = (exponent / row_total).astype(jnp.bfloat16)
    mixed_heads = jnp.einsum("hqk,khd->qhd", attn_probs, values, preferred_element_type=jnp.float32)
    return (mixed_heads.astype(jnp.bfloat16), row_max + jnp.log(row_total))


def attend_backward(packed):
    queries, keys_in, values, segment_row, logsum, grad_mixed = packed
    score_scale = queries.shape[2] ** (-0.5)
    scores = masked_scores(queries, keys_in, segment_row)
    attn_probs = jnp.exp(scores - logsum)
    grad_probs = jnp.einsum("qhd,khd->hqk", grad_mixed, values, preferred_element_type=jnp.float32)
    grad_values = jnp.einsum(
        "hqk,qhd->khd",
        attn_probs.astype(jnp.bfloat16),
        grad_mixed,
        preferred_element_type=jnp.float32,
    )
    inner_sum = jnp.sum(attn_probs * grad_probs, axis=-1, keepdims=True)
    grad_scores = (attn_probs * (grad_probs - inner_sum)).astype(jnp.bfloat16)
    grad_queries = (
        jnp.einsum("hqk,khd->qhd", grad_scores, keys_in, preferred_element_type=jnp.float32)
        * score_scale
    )
    grad_keys = (
        jnp.einsum("hqk,qhd->khd", grad_scores, queries, preferred_element_type=jnp.float32)
        * score_scale
    )
    return (
        grad_queries.astype(jnp.bfloat16),
        grad_keys.astype(jnp.bfloat16),
        grad_values.astype(jnp.bfloat16),
    )


def matmul_t(left, right):
    return lax.dot_general(left, right, (((1,), (1,)), ((), ())), preferred_element_type=jnp.float32)


TILE = 256
SCORE = 1.4426950408889634


def row_tiles(count, size, body):
    def step(i, carry):
        body(pl.ds(pl.multiple_of(i * size, size), size))
        return carry

    lax.fori_loop(0, count // size, step, 0)


def key_window(block, blocks, span):
    return max(0, block - 1) * span, min(blocks, block + 2) * span


def fold(values):
    return jnp.sum(values.reshape(-1, 8, values.shape[-1]), axis=0)


def make_mask(mask, seg_col, seg_row):
    def step(r, carry):
        mask[r] = jnp.where(seg_col[r] == seg_row[r], 0.0, -1.0e9)
        return carry

    lax.fori_loop(0, mask.shape[0], step, 0)


def forward_kernel(groups, parts, *refs):
    (first, w_hidden, w_project, inputs, cot_in, small, rows, seg_row, seg_col) = refs[:9]
    (out, dz_out, h_out, qkv_out, mixed_out, g_out, gp_out, lse_out, w0_out, w1_out, w2_out, sums) = refs[9:21]
    (held0, held1, held2, small_all, tok, mask, hacc, facc, yb, qkv, mixed, act, slope, lse, cot) = refs[21:36]
    (load_sem, store_sem, z_send, z_recv, x_send, x_recv, s_send, s_recv) = refs[36:]
    me = Place(groups, parts)
    n = me.count
    wide, width = jnp.float32, tok.shape[1]
    count, seq = tok.shape[0], mask.shape[1]
    split = mixed.shape[2]
    heads = split // HD
    shards, held, weights = (first, w_hidden, w_project), (held0, held1, held2), (w0_out, w1_out, w2_out)
    half = width // 2
    bits_order = orders(n)
    loads, stores = [], []

    def load(src, dst):
        loads.append(pltpu.make_async_copy(src, dst, load_sem.at[len(loads)]))
        loads[-1].start()

    def store(src, dst):
        stores.append(pltpu.make_async_copy(src, dst, store_sem.at[len(stores)]))
        stores[-1].start()

    load(first, held0.at[me.t])
    load(inputs.at[pl.ds(me.t * count, count)], tok)
    load(w_hidden, held1.at[me.t])
    load(w_project, held2.at[me.t])
    load(cot_in, cot)
    me.enter()
    mine = me.pieces(())
    turn = [(0, j) for j in range(1, groups)]
    turn += [(a, j) for j in range(1, groups) for a in (1, 2)]
    units = len(turn)
    hops, doubles, tiny = {}, {}, []
    for j in range(1, groups):
        tiny.append(send(small, small_all.at[me.t], (s_send, s_recv), j - 1, me.along(j)))
        tiny[-1].start()
    for u, (a, j) in enumerate(turn):
        hops[u] = send(shards[a].at[mine], held[a].at[(me.t,) + mine], (z_send, z_recv), u, me.along(j))
        hops[u].start()

    def advance(u, stage):
        a, j = turn[u]
        source = (me.t + groups - j) % groups
        if stage == 0:
            hops[u].wait_recv()
        else:
            for h in range(2):
                if stage < n or h == 0:
                    doubles[u, stage - 1, h].wait_recv()
        if stage == n:
            store(held[a].at[source], weights[a].at[source])
            return
        for h in range(2):
            if stage == n - 1:
                if h == 1:
                    continue
                bit, done, cols = 0, set(range(1, n)), slice(None)
            else:
                bit, done = bits_order[h][stage], set(bits_order[h][:stage])
                cols = pl.ds(h * half, half)
            view = (source,) + me.pieces(done) + (slice(None), cols)
            slot = (u * n + stage) * 2 + h
            copy = send(held[a].at[view], held[a].at[view], (x_send, x_recv), slot, me.partner(bit))
            copy.start()
            doubles[u, stage, h] = copy

    ticks = [0]

    def tick(upto):
        while ticks[0] <= upto:
            for stage in range(n + 1):
                u = ticks[0] - stage
                if 0 <= u < units:
                    advance(u, stage)
            ticks[0] += 1

    def ready(a, j):
        if j:
            tick(turn.index((a, j)) + n)

    def group(j):
        return (me.t + groups - j) % groups

    def weight(a, g):
        return held[a][g].reshape(width, width)

    def project(g):
        bias = small_all[g, 0:1, : 3 * split].astype(wide)

        def body(r):
            total = jnp.dot(tok[r, :], weight(0, g)[:, : 3 * split], preferred_element_type=wide)
            qkv[g, r, :] = (total + bias).astype(LOW)

        row_tiles(count, TILE, body)

    span = 128
    blocks = seq // span
    factor = SCORE * HD ** (-0.5)

    def attend(g):
        def packed_row(p, carry):
            base = p * seq
            for b in range(blocks):
                lo, hi = key_window(b, blocks, span)
                rq = pl.ds(pl.multiple_of(base + b * span, span), span)
                rk = pl.ds(pl.multiple_of(base + lo, span), hi - lo)
                bias = mask[p, b * span : (b + 1) * span, lo:hi]
                parts_o, lane = [], lax.broadcasted_iota(jnp.int32, (span, 128), 1)
                kept = jnp.zeros((span, 128), wide)
                for h in range(heads):
                    q = qkv[g, rq, h * HD : (h + 1) * HD]
                    k = qkv[g, rk, split + h * HD : split + (h + 1) * HD]
                    v = qkv[g, rk, 2 * split + h * HD : 2 * split + (h + 1) * HD]
                    s = matmul_t(q, k) * factor + bias
                    top = jnp.max(s, axis=1, keepdims=True)
                    e = jnp.exp2(s - top)
                    total = jnp.sum(e, axis=1, keepdims=True)
                    o = jnp.dot(e.astype(LOW), v, preferred_element_type=wide)
                    parts_o.append(o * (1.0 / total))
                    kept = jnp.where(lane == h, top + jnp.log(total) * SCORE, kept)
                mixed[g, rq, :] = jnp.concatenate(parts_o, axis=1).astype(LOW)
                lse[g, rq, :] = kept
            return carry

        lax.fori_loop(0, count // seq, packed_row, 0)

    def combine(g, start):
        def body(r):
            total = matmul_t(mixed[g, r, :], weight(0, g)[:, 3 * split :])
            if start:
                hacc[r, :] = total + (tok[r, :].astype(wide) + rows[0:1])
            else:
                hacc[r, :] = hacc[r, :] + total

        row_tiles(count, TILE, body)
        store(qkv.at[g], qkv_out.at[g])
        store(mixed.at[g], mixed_out.at[g])
        store(lse.at[g], lse_out.at[g])

    def first_norm():
        def body(r):
            y, _, _ = norm_forward(hacc[r, :], rows[1:2], rows[2:3])
            yb[r, :] = y.astype(LOW)
            facc[r, :] = y + rows[5:6]

        row_tiles(count, 64, body)
        store(hacc, h_out)

    def ffn_up(g):
        bias = small_all[g, 1:2, :].astype(wide)

        def body(r):
            u = jnp.dot(yb[r, :], weight(1, g), preferred_element_type=wide) + bias
            below = 0.5 + 0.5 * lax.erf(u * root_half)
            act[g, r, :] = (u * below).astype(LOW)
            bell = jnp.exp2(u * u * (-0.5 * SCORE)) * 0.3989422804014327
            slope[g, r, :] = (below + u * bell).astype(LOW)

        row_tiles(count, TILE, body)
        store(act.at[g], g_out.at[g])
        store(slope.at[g], gp_out.at[g])

    def ffn_down(g):
        def body(r):
            facc[r, :] = facc[r, :] + jnp.dot(act[g, r, :], weight(2, g), preferred_element_type=wide)

        row_tiles(count, TILE, body)

    def last_norm():
        def step(i, carry):
            r = pl.ds(pl.multiple_of(i * 64, 64), 64)
            y, scaled, inverse = norm_forward(facc[r, :], rows[3:4], rows[4:5])
            tok[r, :] = y.astype(LOW)
            grad = cot[r, :].astype(wide)
            dz = norm_backward(grad, scaled, inverse, rows[3:4])
            facc[r, :] = dz
            return (
                carry[0] + fold(grad * scaled),
                carry[1] + fold(grad),
                carry[2] + fold(dz.astype(LOW).astype(wide)),
            )

        zero = jnp.zeros((8, width), wide)
        found = lax.fori_loop(0, count // 64, step, (zero, zero, zero))
        for i in range(3):
            sums[i : i + 1, :] = jnp.sum(found[i], axis=0, keepdims=True)

    small_all[me.t] = small[...]
    make_mask(mask, seg_col, seg_row)
    loads[0].wait()
    loads[1].wait()
    for j in range(groups):
        if j == 1:
            for t in tiny:
                t.wait()
        g = group(j)
        ready(0, j)
        project(g)
        if j == 0:
            tick(0)
        attend(g)
        tick(n + j if j else 1)
        combine(g, j == 0)
    loads[2].wait()
    loads[3].wait()
    loads[4].wait()
    first_norm()
    tick(turn.index((1, 1)) + n)
    for j in range(groups):
        g = group(j)
        ready(1, j)
        ffn_up(g)
        if j == 0:
            tick(turn.index((2, 1)) + n)
        ready(2, j)
        ffn_down(g)
        if j == 0:
            tick(turn.index((1, 2)) + n)
    last_norm()
    store(tok, out)
    store(facc, dz_out)
    for a in range(3):
        store(held[a].at[me.t], weights[a].at[me.t])
    for copy in hops.values():
        copy.wait_send()
    for copy in doubles.values():
        copy.wait_send()
    for copy in stores:
        copy.wait()


def forward(shards, inputs, cotangent, small, rows, segments, groups, parts):
    n = parts.bit_length() - 1
    width, count = inputs.shape[1], cotangent.shape[0]
    split = width // groups
    shape = (2,) * n + (width // parts, width)
    packed, seq = segments.shape
    units = 3 * (groups - 1)
    anywhere, vmem = pl.BlockSpec(memory_space=pl.ANY), pl.BlockSpec(memory_space=pltpu.VMEM)
    wide = jnp.float32

    def made(*dims):
        return lambda kind, dtype: kind(dims, dtype)

    tokens, grouped = made(count, width), made(groups, count, width)
    layout = [
        (tokens, LOW),
        (tokens, wide),
        (tokens, wide),
        (made(groups, count, 3 * split), LOW),
        (made(groups, count, split), LOW),
        (grouped, LOW),
        (grouped, LOW),
        (made(groups, count, 128), wide),
    ] + [(made(groups, *shape), LOW)] * 3 + [(made(8, width), wide)]
    dma = pltpu.SemaphoreType.DMA
    outs = pl.pallas_call(
        functools.partial(forward_kernel, groups, parts),
        out_shape=[f(jax.ShapeDtypeStruct, dtype) for f, dtype in layout],
        in_specs=[anywhere] * 5 + [vmem] * 4,
        out_specs=[anywhere] * (len(layout) - 1) + [vmem],
        scratch_shapes=[pltpu.VMEM((groups,) + shape, LOW)] * 3
        + [
            pltpu.VMEM((groups,) + small.shape, LOW),
            pltpu.VMEM((count, width), LOW),
            pltpu.VMEM((packed, seq, seq), wide),
            pltpu.VMEM((count, width), wide),
            pltpu.VMEM((count, width), wide),
            pltpu.VMEM((count, width), LOW),
            pltpu.VMEM((groups, count, 3 * split), LOW),
            pltpu.VMEM((groups, count, split), LOW),
            pltpu.VMEM((groups, count, width), LOW),
            pltpu.VMEM((groups, count, width), LOW),
            pltpu.VMEM((groups, count, 128), wide),
            pltpu.VMEM((count, width), LOW),
            dma((5,)),
            dma((5 * groups + 3 * groups + 3,)),
            dma((units,)),
            dma((units,)),
            dma((units * n * 2,)),
            dma((units * n * 2,)),
            dma((groups - 1,)),
            dma((groups - 1,)),
        ],
        compiler_params=pltpu.CompilerParams(
            collective_id=2, has_side_effects=True, vmem_limit_bytes=63 << 20
        ),
        name="gather_and_forward",
    )(
        *[s.reshape(shape) for s in shards],
        inputs,
        cotangent,
        small,
        rows,
        segments[:, None, :],
        segments[:, :, None],
    )
    weights = [w.reshape(groups, width, width) for w in outs[8:11]]
    return outs[:8], weights, outs[11]


def backward_kernel(groups, parts, *refs):
    (dz_in, h_in, qkv_in, mixed_in, act_in, slope_in, lse_in, w0_in, w1_in, w2_in, inputs) = refs[:11]
    rows, seg_row, seg_col, sums = refs[11:15]
    gi_out, out0, out1, out2, vec_out = refs[15:20]
    (held0, held1, held2, landing, final) = refs[20:25]
    (w_buf, d_buf, act, slope, grad, low, low_t, row_t, du, hid, mask, qkv, mixed, lse, dmix, dqkv) = refs[25:41]
    (vec, vec_sum, vec_land) = refs[41:44]
    (load_sem, x_send, x_recv, z_send, z_recv, v_send, v_recv) = refs[44:51]
    halves = refs[51:]
    me = Place(groups, parts)
    n = me.count
    wide, width = jnp.float32, du.shape[1]
    count, seq = du.shape[0], mask.shape[1]
    split = mixed.shape[2]
    heads = split // HD
    held = (held0, held1, held2)
    half = width // 2
    bits_order = orders(n)
    turn = [(a, i) for i in range(groups) for a in (2, 1)] + [(0, i) for i in range(groups)]
    slots = list(range(2 * groups)) + [2 * groups + 1 + 2 * i for i in range(groups)]
    units = len(turn)
    loads = {}

    def load(name, src, dst):
        loads[name] = pltpu.make_async_copy(src, dst, load_sem.at[len(loads)])
        loads[name].start()

    def group(i):
        return (me.t + 1 + i) % groups

    def load_ffn(i):
        load(("slope", i), slope_in.at[group(i)], slope.at[i % 2])
        load(("down", i), w2_in.at[group(i)], d_buf.at[i % 2])
        load(("up", i), w1_in.at[group(i)], w_buf.at[i % 2])
        load(("act", i), act_in.at[group(i)], act.at[i % 2])

    def load_heads(i):
        load(("first", i), w0_in.at[group(i)], w_buf.at[(groups + i) % 2])
        load(("qkv", i), qkv_in.at[group(i)], qkv.at[i % 2])
        load(("mixed", i), mixed_in.at[group(i)], mixed.at[i % 2])
        load(("lse", i), lse_in.at[group(i)], lse.at[i % 2])

    load("grad", dz_in, grad)
    load("hid", h_in, hid)
    load_ffn(0)
    me.enter()
    copies, hops, tiny = {}, {}, {}

    def advance_vectors(stage):
        source = vec if stage == 0 else vec_sum.at[stage - 1]
        if stage:
            tiny[stage - 1].wait_recv()
            before = vec[...] if stage == 1 else vec_sum[stage - 2]
            vec_sum[stage - 1] = before + vec_land[stage - 1]
        peers = [me.partner(stage)] if stage < n else [me.along(j) for j in range(1, groups)]
        for k, peer in enumerate(peers):
            copy = send(source, vec_land.at[stage + k], (v_send, v_recv), stage + k, peer)
            copy.start()
            tiny[stage + k] = copy

    def advance(u, stage):
        a, i = turn[u]
        target = group(i)
        if stage == 0:
            copy = send(
                held[a].at[(target,) + me.pieces(set(range(1, n)), 0)],
                landing.at[u],
                (x_send, x_recv),
                u * 2 * n,
                me.partner(0),
            )
            copy.start()
            copies[u, 0, 0] = copy
            return
        for h in range(2):
            if stage == 1:
                if h == 1:
                    continue
                left, cols, source = set(range(1, n)), slice(None), landing.at[u]
            else:
                bits = bits_order[h]
                left, cols = set(bits[stage - 1 :]), pl.ds(h * half, half)
                source = halves[stage - 2].at[u, h]
            copies[u, stage - 1, h].wait_recv()
            view = (target,) + me.pieces(left) + (slice(None), cols)
            add_into(held[a].at[view], source, [2] * len(left))
        if stage == n:
            if i < groups - 1:
                slot = a * (groups - 1) + i
                hops[slot] = send(
                    held[a].at[(target,) + me.pieces(())], final.at[slot], (z_send, z_recv), slot, me.along(i + 1)
                )
                hops[slot].start()
            return
        for h in range(2):
            bits = bits_order[h]
            bit, left = bits[stage - 1], set(bits[stage:])
            view = (target,) + me.pieces(left, bit) + (slice(None), pl.ds(h * half, half))
            copy = send(
                held[a].at[view],
                halves[stage - 1].at[u, h],
                (x_send, x_recv),
                u * 2 * n + stage * 2 + h,
                me.partner(bit),
            )
            copy.start()
            copies[u, stage, h] = copy

    ticks = [0]

    def tick(upto):
        while ticks[0] <= upto:
            for stage in reversed(range(n + 1)):
                for u in range(units):
                    if slots[u] == ticks[0] - stage:
                        advance(u, stage)
            ticks[0] += 1

    def put(a, g, cols, value):
        shape = held[a].shape[1:-1] + value.shape[1:]
        held[a][(g,) + (slice(None),) * (n + 1) + (cols,)] = value.astype(LOW).reshape(shape)

    def products(a, g, left, right):
        def step(i, carry):
            cols = pl.ds(pl.multiple_of(i * TILE, TILE), TILE)
            put(a, g, cols, jnp.dot(left[...], right[:, cols], preferred_element_type=wide))
            return carry

        lax.fori_loop(0, width // TILE, step, 0)

    def flip(dst, r, value):
        dst[:, r] = value.T

    vec[...] = jnp.zeros_like(vec)
    loads["grad"].wait()
    loads["hid"].wait()

    def prepare(i, carry):
        r = pl.ds(pl.multiple_of(i * 128, 128), 128)
        g = grad[r, :].astype(LOW)
        low[r, :] = g
        flip(low_t, r, g)
        y, _, _ = norm_forward(hid[r, :], rows[1:2], rows[2:3])
        flip(row_t, r, y.astype(LOW))
        return carry

    lax.fori_loop(0, count // 128, prepare, 0)
    make_mask(mask, seg_col, seg_row)

    for i in range(groups):
        g, s = group(i), i % 2
        if i + 1 < groups:
            load_ffn(i + 1)
        else:
            load_heads(0)
        loads["slope", i].wait()
        loads["down", i].wait()
        loads["up", i].wait()
        loads["act", i].wait()
        products(2, g, low_t, act.at[s])
        tick(2 * i)

        def back(k, carry):
            r = pl.ds(pl.multiple_of(k * TILE, TILE), TILE)
            part = matmul_t(low[r, :], d_buf[s])
            part = (part * slope[s, r, :].astype(wide)).astype(LOW)
            du[r, :] = part
            grad[r, :] = grad[r, :] + matmul_t(part, w_buf[s])
            return carry + fold(part.astype(wide))

        total = lax.fori_loop(0, count // TILE, back, jnp.zeros((8, width), wide))
        vec[pl.ds(groups + g, 1), :] = jnp.sum(total, axis=0, keepdims=True)
        products(1, g, row_t, du)
        tick(2 * i + 1)

    load("tokens", inputs.at[pl.ds(me.t * count, count)], du)

    def norm(i, carry):
        r = pl.ds(pl.multiple_of(i * 64, 64), 64)
        _, scaled, inverse = norm_forward(hid[r, :], rows[1:2], rows[2:3])
        dy = grad[r, :]
        dh = norm_backward(dy, scaled, inverse, rows[1:2])
        dh_low = dh.astype(LOW)
        grad[r, :] = dh
        low[r, :] = dh_low
        return (carry[0] + fold(dy * scaled), carry[1] + fold(dy), carry[2] + fold(dh_low.astype(wide)))

    zero = jnp.zeros((8, width), wide)
    found = lax.fori_loop(0, count // 64, norm, (zero, zero, zero))
    for k in range(3):
        vec[2 * groups + k : 2 * groups + k + 1, :] = jnp.sum(found[k], axis=0, keepdims=True)
    vec[2 * groups + 3 : 2 * groups + 6, :] = sums[0:3, :]
    loads["tokens"].wait()

    def turn_over(i, carry):
        r = pl.ds(pl.multiple_of(i * 128, 128), 128)
        flip(low_t, r, low[r, :])
        flip(row_t, r, du[r, :])
        return carry

    lax.fori_loop(0, count // 128, turn_over, 0)
    tick(2 * groups)

    span = 128
    blocks = seq // span
    scale = HD ** (-0.5)
    for i in range(groups):
        g, s, ws = group(i), i % 2, (groups + i) % 2
        if i + 1 < groups:
            load_heads(i + 1)
        for name in ("first", "qkv", "mixed", "lse"):
            loads[name, i].wait()

        def mix(k, carry):
            r = pl.ds(pl.multiple_of(k * TILE, TILE), TILE)
            dmix[r, :] = jnp.dot(low[r, :], w_buf[ws][:, 3 * split :], preferred_element_type=wide).astype(LOW)
            return carry

        lax.fori_loop(0, count // TILE, mix, 0)

        def packed_row(p, carry):
            base = p * seq

            def at(lo, hi):
                return pl.ds(pl.multiple_of(base + lo, span), hi - lo)

            def place(h, lo, hi):
                return h // 2, pl.ds((h % 2) * seq + lo, hi - lo)

            dqs = []
            for b in range(blocks):
                lo, hi = key_window(b, blocks, span)
                mine = (b * span, (b + 1) * span)
                bias = mask[p, mine[0] : mine[1], lo:hi]
                dq = []
                for h in range(heads):
                    q = qkv[s, at(*mine), h * HD : (h + 1) * HD]
                    k = qkv[s, at(lo, hi), split + h * HD : split + (h + 1) * HD]
                    v = qkv[s, at(lo, hi), 2 * split + h * HD : 2 * split + (h + 1) * HD]
                    do = dmix[at(*mine), h * HD : (h + 1) * HD]
                    score = matmul_t(q, k) * (SCORE * scale) + bias
                    prob = jnp.exp2(score - lse[s, at(*mine), h : h + 1])
                    dp = matmul_t(do, v)
                    inner = jnp.sum(prob * dp, axis=1, keepdims=True)
                    ds = (prob * (dp - inner)).astype(LOW)
                    where, sub = place(h, *mine)
                    slope[where, sub, lo:hi] = prob.astype(LOW)
                    act[where, sub, lo:hi] = ds
                    dq.append(jnp.dot(ds, k, preferred_element_type=wide) * scale)
                dqs.append(jnp.concatenate(dq, axis=1))
            for b in range(blocks):
                lo, hi = key_window(b, blocks, span)
                mine = (b * span, (b + 1) * span)
                dk, dv = [], []
                for h in range(heads):
                    where, sub = place(h, lo, hi)
                    q = qkv[s, at(lo, hi), h * HD : (h + 1) * HD]
                    do = dmix[at(lo, hi), h * HD : (h + 1) * HD]
                    dk.append(cross_rows(q, act[where, sub, mine[0] : mine[1]]) * scale)
                    dv.append(cross_rows(do, slope[where, sub, mine[0] : mine[1]]))
                dk = jnp.concatenate(dk, axis=0).T
                dv = jnp.concatenate(dv, axis=0).T
                dqkv[at(*mine), :] = jnp.concatenate([dqs[b], dk, dv], axis=1).astype(LOW)
            return carry

        lax.fori_loop(0, count // seq, packed_row, 0)
        tick(2 * groups + 2 * i)

        def first_cols(k, carry):
            cols = pl.ds(pl.multiple_of(k * TILE, TILE), TILE)
            put(0, g, cols, jnp.dot(row_t[...], dqkv[:, cols], preferred_element_type=wide))
            return carry

        edge = 3 * split // TILE * TILE
        lax.fori_loop(0, edge // TILE, first_cols, 0)
        tail = jnp.concatenate(
            [
                jnp.dot(row_t[...], dqkv[:, edge:], preferred_element_type=wide),
                jnp.dot(low_t[...], mixed[s], preferred_element_type=wide),
            ],
            axis=1,
        )
        put(0, g, slice(edge, width), tail)
        tick(2 * groups + 2 * i + 1)

        def finish(k, carry):
            r = pl.ds(pl.multiple_of(k * TILE, TILE), TILE)
            part = dqkv[r, :]
            grad[r, :] = grad[r, :] + matmul_t(part, w_buf[ws][:, : 3 * split])
            return carry + fold(part.astype(wide))

        total = lax.fori_loop(0, count // TILE, finish, jnp.zeros((8, 3 * split), wide))
        vec[pl.ds(g, 1), : 3 * split] = jnp.sum(total, axis=0, keepdims=True)
    load("result", grad, gi_out)
    last = slots[-1]
    for stage in range(n + 1):
        advance_vectors(stage)
        if stage < n:
            tick(last + 1 + stage)
    total = vec_sum[n - 1]
    for j in range(groups - 1):
        tiny[n + j].wait_recv()
        total = total + vec_land[n + j]
    vec_out[...] = total
    for a, out in ((2, out2), (1, out1), (0, out0)):
        total = held[a][(me.t,) + me.pieces(())].astype(wide)
        for j in range(groups - 1):
            slot = a * (groups - 1) + j
            hops[slot].wait_recv()
            total = total + final[slot].astype(wide)
        out[...] = total
    for copy in list(tiny.values()) + list(copies.values()) + list(hops.values()):
        copy.wait_send()
    loads["result"].wait()


def backward(saved, weights, sums, inputs, rows, segments, groups, parts):
    n = parts.bit_length() - 1
    _, dz, hid, qkv, mixed, act, slope, lse = saved
    count, width = dz.shape
    split = width // groups
    piece = width // parts
    shape = (groups,) + (2,) * n + (piece, width)
    packed, seq = segments.shape
    units = 3 * groups
    anywhere, vmem = pl.BlockSpec(memory_space=pl.ANY), pl.BlockSpec(memory_space=pltpu.VMEM)
    wide, dma = jnp.float32, pltpu.SemaphoreType.DMA
    lines = -(-(2 * groups + 6) // 8) * 8
    return pl.pallas_call(
        functools.partial(backward_kernel, groups, parts),
        out_shape=[jax.ShapeDtypeStruct((count, width), wide)]
        + [jax.ShapeDtypeStruct((piece, width), wide)] * 3
        + [jax.ShapeDtypeStruct((lines, width), wide)],
        in_specs=[anywhere] * 11 + [vmem] * 4,
        out_specs=[anywhere] + [vmem] * 4,
        scratch_shapes=[pltpu.VMEM(shape, LOW)] * 3
        + [
            pltpu.VMEM((units,) + (2,) * (n - 1) + (piece, width), LOW),
            pltpu.VMEM((3 * (groups - 1), piece, width), LOW),
            pltpu.VMEM((2, width, width), LOW),
            pltpu.VMEM((2, width, width), LOW),
            pltpu.VMEM((2, count, width), LOW),
            pltpu.VMEM((2, count, width), LOW),
            pltpu.VMEM((count, width), wide),
            pltpu.VMEM((count, width), LOW),
            pltpu.VMEM((width, count), LOW),
            pltpu.VMEM((width, count), LOW),
            pltpu.VMEM((count, width), LOW),
            pltpu.VMEM((count, width), wide),
            pltpu.VMEM((packed, seq, seq), wide),
            pltpu.VMEM((2, count, 3 * split), LOW),
            pltpu.VMEM((2, count, split), LOW),
            pltpu.VMEM((2, count, 128), wide),
            pltpu.VMEM((count, split), LOW),
            pltpu.VMEM((count, 3 * split), LOW),
            pltpu.VMEM((lines, width), wide),
            pltpu.VMEM((n, lines, width), wide),
            pltpu.VMEM((n + groups - 1, lines, width), wide),
            dma((8 * groups + 4,)),
            dma((units * 2 * n,)),
            dma((units * 2 * n,)),
            dma((3 * (groups - 1),)),
            dma((3 * (groups - 1),)),
            dma((n + groups - 1,)),
            dma((n + groups - 1,)),
        ]
        + [pltpu.VMEM((units, 2) + (2,) * (n - 1 - s) + (piece, width // 2), LOW) for s in range(1, n)],
        compiler_params=pltpu.CompilerParams(
            collective_id=3, has_side_effects=True, vmem_limit_bytes=67043328
        ),
        name="backward_and_scatter",
    )(dz, hid, qkv, mixed, act, slope, lse, *weights, inputs, rows, segments[:, None, :], segments[:, :, None], sums)


def per_device_small(
    inputs,
    segments,
    w_query,
    w_key,
    w_value,
    b_query,
    b_value,
    w_output,
    b_output,
    gain_attn,
    shift_attn,
    w_hidden,
    b_hidden,
    w_project,
    b_project,
    gain_ffn,
    shift_ffn,
    cotangent,
):
    seq_len = segments.shape[1]
    share_tokens = cotangent.shape[0]
    share_rows = share_tokens // seq_len
    width = inputs.shape[1]
    groups, parts = lax.axis_size("tensor"), lax.axis_size("dp")
    place, part = lax.axis_index("tensor"), lax.axis_index("dp")
    low = jnp.bfloat16
    wide = jnp.float32

    tokens = lax.dynamic_slice_in_dim(inputs, place * share_tokens, share_tokens, 0)
    rows_segments = lax.dynamic_slice_in_dim(segments, place * share_rows, share_rows, 0)
    split = w_query.shape[1]
    small = jnp.concatenate([b_query, b_value, b_hidden]).reshape(-1, 128)
    small_rows = small.shape[0]
    small = jnp.pad(small, ((0, -small_rows % 16), (0, 0)))
    first = jnp.concatenate([w_query, w_key, w_value, w_output.T], axis=1)
    (first, w_up, w_down), small = gather([first, w_hidden, w_project], small, groups, parts)
    w_in = first[:, :, : 3 * split].reshape(groups, width, 3, split).transpose(1, 2, 0, 3)
    w_in = w_in.reshape(width, 3 * groups * split)
    w_out = first[:, :, 3 * split :].transpose(0, 2, 1).reshape(groups * split, width)
    w_up = w_up.transpose(1, 0, 2).reshape(width, -1)
    w_down = w_down.reshape(-1, width)
    small = small[:, :small_rows].reshape(groups, -1).astype(wide)
    bias_query = small[:, :split].reshape(-1)
    bias_value = small[:, split : 2 * split].reshape(-1)
    bias_hidden = small[:, 2 * split :].reshape(-1)
    full = groups * split
    head_shape = (share_rows, seq_len, full // HD, HD)

    attn_gain = gain_attn.astype(wide)
    attn_shift = shift_attn.astype(wide)
    attn_bias = b_output.astype(wide)
    ffn_gain = gain_ffn.astype(wide)
    ffn_shift = shift_ffn.astype(wide)
    ffn_bias = b_project.astype(wide)
    grad_out = cotangent.astype(wide)

    projected = jnp.dot(tokens, w_in, preferred_element_type=wide)
    queries = (projected[:, :full] + bias_query).astype(low)
    keys_in = projected[:, full : 2 * full].astype(low)
    values = (projected[:, 2 * full :] + bias_value).astype(low)
    query_heads = queries.reshape(head_shape)
    key_heads = keys_in.reshape(head_shape)
    value_heads = values.reshape(head_shape)
    mixed_heads, logsum = lax.map(attend_forward, (query_heads, key_heads, value_heads, rows_segments))
    mixed = mixed_heads.reshape(share_tokens, full)
    hidden = tokens.astype(wide) + (jnp.dot(mixed, w_out, preferred_element_type=wide) + attn_bias)
    normed, scaled, inverse = norm_forward(hidden, attn_gain, attn_shift)
    normed_low = normed.astype(low)
    hidden_pre = jnp.dot(normed_low, w_up, preferred_element_type=wide) + bias_hidden
    active, gelu_pull = jax.vjp(gelu_exact, hidden_pre)
    active_low = active.astype(low)
    block_sum = normed + (jnp.dot(active_low, w_down, preferred_element_type=wide) + ffn_bias)
    output, scaled_out, inverse_out = norm_forward(block_sum, ffn_gain, ffn_shift)
    grad_sum = norm_backward(grad_out, scaled_out, inverse_out, ffn_gain)
    grad_ffn_gain = jnp.sum(grad_out * scaled_out, axis=0)
    grad_ffn_shift = jnp.sum(grad_out, axis=0)
    grad_sum_low = grad_sum.astype(low)
    grad_ffn_bias = jnp.sum(grad_sum_low.astype(wide), axis=0)
    grad_active = times_transposed(grad_sum_low, w_down)
    grad_w_down = cross_rows(grad_sum_low, active_low)
    grad_hidden_pre = gelu_pull(grad_active)[0].astype(low)
    grad_b_hidden = jnp.sum(grad_hidden_pre.astype(wide), axis=0)
    grad_w_up = cross_rows(normed_low, grad_hidden_pre)
    grad_normed = grad_sum + times_transposed(grad_hidden_pre, w_up)
    grad_hidden = norm_backward(grad_normed, scaled, inverse, attn_gain)
    grad_hidden_low = grad_hidden.astype(low)
    grad_attn_gain = jnp.sum(grad_normed * scaled, axis=0)
    grad_attn_shift = jnp.sum(grad_normed, axis=0)
    grad_attn_bias = jnp.sum(grad_hidden_low.astype(wide), axis=0)
    grad_w_out = cross_rows(grad_hidden_low, mixed)
    grad_mixed = times_transposed(grad_hidden_low, w_out).astype(low).reshape(head_shape)
    grad_q, grad_k, grad_v = lax.map(
        attend_backward, (query_heads, key_heads, value_heads, rows_segments, logsum, grad_mixed)
    )
    grad_q = grad_q.reshape(share_tokens, full)
    grad_k = grad_k.reshape(share_tokens, full)
    grad_v = grad_v.reshape(share_tokens, full)
    grad_projected = jnp.concatenate([grad_q, grad_k, grad_v], axis=1)
    grad_w_in = cross_rows(tokens, grad_projected)
    grad_b_query = jnp.sum(grad_q.astype(wide), axis=0)
    grad_b_value = jnp.sum(grad_v.astype(wide), axis=0)
    grad_input = grad_hidden + times_transposed(grad_projected, w_in)

    def parted(grad):
        return grad.astype(low).reshape(width, groups, -1).transpose(1, 0, 2)

    first = jnp.concatenate(
        [parted(grad_w_in[:, i * full : (i + 1) * full]) for i in range(3)] + [parted(grad_w_out)], axis=2
    )
    vectors = jnp.concatenate(
        [
            jnp.stack([grad_b_query, grad_b_value]).reshape(2 * groups, split),
            grad_b_hidden.reshape(-1, split),
            jnp.stack(
                [
                    grad_attn_gain,
                    grad_attn_shift,
                    grad_attn_bias,
                    grad_ffn_gain,
                    grad_ffn_shift,
                    grad_ffn_bias,
                ]
            ).reshape(-1, split),
        ],
        axis=0,
    )
    count = vectors.size // split
    vectors = vectors.reshape(-1, 128)
    (sum_first, sum_up, sum_down, vectors) = scatter(
        [first, parted(grad_w_up), parted(grad_w_down)], vectors, groups, parts
    )
    vectors = vectors.reshape(count, split)
    bias_qv = vectors[: 2 * groups].reshape(2, groups, split // HD, HD)
    rest = vectors[2 * groups :]
    hid = bias_hidden.shape[0] // split
    bias_h = rest[:hid].reshape(groups, -1, HD)
    vec = rest[hid:].reshape(6, -1)
    piece = HD // parts
    bias_qv = lax.dynamic_slice_in_dim(bias_qv, place, 1, 1)[:, 0]
    bias_qv = lax.dynamic_slice_in_dim(bias_qv, part * piece, piece, 2)
    bias_h = lax.dynamic_slice_in_dim(bias_h, place, 1, 0)[0]
    bias_h = lax.dynamic_slice_in_dim(bias_h, part * piece, piece, 1)
    piece = width // (parts * groups)
    vec = lax.dynamic_slice_in_dim(vec, (part * groups + place) * piece, piece, 1)
    return (
        output.astype(low),
        grad_input,
        sum_first[:, :split],
        sum_first[:, split : 2 * split],
        sum_first[:, 2 * split : 3 * split],
        sum_first[:, 3 * split :].T,
        sum_up,
        sum_down.T,
        bias_qv,
        bias_h,
        vec,
    )


def per_device(
    inputs,
    segments,
    w_query,
    w_key,
    w_value,
    b_query,
    b_value,
    w_output,
    b_output,
    gain_attn,
    shift_attn,
    w_hidden,
    b_hidden,
    w_project,
    b_project,
    gain_ffn,
    shift_ffn,
    cotangent,
):

    if (inputs.shape[1] // lax.axis_size("dp")) % 16:
        return per_device_small(
            inputs, segments, w_query, w_key, w_value, b_query, b_value, w_output, b_output, gain_attn, shift_attn,
            w_hidden, b_hidden, w_project, b_project, gain_ffn, shift_ffn, cotangent,
        )
    seq_len = segments.shape[1]
    share_tokens = cotangent.shape[0]
    share_rows = share_tokens // seq_len
    width = inputs.shape[1]
    groups, parts = lax.axis_size("tensor"), lax.axis_size("dp")
    place, part = lax.axis_index("tensor"), lax.axis_index("dp")
    low, wide = jnp.bfloat16, jnp.float32
    split = w_query.shape[1]
    nothing = jnp.zeros((split,), low)
    small = jnp.concatenate([b_query, nothing, b_value, nothing, b_hidden]).reshape(2, width)
    small = jnp.pad(small, ((0, 14), (0, 0)))
    nothing = jnp.zeros((width,), low)
    rows = [b_output, gain_attn, shift_attn, gain_ffn, shift_ffn, b_project, nothing, nothing]
    rows = jnp.concatenate(rows).reshape(8, width).astype(wide)
    rows_segments = lax.dynamic_slice_in_dim(segments, place * share_rows, share_rows, 0)
    first = jnp.concatenate([w_query, w_key, w_value, w_output.T], axis=1)
    saved, weights, sums = forward(
        [first, w_hidden, w_project], inputs, cotangent, small, rows, rows_segments, groups, parts
    )
    output = saved[0]
    grad_input, sum_first, sum_up, sum_down, vectors = backward(
        saved, weights, sums, inputs, rows, rows_segments, groups, parts
    )
    bias_qv = jnp.stack([vectors[:groups, :split], vectors[:groups, 2 * split : 3 * split]])
    bias_qv = bias_qv.reshape(2, groups, split // HD, HD)
    bias_h = vectors[groups : 2 * groups].reshape(groups, -1, HD)
    vec = vectors[2 * groups : 2 * groups + 6]
    piece = HD // parts
    bias_qv = lax.dynamic_slice_in_dim(bias_qv, place, 1, 1)[:, 0]
    bias_qv = lax.dynamic_slice_in_dim(bias_qv, part * piece, piece, 2)
    bias_h = lax.dynamic_slice_in_dim(bias_h, place, 1, 0)[0]
    bias_h = lax.dynamic_slice_in_dim(bias_h, part * piece, piece, 1)
    piece = width // (parts * groups)
    vec = lax.dynamic_slice_in_dim(vec, (part * groups + place) * piece, piece, 1)
    return (
        output.astype(low),
        grad_input,
        sum_first[:, :split],
        sum_first[:, split : 2 * split],
        sum_first[:, 2 * split : 3 * split],
        sum_first[:, 3 * split :].T,
        sum_up,
        sum_down.T,
        bias_qv,
        bias_h,
        vec,
    )


def solution(mesh):
    in_specs = (
        P("dp", None),
        P("dp", None),
        P(None, "tensor"),
        P(None, "tensor"),
        P(None, "tensor"),
        P("tensor"),
        P("tensor"),
        P("tensor", None),
        P(),
        P(),
        P(),
        P(None, "tensor"),
        P("tensor"),
        P("tensor", None),
        P(),
        P(),
        P(),
        P(("dp", "tensor"), None),
    )
    out_specs = (
        P(("dp", "tensor"), None),
        P(("dp", "tensor"), None),
        P("dp", "tensor"),
        P("dp", "tensor"),
        P("dp", "tensor"),
        P("tensor", "dp"),
        P("dp", "tensor"),
        P("tensor", "dp"),
        P(None, "tensor", "dp"),
        P("tensor", "dp"),
        P(None, ("dp", "tensor")),
    )
    return jax.shard_map(
        per_device, mesh=mesh, in_specs=in_specs, out_specs=out_specs, check_vma=False
    )
```

```python
import functools
import jax
import jax.numpy as jnp
from jax import lax
from jax.experimental import pallas as pl
from jax.experimental.pallas import tpu as pltpu
from jax.sharding import PartitionSpec as P

HD = 64
MESH = pl.DeviceIdType.MESH
LOW = jnp.bfloat16


class Place:
    def __init__(self, groups, parts):
        self.groups, self.parts = groups, parts
        self.t, self.d = lax.axis_index("tensor"), lax.axis_index("dp")
        self.count = parts.bit_length() - 1
        self.bits = [(self.d // (1 << i)) % 2 for i in range(self.count)]

    def partner(self, bit):
        return (self.d + (1 - 2 * self.bits[bit]) * (1 << bit), self.t)

    def along(self, step):
        return (self.d, (self.t + step) % self.groups)

    def enter(self):
        barrier = pltpu.get_barrier_semaphore()
        peers = [self.partner(b) for b in range(self.count)]
        peers += [self.along(j) for j in range(1, self.groups)]
        for peer in peers:
            pl.semaphore_signal(barrier, inc=1, device_id=peer, device_id_type=MESH)
        pl.semaphore_wait(barrier, len(peers))

    def pieces(self, open_bits, flipped=None):
        index = []
        for bit in reversed(range(self.count)):
            own = self.bits[bit]
            index.append(slice(None) if bit in open_bits else 1 - own if bit == flipped else own)
        return tuple(index)


def send(src, dst, sems, slot, peer):
    return pltpu.make_async_remote_copy(
        src_ref=src,
        dst_ref=dst,
        send_sem=sems[0].at[slot],
        recv_sem=sems[1].at[slot],
        device_id=peer,
        device_id_type=MESH,
    )


def orders(count):
    rest = list(range(1, count))
    return [rest, rest[::-1]]


def gather_kernel(groups, parts, arrays, *refs):
    shards, small = refs[:arrays], refs[arrays]
    outs, small_out = refs[arrays + 1 : 2 * arrays + 1], refs[2 * arrays + 1]
    held, small_held = refs[2 * arrays + 2 : 3 * arrays + 2], refs[3 * arrays + 2]
    load_sem, store_sem, z_send, z_recv, x_send, x_recv, s_send, s_recv = refs[3 * arrays + 3 :]
    me = Place(groups, parts)
    n = me.count
    half = shards[0].shape[-1] // 2
    bits_order = orders(n)
    me.enter()
    own = [me.t] + list(me.pieces(()))
    hops, doubles, tiny = {}, {}, []
    for j in range(1, groups):
        tiny.append(send(small, small_held.at[j - 1], (s_send, s_recv), j - 1, me.along(j)))
        tiny[-1].start()
    for a in range(arrays):
        for j in range(1, groups):
            u = a * (groups - 1) + j - 1
            hops[u] = send(
                shards[a].at[tuple(me.pieces(()))], held[a].at[tuple(own)], (z_send, z_recv), u, me.along(j)
            )
            hops[u].start()
    loads = []
    for a in range(arrays):
        loads.append(pltpu.make_async_copy(shards[a], held[a].at[me.t], load_sem.at[a]))
        loads[-1].start()

    units = arrays * (groups - 1)
    stores = []

    def advance(u, stage):
        a, j = divmod(u, groups - 1)
        source = (me.t + groups - 1 - j) % groups
        if stage == 0:
            hops[u].wait_recv()
        else:
            for h in range(2):
                if stage < n or h == 0:
                    doubles[u, stage - 1, h].wait_recv()
        if stage == n:
            out = pltpu.make_async_copy(held[a].at[source], outs[a].at[source], store_sem.at[u])
            out.start()
            stores.append(out)
            return
        for h in range(2):
            if stage == n - 1:
                if h == 1:
                    continue
                bit, done, cols = 0, set(range(1, n)), slice(None)
            else:
                bit, done = bits_order[h][stage], set(bits_order[h][:stage])
                cols = pl.ds(h * half, half)
            view = (source,) + me.pieces(done) + (slice(None), cols)
            slot = (u * n + stage) * 2 + h
            copy = send(held[a].at[view], held[a].at[view], (x_send, x_recv), slot, me.partner(bit))
            copy.start()
            doubles[u, stage, h] = copy

    for tick in range(units + n):
        for stage in range(n + 1):
            u = tick - stage
            if 0 <= u < units:
                advance(u, stage)
    for a in range(arrays):
        loads[a].wait()
        out = pltpu.make_async_copy(held[a].at[me.t], outs[a].at[me.t], store_sem.at[units + a])
        out.start()
        stores.append(out)
    small_out[me.t] = small[...]
    for j in range(1, groups):
        tiny[j - 1].wait()
        small_out[(me.t + groups - j) % groups] = small_held[j - 1]
    for copy in hops.values():
        copy.wait_send()
    for copy in doubles.values():
        copy.wait_send()
    for copy in stores:
        copy.wait()


def gather(shards, small, groups, parts):
    arrays, n = len(shards), parts.bit_length() - 1
    rows, cols = shards[0].shape[0] // parts, shards[0].shape[1]
    shape = (2,) * n + (rows, cols)
    units = arrays * (groups - 1)
    any_space = pl.BlockSpec(memory_space=pl.ANY)
    vmem = pl.BlockSpec(memory_space=pltpu.VMEM)
    *outs, small = pl.pallas_call(
        functools.partial(gather_kernel, groups, parts, arrays),
        out_shape=[jax.ShapeDtypeStruct((groups,) + shape, LOW)] * arrays
        + [jax.ShapeDtypeStruct((groups,) + small.shape, LOW)],
        in_specs=[any_space] * arrays + [vmem],
        out_specs=[any_space] * arrays + [vmem],
        scratch_shapes=[pltpu.VMEM((groups,) + shape, LOW)] * arrays
        + [
            pltpu.VMEM((groups - 1,) + small.shape, LOW),
            pltpu.SemaphoreType.DMA((arrays,)),
            pltpu.SemaphoreType.DMA((units + arrays,)),
            pltpu.SemaphoreType.DMA((units,)),
            pltpu.SemaphoreType.DMA((units,)),
            pltpu.SemaphoreType.DMA((units * n * 2,)),
            pltpu.SemaphoreType.DMA((units * n * 2,)),
            pltpu.SemaphoreType.DMA((groups - 1,)),
            pltpu.SemaphoreType.DMA((groups - 1,)),
        ],
        compiler_params=pltpu.CompilerParams(
            collective_id=0, has_side_effects=True, vmem_limit_bytes=60 << 20
        ),
        name="gather_weights",
    )(*[s.reshape(shape) for s in shards], small)
    return [o.reshape(groups, parts * rows, cols) for o in outs], small


def add_into(dst, src, lead):
    def one(i, carry):
        index = []
        for size in reversed(lead):
            index.append(i % size)
            i = i // size
        index = tuple(reversed(index))
        total = dst[index].astype(jnp.float32) + src[index].astype(jnp.float32)
        dst[index] = total.astype(LOW)
        return carry

    total = 1
    for size in lead:
        total *= size
    lax.fori_loop(0, total, one, 0)


def scatter_kernel(groups, parts, arrays, *refs):
    parted, vec = refs[:arrays], refs[arrays]
    outs, vec_out = refs[arrays + 1 : 2 * arrays + 1], refs[2 * arrays + 1]
    p = 2 * arrays + 2
    held = refs[p : p + arrays]
    n = parts.bit_length() - 1
    p += arrays
    landing = refs[p]
    halves = refs[p + 1 : p + n]
    final = refs[p + n]
    load_sem, x_send, x_recv, z_send, z_recv, vec_sum, vec_land, v_send, v_recv = refs[p + n + 1 :]
    me = Place(groups, parts)
    half = parted[0].shape[-1] // 2
    bits_order = orders(n)
    units = arrays * groups
    loads = []
    turn = [(u // groups, (me.t + 1 + u % groups) % groups) for u in range(units)]
    for u in range(units):
        a, target = turn[u]
        copy = pltpu.make_async_copy(parted[a].at[target], held[a].at[target], load_sem.at[u])
        copy.start()
        loads.append(copy)
    me.enter()
    copies, hops, tiny = {}, {}, {}

    def advance_vectors(stage):
        source = vec if stage == 0 else vec_sum.at[stage - 1]
        if stage:
            tiny[stage - 1].wait_recv()
            before = vec[...] if stage == 1 else vec_sum[stage - 2]
            vec_sum[stage - 1] = before + vec_land[stage - 1]
        peers = [me.partner(stage)] if stage < n else [me.along(j) for j in range(1, groups)]
        for k, peer in enumerate(peers):
            copy = send(source, vec_land.at[stage + k], (v_send, v_recv), stage + k, peer)
            copy.start()
            tiny[stage + k] = copy

    def advance(u, stage):
        a, target = turn[u]
        if stage == 0:
            loads[u].wait()
            copy = send(
                held[a].at[(target,) + me.pieces(set(range(1, n)), 0)],
                landing.at[u],
                (x_send, x_recv),
                u * 2 * n,
                me.partner(0),
            )
            copy.start()
            copies[u, 0, 0] = copy
            return
        for h in range(2):
            if stage == 1:
                if h == 1:
                    continue
                left, cols, source = set(range(1, n)), slice(None), landing.at[u]
            else:
                bits = bits_order[h]
                left, cols = set(bits[stage - 1 :]), pl.ds(h * half, half)
                source = halves[stage - 2].at[u, h]
            copies[u, stage - 1, h].wait_recv()
            view = (target,) + me.pieces(left) + (slice(None), cols)
            add_into(held[a].at[view], source, [2] * len(left))
        if stage == n:
            if u % groups < groups - 1:
                j = u % groups + 1
                slot = a * (groups - 1) + j - 1
                hops[slot] = send(
                    held[a].at[(target,) + me.pieces(())], final.at[slot], (z_send, z_recv), slot, me.along(j)
                )
                hops[slot].start()
            return
        for h in range(2):
            bits = bits_order[h]
            bit, left = bits[stage - 1], set(bits[stage:])
            view = (target,) + me.pieces(left, bit) + (slice(None), pl.ds(h * half, half))
            copy = send(
                held[a].at[view],
                halves[stage - 1].at[u, h],
                (x_send, x_recv),
                u * 2 * n + stage * 2 + h,
                me.partner(bit),
            )
            copy.start()
            copies[u, stage, h] = copy

    for tick in range(units + n):
        if tick <= n:
            advance_vectors(tick)
        for stage in reversed(range(n + 1)):
            u = tick - stage
            if 0 <= u < units:
                advance(u, stage)
    total = vec_sum[n - 1]
    for j in range(groups - 1):
        tiny[n + j].wait_recv()
        total = total + vec_land[n + j]
    vec_out[...] = total
    for a in range(arrays):
        total = held[a][(me.t,) + me.pieces(())].astype(jnp.float32)
        for j in range(groups - 1):
            slot = a * (groups - 1) + j
            hops[slot].wait_recv()
            total = total + final[slot].astype(jnp.float32)
        outs[a][...] = total
    for copy in tiny.values():
        copy.wait_send()
    for copy in copies.values():
        copy.wait_send()
    for copy in hops.values():
        copy.wait_send()


def scatter(parted, vec, groups, parts):
    arrays, n = len(parted), parts.bit_length() - 1
    rows, cols = parted[0].shape[1] // parts, parted[0].shape[2]
    shape = (groups,) + (2,) * n + (rows, cols)
    units = arrays * groups
    vmem = pl.BlockSpec(memory_space=pltpu.VMEM)
    return pl.pallas_call(
        functools.partial(scatter_kernel, groups, parts, arrays),
        out_shape=[jax.ShapeDtypeStruct((rows, cols), jnp.float32)] * arrays
        + [jax.ShapeDtypeStruct(vec.shape, jnp.float32)],
        in_specs=[pl.BlockSpec(memory_space=pl.ANY)] * arrays + [vmem],
        out_specs=[vmem] * (arrays + 1),
        scratch_shapes=[pltpu.VMEM(shape, LOW)] * arrays
        + [pltpu.VMEM((units,) + (2,) * (n - 1) + (rows, cols), LOW)]
        + [pltpu.VMEM((units, 2) + (2,) * (n - 1 - s) + (rows, cols // 2), LOW) for s in range(1, n)]
        + [
            pltpu.VMEM((arrays * (groups - 1), rows, cols), LOW),
            pltpu.SemaphoreType.DMA((units,)),
            pltpu.SemaphoreType.DMA((units * 2 * n,)),
            pltpu.SemaphoreType.DMA((units * 2 * n,)),
            pltpu.SemaphoreType.DMA((arrays * (groups - 1),)),
            pltpu.SemaphoreType.DMA((arrays * (groups - 1),)),
            pltpu.VMEM((n,) + vec.shape, jnp.float32),
            pltpu.VMEM((n + groups - 1,) + vec.shape, jnp.float32),
            pltpu.SemaphoreType.DMA((n + groups - 1,)),
            pltpu.SemaphoreType.DMA((n + groups - 1,)),
        ],
        compiler_params=pltpu.CompilerParams(
            collective_id=1, has_side_effects=True, vmem_limit_bytes=60 << 20
        ),
        name="scatter_gradients",
    )(*[g.reshape(shape) for g in parted], vec)


norm_epsilon = 1e-12
root_half = 0.7071067811865476


def norm_forward(values, norm_gain, norm_shift):
    average = jnp.mean(values, axis=-1, keepdims=True)
    centered = values - average
    variance = jnp.mean(centered * centered, axis=-1, keepdims=True)
    inverse = lax.rsqrt(variance + norm_epsilon)
    scaled = centered * inverse
    return (scaled * norm_gain + norm_shift, scaled, inverse)


def norm_backward(grad_out, scaled, inverse, norm_gain):
    weighted = grad_out * norm_gain
    mean_grad = jnp.mean(weighted, axis=-1, keepdims=True)
    mean_proj = jnp.mean(weighted * scaled, axis=-1, keepdims=True)
    return inverse * (weighted - mean_grad - scaled * mean_proj)


def gelu_exact(values):
    return 0.5 * values * (1.0 + lax.erf(values * root_half))


def cross_rows(left, right):
    return lax.dot_general(
        left, right, (((0,), (0,)), ((), ())), preferred_element_type=jnp.float32
    )


def times_transposed(left, right):
    return lax.dot_general(
        left, right, (((1,), (1,)), ((), ())), preferred_element_type=jnp.float32
    )


def masked_scores(queries, keys_in, segment_row):
    same_text = segment_row[:, None] == segment_row[None, :]
    scores = jnp.einsum("qhd,khd->hqk", queries, keys_in, preferred_element_type=jnp.float32)
    scores = scores * queries.shape[2] ** (-0.5)
    return jnp.where(same_text[None], scores, -1000000000.0)


def attend_forward(packed):
    queries, keys_in, values, segment_row = packed
    scores = masked_scores(queries, keys_in, segment_row)
    row_max = jnp.max(scores, axis=-1, keepdims=True)
    exponent = jnp.exp(scores - row_max)
    row_total = jnp.sum(exponent, axis=-1, keepdims=True)
    attn_probs = (exponent / row_total).astype(jnp.bfloat16)
    mixed_heads = jnp.einsum("hqk,khd->qhd", attn_probs, values, preferred_element_type=jnp.float32)
    return (mixed_heads.astype(jnp.bfloat16), row_max + jnp.log(row_total))


def attend_backward(packed):
    queries, keys_in, values, segment_row, logsum, grad_mixed = packed
    score_scale = queries.shape[2] ** (-0.5)
    scores = masked_scores(queries, keys_in, segment_row)
    attn_probs = jnp.exp(scores - logsum)
    grad_probs = jnp.einsum("qhd,khd->hqk", grad_mixed, values, preferred_element_type=jnp.float32)
    grad_values = jnp.einsum(
        "hqk,qhd->khd",
        attn_probs.astype(jnp.bfloat16),
        grad_mixed,
        preferred_element_type=jnp.float32,
    )
    inner_sum = jnp.sum(attn_probs * grad_probs, axis=-1, keepdims=True)
    grad_scores = (attn_probs * (grad_probs - inner_sum)).astype(jnp.bfloat16)
    grad_queries = (
        jnp.einsum("hqk,khd->qhd", grad_scores, keys_in, preferred_element_type=jnp.float32)
        * score_scale
    )
    grad_keys = (
        jnp.einsum("hqk,qhd->khd", grad_scores, queries, preferred_element_type=jnp.float32)
        * score_scale
    )
    return (
        grad_queries.astype(jnp.bfloat16),
        grad_keys.astype(jnp.bfloat16),
        grad_values.astype(jnp.bfloat16),
    )


def matmul_t(left, right):
    return lax.dot_general(left, right, (((1,), (1,)), ((), ())), preferred_element_type=jnp.float32)


TILE = 256
HOP = (10.0, 6.0, 5.0)
PASS = (8.0, 7.0)
SCORE = 1.4426950408889634


def row_tiles(count, size, body, hook=None):
    def step(i, carry):
        body(pl.ds(pl.multiple_of(i * size, size), size))
        if hook:
            hook(i)
        return carry

    lax.fori_loop(0, count // size, step, 0)


class Plan:
    def __init__(self):
        self.now, self.tasks, self.at = 0.0, [], {}

    def add(self, when, task):
        self.tasks.append((when, task))
        self.tasks.sort(key=lambda pair: pair[0])

    def point(self, name, spent, until=None):
        self.now += spent
        if until is not None:
            whens = [when for when, task in self.tasks if task == until]
            if whens:
                self.now = max(self.now, whens[0])
        self.at[name] = [task for when, task in self.tasks if when <= self.now]
        self.tasks = [pair for pair in self.tasks if pair[0] > self.now]


def at_point(plan, run, count, index, name, extra=None):
    for k in range(count):
        tasks = plan.at.get((name, k), [])
        if tasks:
            condition = index == k
            if extra is not None:
                condition = jnp.logical_and(condition, extra)

            @pl.when(condition)
            def _():
                for task in tasks:
                    run(*task)


def key_window(block, blocks, span):
    return max(0, block - 1) * span, min(blocks, block + 2) * span


def fold(values):
    return jnp.sum(values.reshape(-1, 8, values.shape[-1]), axis=0)


def make_mask(mask, seg_col, seg_row):
    def step(r, carry):
        mask[r] = jnp.where(seg_col[r] == seg_row[r], 0.0, -1.0e9)
        return carry

    lax.fori_loop(0, mask.shape[0], step, 0)


def forward_kernel(groups, parts, *refs):
    (first, w_hidden, w_project, inputs, cot_in, small, rows, seg_row, seg_col) = refs[:9]
    (out, dz_out, h_out, qkv_out, mixed_out, g_out, gp_out, lse_out, w0_out, w1_out, w2_out, sums) = refs[9:21]
    (held0, held1, held2, small_all, tok, mask, hacc, facc, yb, qkv, mixed, act, slope, lse, cot) = refs[21:36]
    (load_sem, store_sem, z_send, z_recv, x_send, x_recv, s_send, s_recv) = refs[36:]
    me = Place(groups, parts)
    n = me.count
    wide, width = jnp.float32, tok.shape[1]
    count, seq = tok.shape[0], mask.shape[1]
    split = mixed.shape[2]
    heads = split // HD
    shards, held, weights = (first, w_hidden, w_project), (held0, held1, held2), (w0_out, w1_out, w2_out)
    half = width // 2
    bits_order = orders(n)
    loads, stores = [], []

    def load(src, dst):
        loads.append(pltpu.make_async_copy(src, dst, load_sem.at[len(loads)]))
        loads[-1].start()

    def store(src, dst, slot):
        return pltpu.make_async_copy(src, dst, store_sem.at[slot])

    load(first, held0.at[me.t])
    load(inputs.at[pl.ds(me.t * count, count)], tok)
    load(w_hidden, held1.at[me.t])
    load(w_project, held2.at[me.t])
    load(cot_in, cot)
    me.enter()
    mine = me.pieces(())
    turn = [(0, j) for j in range(1, groups)]
    turn += [(a, j) for j in range(1, groups) for a in (1, 2)]
    units = len(turn)
    hops, doubles, tiny = {}, {}, []
    for j in range(1, groups):
        tiny.append(send(small, small_all.at[me.t], (s_send, s_recv), j - 1, me.along(j)))
        tiny[-1].start()
    for u, (a, j) in enumerate(turn):
        hops[u] = send(shards[a].at[mine], held[a].at[(me.t,) + mine], (z_send, z_recv), u, me.along(j))
        hops[u].start()
    for u, (a, j) in enumerate(turn):
        source = (me.t + groups - j) % groups
        stores.append(store(held[a].at[source], weights[a].at[source], u))
        for stage in range(n):
            for h in range(2 if stage < n - 1 else 1):
                if stage == n - 1:
                    bit, done, cols = 0, set(range(1, n)), slice(None)
                else:
                    bit, done = bits_order[h][stage], set(bits_order[h][:stage])
                    cols = pl.ds(h * half, half)
                view = (source,) + me.pieces(done) + (slice(None), cols)
                slot = (u * n + stage) * 2 + h
                doubles[u, stage, h] = send(
                    held[a].at[view], held[a].at[view], (x_send, x_recv), slot, me.partner(bit)
                )

    def advance(u, stage):
        for h in range(2):
            if stage == 0:
                if h == 0:
                    hops[u].wait_recv()
            elif (u, stage - 1, h) in doubles:
                doubles[u, stage - 1, h].wait_recv()
        if stage == n:
            stores[u].start()
        for h in range(2):
            if (u, stage, h) in doubles:
                doubles[u, stage, h].start()

    plan = Plan()
    for u in range(units):
        for stage in range(n + 1):
            plan.add(HOP[0] + HOP[1] * u + HOP[2] * stage, (u, stage))
    for j in range(groups):
        plan.point(("start", j), 0.0, (turn.index((0, j)), n) if j else None)
        plan.point(("project", j), 1.8)
        plan.point(("attend", j), 1.7)
        plan.point(("combine", j), 1.7)
        plan.point(("combined", j), 1.0)
    plan.point(("norm", 0), 1.5)
    for j in range(groups):
        plan.point(("up", j), 0.0, (turn.index((1, j)), n) if j else None)
        plan.point(("upped", j), 1.8)
        plan.point(("down", j), 1.8, (turn.index((2, j)), n) if j else None)
        plan.point(("downed", j), 1.3)
        plan.point(("next", j), 1.3)

    def run(index, name, extra=None):
        at_point(plan, advance, groups, index, name, extra)

    def group(j):
        return (me.t + groups - j) % groups

    def weight(a, g):
        return held[a][g].reshape(width, width)

    def project(g):
        bias = small_all[g, 0:1, : 3 * split].astype(wide)

        def body(r):
            total = jnp.dot(tok[r, :], weight(0, g)[:, : 3 * split], preferred_element_type=wide)
            qkv[g, r, :] = (total + bias).astype(LOW)

        row_tiles(count, TILE, body)

    span = 128
    blocks = seq // span
    factor = SCORE * HD ** (-0.5)

    def attend(g, hook):
        def packed_row(p, carry):
            base = p * seq

            def at(lo, hi):
                return pl.ds(pl.multiple_of(base + lo, span), hi - lo)

            turned = qkv[g, at(0, seq), 2 * split :].T
            for b in range(blocks):
                lo, hi = key_window(b, blocks, span)
                here = (b * span, (b + 1) * span)
                bias = mask[p, lo:hi, here[0] : here[1]]
                scores, sums_e, mixes = [], [], []
                for h in range(heads):
                    q = qkv[g, at(*here), h * HD : (h + 1) * HD]
                    k = qkv[g, at(lo, hi), split + h * HD : split + (h + 1) * HD]
                    scores.append(matmul_t(k, q))
                for h in range(heads):
                    s = scores[h] * factor + bias
                    top = jnp.max(s, axis=0, keepdims=True)
                    e = jnp.exp2(s - top)
                    total = jnp.sum(e, axis=0, keepdims=True)
                    lse[g, p * blocks + b, h : h + 1, :] = top + jnp.log(total) * SCORE
                    sums_e.append((e.astype(LOW), total))
                for h in range(heads):
                    e, total = sums_e[h]
                    o = jnp.dot(turned[h * HD : (h + 1) * HD, lo:hi], e, preferred_element_type=wide)
                    mixes.append(o * (1.0 / total))
                mixed[g, at(*here), :] = jnp.concatenate(mixes, axis=0).T.astype(LOW)
            hook(p)
            return carry

        lax.fori_loop(0, count // seq, packed_row, 0)

    def combine(g):
        def body(r):
            hacc[r, :] = hacc[r, :] + matmul_t(mixed[g, r, :], weight(0, g)[:, 3 * split :])

        row_tiles(count, TILE, body)

    def start_sum():
        def body(r):
            hacc[r, :] = tok[r, :].astype(wide) + rows[0:1]

        row_tiles(count, TILE, body)

    def first_norm():
        def body(r):
            y, _, _ = norm_forward(hacc[r, :], rows[1:2], rows[2:3])
            yb[r, :] = y.astype(LOW)
            facc[r, :] = y + rows[5:6]

        row_tiles(count, 64, body)

    def ffn_up(g, hook):
        bias = small_all[g, 1:2, :].astype(wide)

        def body(r):
            u = jnp.dot(yb[r, :], weight(1, g), preferred_element_type=wide) + bias
            below = 0.5 + 0.5 * lax.erf(u * root_half)
            act[g, r, :] = (u * below).astype(LOW)
            bell = jnp.exp2(u * u * (-0.5 * SCORE)) * 0.3989422804014327
            slope[g, r, :] = (below + u * bell).astype(LOW)

        row_tiles(count, TILE, body, hook)

    def ffn_down(g, hook):
        def body(r):
            facc[r, :] = facc[r, :] + jnp.dot(act[g, r, :], weight(2, g), preferred_element_type=wide)

        row_tiles(count, TILE, body, hook)

    def last_norm():
        def step(i, carry):
            r = pl.ds(pl.multiple_of(i * 64, 64), 64)
            y, scaled, inverse = norm_forward(facc[r, :], rows[3:4], rows[4:5])
            tok[r, :] = y.astype(LOW)
            grad = cot[r, :].astype(wide)
            dz = norm_backward(grad, scaled, inverse, rows[3:4])
            facc[r, :] = dz
            return (
                carry[0] + fold(grad * scaled),
                carry[1] + fold(grad),
                carry[2] + fold(dz.astype(LOW).astype(wide)),
            )

        zero = jnp.zeros((8, width), wide)
        found = lax.fori_loop(0, count // 64, step, (zero, zero, zero))
        for i in range(3):
            sums[i : i + 1, :] = jnp.sum(found[i], axis=0, keepdims=True)

    small_all[me.t] = small[...]
    make_mask(mask, seg_col, seg_row)
    loads[0].wait()
    loads[1].wait()
    half_way = count // TILE // 2 - 1
    start_sum()

    def attend_stores(g, j):
        return [
            store(a.at[g], b.at[g], units + groups * i + j)
            for i, (a, b) in enumerate(((qkv, qkv_out), (mixed, mixed_out), (lse, lse_out)))
        ]

    def ffn_stores(g, j):
        return [
            store(a.at[g], b.at[g], units + groups * (3 + i) + j)
            for i, (a, b) in enumerate(((act, g_out), (slope, gp_out)))
        ]

    def attend_group(j, carry):
        @pl.when(j == 1)
        def _():
            for t in tiny:
                t.wait()

        g = group(j)
        run(j, "start")
        project(g)
        run(j, "project")
        attend(g, lambda p: run(j, "attend", p == 0))
        run(j, "combine")
        combine(g)
        for copy in attend_stores(g, j):
            copy.start()
        run(j, "combined")
        return carry

    def ffn_group(j, carry):
        g = group(j)
        run(j, "up")
        ffn_up(g, lambda i: run(j, "upped", i == half_way))
        run(j, "down")
        ffn_down(g, lambda i: run(j, "downed", i == half_way))
        for copy in ffn_stores(g, j):
            copy.start()
        run(j, "next")
        return carry

    lax.fori_loop(0, groups, attend_group, 0)
    for i in range(2, 5):
        loads[i].wait()
    first_norm()
    base = units + 5 * groups
    others = [store(hacc, h_out, base)]
    others[0].start()
    for task in plan.at["norm", 0]:
        advance(*task)
    lax.fori_loop(0, groups, ffn_group, 0)
    for _, task in plan.tasks:
        advance(*task)
    last_norm()
    others += [store(tok, out, base + 1), store(facc, dz_out, base + 2)]
    for a in range(3):
        others.append(store(held[a].at[me.t], weights[a].at[me.t], base + 3 + a))
    for copy in others[1:]:
        copy.start()
    stores += others
    for j in range(groups):
        stores += attend_stores(group(j), j) + ffn_stores(group(j), j)
    for copy in hops.values():
        copy.wait_send()
    for copy in doubles.values():
        copy.wait_send()
    for copy in stores:
        copy.wait()


def forward(shards, inputs, cotangent, small, rows, segments, groups, parts):
    n = parts.bit_length() - 1
    width, count = inputs.shape[1], cotangent.shape[0]
    split = width // groups
    shape = (2,) * n + (width // parts, width)
    packed, seq = segments.shape
    units = 3 * (groups - 1)
    anywhere, vmem = pl.BlockSpec(memory_space=pl.ANY), pl.BlockSpec(memory_space=pltpu.VMEM)
    wide = jnp.float32

    def made(*dims):
        return lambda kind, dtype: kind(dims, dtype)

    tokens, grouped = made(count, width), made(groups, count, width)
    layout = [
        (tokens, LOW),
        (tokens, wide),
        (tokens, wide),
        (made(groups, count, 3 * split), LOW),
        (made(groups, count, split), LOW),
        (grouped, LOW),
        (grouped, LOW),
        (made(groups, packed * seq // 128, 8, 128), wide),
    ] + [(made(groups, *shape), LOW)] * 3 + [(made(8, width), wide)]
    dma = pltpu.SemaphoreType.DMA
    outs = pl.pallas_call(
        functools.partial(forward_kernel, groups, parts),
        out_shape=[f(jax.ShapeDtypeStruct, dtype) for f, dtype in layout],
        in_specs=[anywhere] * 5 + [vmem] * 4,
        out_specs=[anywhere] * (len(layout) - 1) + [vmem],
        scratch_shapes=[pltpu.VMEM((groups,) + shape, LOW)] * 3
        + [
            pltpu.VMEM((groups,) + small.shape, LOW),
            pltpu.VMEM((count, width), LOW),
            pltpu.VMEM((packed, seq, seq), wide),
            pltpu.VMEM((count, width), wide),
            pltpu.VMEM((count, width), wide),
            pltpu.VMEM((count, width), LOW),
            pltpu.VMEM((groups, count, 3 * split), LOW),
            pltpu.VMEM((groups, count, split), LOW),
            pltpu.VMEM((groups, count, width), LOW),
            pltpu.VMEM((groups, count, width), LOW),
            pltpu.VMEM((groups, packed * seq // 128, 8, 128), wide),
            pltpu.VMEM((count, width), LOW),
            dma((5,)),
            dma((units + 5 * groups + 6,)),
            dma((units,)),
            dma((units,)),
            dma((units * n * 2,)),
            dma((units * n * 2,)),
            dma((groups - 1,)),
            dma((groups - 1,)),
        ],
        compiler_params=pltpu.CompilerParams(
            collective_id=2, has_side_effects=True, vmem_limit_bytes=63 << 20
        ),
        name="gather_and_forward",
    )(
        *[s.reshape(shape) for s in shards],
        inputs,
        cotangent,
        small,
        rows,
        segments[:, None, :],
        segments[:, :, None],
    )
    weights = [w.reshape(groups, width, width) for w in outs[8:11]]
    return outs[:8], weights, outs[11]


def backward_kernel(groups, parts, *refs):
    (dz_in, h_in, qkv_in, mixed_in, act_in, slope_in, lse_in, w0_in, w1_in, w2_in, inputs) = refs[:11]
    rows, seg_row, seg_col, sums = refs[11:15]
    gi_out, out0, out1, out2, vec_out = refs[15:20]
    (held0, held1, held2, landing, final) = refs[20:25]
    (w_buf, d_buf, act, slope, grad, low, low_t, row_t, du, hid, mask, qkv, mixed, lse, dmix, dqkv) = refs[25:41]
    (vec, vec_sum, vec_land) = refs[41:44]
    (load_sem, x_send, x_recv, z_send, z_recv, v_send, v_recv) = refs[44:51]
    halves = refs[51:]
    me = Place(groups, parts)
    n = me.count
    wide, width = jnp.float32, du.shape[1]
    count, seq = du.shape[0], mask.shape[1]
    split = mixed.shape[2]
    heads = split // HD
    held = (held0, held1, held2)
    half = width // 2
    bits_order = orders(n)
    turn = [(a, i) for i in range(groups) for a in (2, 1)] + [(0, i) for i in range(groups)]
    slots = list(range(2 * groups)) + [2 * groups + 1 + 2 * i for i in range(groups)]
    units = len(turn)

    def load(slot, src, dst):
        return pltpu.make_async_copy(src, dst, load_sem.at[slot])

    def group(i):
        return (me.t + 1 + i) % groups

    def load_ffn(i):
        g, s = group(i), i % 2
        pairs = ((slope_in, slope), (w2_in, d_buf), (w1_in, w_buf), (act_in, act))
        return [load(4 + 4 * i + k, a.at[g], b.at[s]) for k, (a, b) in enumerate(pairs)]

    def load_heads(i):
        g, s = group(i), i % 2
        pairs = ((w0_in, w_buf.at[(groups + i) % 2]), (qkv_in, qkv.at[s]), (mixed_in, mixed.at[s]), (lse_in, lse.at[s]))
        return [load(4 + 4 * groups + 4 * i + k, a.at[g], b) for k, (a, b) in enumerate(pairs)]

    def start(copies):
        for copy in copies:
            copy.start()

    def finish_all(copies):
        for copy in copies:
            copy.wait()

    entry = [load(0, dz_in, grad), load(1, h_in, hid)]
    start(entry)
    start(load_ffn(0))
    me.enter()
    copies, hops, tiny = {}, {}, {}

    def advance_vectors(stage):
        source = vec if stage == 0 else vec_sum.at[stage - 1]
        if stage:
            tiny[stage - 1].wait_recv()
            before = vec[...] if stage == 1 else vec_sum[stage - 2]
            vec_sum[stage - 1] = before + vec_land[stage - 1]
        peers = [me.partner(stage)] if stage < n else [me.along(j) for j in range(1, groups)]
        for k, peer in enumerate(peers):
            copy = send(source, vec_land.at[stage + k], (v_send, v_recv), stage + k, peer)
            copy.start()
            tiny[stage + k] = copy

    for u, (a, i) in enumerate(turn):
        target = group(i)
        copies[u, 0, 0] = send(
            held[a].at[(target,) + me.pieces(set(range(1, n)), 0)],
            landing.at[u],
            (x_send, x_recv),
            u * 2 * n,
            me.partner(0),
        )
        for stage in range(1, n):
            for h in range(2):
                bits = bits_order[h]
                bit, left = bits[stage - 1], set(bits[stage:])
                copies[u, stage, h] = send(
                    held[a].at[(target,) + me.pieces(left, bit) + (slice(None), pl.ds(h * half, half))],
                    halves[stage - 1].at[u, h],
                    (x_send, x_recv),
                    u * 2 * n + stage * 2 + h,
                    me.partner(bit),
                )
        if i < groups - 1:
            slot = a * (groups - 1) + i
            hops[slot] = send(
                held[a].at[(target,) + me.pieces(())], final.at[slot], (z_send, z_recv), slot, me.along(i + 1)
            )

    def advance(u, stage):
        a, i = turn[u]
        target = group(i)
        for h in range(2):
            if (u, stage - 1, h) not in copies:
                continue
            if stage == 1:
                left, cols, source = set(range(1, n)), slice(None), landing.at[u]
            else:
                left, cols = set(bits_order[h][stage - 1 :]), pl.ds(h * half, half)
                source = halves[stage - 2].at[u, h]
            copies[u, stage - 1, h].wait_recv()
            view = (target,) + me.pieces(left) + (slice(None), cols)
            add_into(held[a].at[view], source, [2] * len(left))
        if stage == n and i < groups - 1:
            hops[a * (groups - 1) + i].start()
        for h in range(2):
            if (u, stage, h) in copies:
                copies[u, stage, h].start()

    plan = Plan()
    before = [-100.0] * (n + 1)

    def made(u):
        for stage in range(n + 1):
            when = plan.now + PASS[0] * stage
            if stage:
                when = max(when, before[stage] + PASS[1], before[stage - 1] + PASS[0])
            before[stage] = when
            plan.add(when, (u, stage))

    for i in range(groups):
        plan.now += 2.8
        made(2 * i)
        plan.point(("down", i), 0.0)
        plan.point(("back", i), 2.8)
        plan.point(("backed", i), 2.8)
        plan.now += 2.8
        made(2 * i + 1)
        plan.point(("up", i), 0.0)
    plan.point(("norm", 0), 3.0)
    plan.point(("norm", 1), 2.0)
    for i in range(groups):
        plan.point(("mix", i), 1.0)
        plan.point(("attend", i), 3.0)
        plan.point(("attended", i), 3.0)
        plan.now += 2.8
        made(2 * groups + i)
        plan.point(("first", i), 0.0)
        plan.point(("finish", i), 2.2)

    def run(index, name, extra=None):
        at_point(plan, advance, groups, index, name, extra)

    def put(a, g, cols, value):
        shape = held[a].shape[1:-1] + value.shape[1:]
        held[a][(g,) + (slice(None),) * (n + 1) + (cols,)] = value.astype(LOW).reshape(shape)

    def products(a, g, left, right):
        def step(i, carry):
            cols = pl.ds(pl.multiple_of(i * TILE, TILE), TILE)
            put(a, g, cols, jnp.dot(left[...], right[:, cols], preferred_element_type=wide))
            return carry

        lax.fori_loop(0, width // TILE, step, 0)

    def flip(dst, r, value):
        dst[:, r] = value.T

    vec[...] = jnp.zeros_like(vec)
    finish_all(entry)

    def prepare(i, carry):
        r = pl.ds(pl.multiple_of(i * 128, 128), 128)
        g = grad[r, :].astype(LOW)
        low[r, :] = g
        flip(low_t, r, g)
        y, _, _ = norm_forward(hid[r, :], rows[1:2], rows[2:3])
        flip(row_t, r, y.astype(LOW))
        return carry

    lax.fori_loop(0, count // 128, prepare, 0)
    make_mask(mask, seg_col, seg_row)

    half_way = count // TILE // 2 - 1

    def ffn_group(i, outer):
        g, s = group(i), i % 2

        @pl.when(i + 1 < groups)
        def _():
            start(load_ffn(i + 1))

        @pl.when(i + 1 == groups)
        def _():
            start(load_heads(0))

        finish_all(load_ffn(i))
        products(2, g, low_t, act.at[s])
        run(i, "down")

        def back(k, carry):
            r = pl.ds(pl.multiple_of(k * TILE, TILE), TILE)
            part = matmul_t(low[r, :], d_buf[s])
            part = (part * slope[s, r, :].astype(wide)).astype(LOW)
            du[r, :] = part
            grad[r, :] = grad[r, :] + matmul_t(part, w_buf[s])
            run(i, "back", k == half_way)
            return carry + fold(part.astype(wide))

        total = lax.fori_loop(0, count // TILE, back, jnp.zeros((8, width), wide))
        vec[pl.ds(groups + g, 1), :] = jnp.sum(total, axis=0, keepdims=True)
        run(i, "backed")
        products(1, g, row_t, du)
        run(i, "up")
        return outer

    lax.fori_loop(0, groups, ffn_group, 0)
    tokens = load(2, inputs.at[pl.ds(me.t * count, count)], du)
    tokens.start()

    def norm(i, carry):
        r = pl.ds(pl.multiple_of(i * 64, 64), 64)
        _, scaled, inverse = norm_forward(hid[r, :], rows[1:2], rows[2:3])
        dy = grad[r, :]
        dh = norm_backward(dy, scaled, inverse, rows[1:2])
        dh_low = dh.astype(LOW)
        grad[r, :] = dh
        low[r, :] = dh_low
        return (carry[0] + fold(dy * scaled), carry[1] + fold(dy), carry[2] + fold(dh_low.astype(wide)))

    zero = jnp.zeros((8, width), wide)
    found = lax.fori_loop(0, count // 64, norm, (zero, zero, zero))
    for k in range(3):
        vec[2 * groups + k : 2 * groups + k + 1, :] = jnp.sum(found[k], axis=0, keepdims=True)
    vec[2 * groups + 3 : 2 * groups + 6, :] = sums[0:3, :]
    for task in plan.at["norm", 0]:
        advance(*task)
    tokens.wait()

    def turn_over(i, carry):
        r = pl.ds(pl.multiple_of(i * 128, 128), 128)
        flip(low_t, r, low[r, :])
        flip(row_t, r, du[r, :])
        return carry

    lax.fori_loop(0, count // 128, turn_over, 0)
    for task in plan.at["norm", 1]:
        advance(*task)

    span = 128
    blocks = seq // span
    scale = HD ** (-0.5)

    def heads_group(i, outer):
        g, s, ws = group(i), i % 2, (groups + i) % 2

        @pl.when(i + 1 < groups)
        def _():
            start(load_heads(i + 1))

        finish_all(load_heads(i))

        def mix(k, carry):
            r = pl.ds(pl.multiple_of(k * TILE, TILE), TILE)
            dmix[r, :] = jnp.dot(low[r, :], w_buf[ws][:, 3 * split :], preferred_element_type=wide).astype(LOW)
            return carry

        lax.fori_loop(0, count // TILE, mix, 0)
        run(i, "mix")

        def packed_row(p, carry):
            base = p * seq

            def at(lo, hi):
                return pl.ds(pl.multiple_of(base + lo, span), hi - lo)

            turned = qkv[s, at(0, seq), split : 2 * split].T
            dks = [[None] * heads for _ in range(blocks)]
            dvs = [[None] * heads for _ in range(blocks)]
            dqs = []

            def gather_sum(total, lo, h, value):
                for c in range(value.shape[0] // span):
                    piece = value[c * span : (c + 1) * span]
                    old = total[lo // span + c][h]
                    total[lo // span + c][h] = piece if old is None else old + piece

            def write(b):
                parts_b = [dqs[b]] + [x * scale for x in dks[b]] + dvs[b]
                dqkv[at(b * span, (b + 1) * span), :] = jnp.concatenate(parts_b, axis=1).astype(LOW)

            for b in range(blocks):
                lo, hi = key_window(b, blocks, span)
                here = (b * span, (b + 1) * span)
                bias = mask[p, lo:hi, here[0] : here[1]]
                work, grads = [], []
                for h in range(heads):
                    q = qkv[s, at(*here), h * HD : (h + 1) * HD]
                    k = qkv[s, at(lo, hi), split + h * HD : split + (h + 1) * HD]
                    v = qkv[s, at(lo, hi), 2 * split + h * HD : 2 * split + (h + 1) * HD]
                    do = dmix[at(*here), h * HD : (h + 1) * HD]
                    work.append((q, do, matmul_t(k, q), matmul_t(v, do)))
                for h in range(heads):
                    q, do, score, dp = work[h]
                    prob = jnp.exp2(score * (SCORE * scale) + bias - lse[s, p * blocks + b, h : h + 1, :])
                    inner = jnp.sum(prob * dp, axis=0, keepdims=True)
                    grads.append((prob.astype(LOW), (prob * (dp - inner)).astype(LOW)))
                dq = []
                for h in range(heads):
                    q, do, _, _ = work[h]
                    prob, ds = grads[h]
                    gather_sum(dvs, lo, h, jnp.dot(prob, do, preferred_element_type=wide))
                    gather_sum(dks, lo, h, jnp.dot(ds, q, preferred_element_type=wide))
                    dq.append(jnp.dot(turned[h * HD : (h + 1) * HD, lo:hi], ds, preferred_element_type=wide))
                dqs.append(jnp.concatenate(dq, axis=0).T * scale)
                if b:
                    write(b - 1)
            write(blocks - 1)
            run(i, "attend", p == 0)
            return carry

        lax.fori_loop(0, count // seq, packed_row, 0)
        run(i, "attended")

        def first_cols(k, carry):
            cols = pl.ds(pl.multiple_of(k * TILE, TILE), TILE)
            put(0, g, cols, jnp.dot(row_t[...], dqkv[:, cols], preferred_element_type=wide))
            return carry

        edge = 3 * split // TILE * TILE
        lax.fori_loop(0, edge // TILE, first_cols, 0)
        tail = jnp.concatenate(
            [
                jnp.dot(row_t[...], dqkv[:, edge:], preferred_element_type=wide),
                jnp.dot(low_t[...], mixed[s], preferred_element_type=wide),
            ],
            axis=1,
        )
        put(0, g, slice(edge, width), tail)
        run(i, "first")

        def finish(k, carry):
            r = pl.ds(pl.multiple_of(k * TILE, TILE), TILE)
            part = dqkv[r, :]
            grad[r, :] = grad[r, :] + matmul_t(part, w_buf[ws][:, : 3 * split])
            return carry + fold(part.astype(wide))

        total = lax.fori_loop(0, count // TILE, finish, jnp.zeros((8, 3 * split), wide))
        vec[pl.ds(g, 1), : 3 * split] = jnp.sum(total, axis=0, keepdims=True)
        run(i, "finish")
        return outer

    lax.fori_loop(0, groups, heads_group, 0)
    result = load(3, grad, gi_out)
    result.start()
    rest = [task for _, task in plan.tasks]
    for stage in range(n + 1):
        advance_vectors(stage)
        for task in rest[:2] if stage < n else rest:
            advance(*task)
        rest = rest[2:]
    total = vec_sum[n - 1]
    for j in range(groups - 1):
        tiny[n + j].wait_recv()
        total = total + vec_land[n + j]
    vec_out[...] = total
    for a, out in ((2, out2), (1, out1), (0, out0)):
        total = held[a][(me.t,) + me.pieces(())].astype(wide)
        for j in range(groups - 1):
            slot = a * (groups - 1) + j
            hops[slot].wait_recv()
            total = total + final[slot].astype(wide)
        out[...] = total
    for copy in list(tiny.values()) + list(copies.values()) + list(hops.values()):
        copy.wait_send()
    result.wait()


def backward(saved, weights, sums, inputs, rows, segments, groups, parts):
    n = parts.bit_length() - 1
    _, dz, hid, qkv, mixed, act, slope, lse = saved
    count, width = dz.shape
    split = width // groups
    piece = width // parts
    shape = (groups,) + (2,) * n + (piece, width)
    packed, seq = segments.shape
    units = 3 * groups
    anywhere, vmem = pl.BlockSpec(memory_space=pl.ANY), pl.BlockSpec(memory_space=pltpu.VMEM)
    wide, dma = jnp.float32, pltpu.SemaphoreType.DMA
    lines = -(-(2 * groups + 6) // 8) * 8
    return pl.pallas_call(
        functools.partial(backward_kernel, groups, parts),
        out_shape=[jax.ShapeDtypeStruct((count, width), wide)]
        + [jax.ShapeDtypeStruct((piece, width), wide)] * 3
        + [jax.ShapeDtypeStruct((lines, width), wide)],
        in_specs=[anywhere] * 11 + [vmem] * 4,
        out_specs=[anywhere] + [vmem] * 4,
        scratch_shapes=[pltpu.VMEM(shape, LOW)] * 3
        + [
            pltpu.VMEM((units,) + (2,) * (n - 1) + (piece, width), LOW),
            pltpu.VMEM((3 * (groups - 1), piece, width), LOW),
            pltpu.VMEM((2, width, width), LOW),
            pltpu.VMEM((2, width, width), LOW),
            pltpu.VMEM((2, count, width), LOW),
            pltpu.VMEM((2, count, width), LOW),
            pltpu.VMEM((count, width), wide),
            pltpu.VMEM((count, width), LOW),
            pltpu.VMEM((width, count), LOW),
            pltpu.VMEM((width, count), LOW),
            pltpu.VMEM((count, width), LOW),
            pltpu.VMEM((count, width), wide),
            pltpu.VMEM((packed, seq, seq), wide),
            pltpu.VMEM((2, count, 3 * split), LOW),
            pltpu.VMEM((2, count, split), LOW),
            pltpu.VMEM((2, count // 128, 8, 128), wide),
            pltpu.VMEM((count, split), LOW),
            pltpu.VMEM((count, 3 * split), LOW),
            pltpu.VMEM((lines, width), wide),
            pltpu.VMEM((n, lines, width), wide),
            pltpu.VMEM((n + groups - 1, lines, width), wide),
            dma((8 * groups + 4,)),
            dma((units * 2 * n,)),
            dma((units * 2 * n,)),
            dma((3 * (groups - 1),)),
            dma((3 * (groups - 1),)),
            dma((n + groups - 1,)),
            dma((n + groups - 1,)),
        ]
        + [pltpu.VMEM((units, 2) + (2,) * (n - 1 - s) + (piece, width // 2), LOW) for s in range(1, n)],
        compiler_params=pltpu.CompilerParams(
            collective_id=3, has_side_effects=True, vmem_limit_bytes=67043328
        ),
        name="backward_and_scatter",
    )(dz, hid, qkv, mixed, act, slope, lse, *weights, inputs, rows, segments[:, None, :], segments[:, :, None], sums)


def per_device_small(
    inputs,
    segments,
    w_query,
    w_key,
    w_value,
    b_query,
    b_value,
    w_output,
    b_output,
    gain_attn,
    shift_attn,
    w_hidden,
    b_hidden,
    w_project,
    b_project,
    gain_ffn,
    shift_ffn,
    cotangent,
):
    seq_len = segments.shape[1]
    share_tokens = cotangent.shape[0]
    share_rows = share_tokens // seq_len
    width = inputs.shape[1]
    groups, parts = lax.axis_size("tensor"), lax.axis_size("dp")
    place, part = lax.axis_index("tensor"), lax.axis_index("dp")
    low = jnp.bfloat16
    wide = jnp.float32

    tokens = lax.dynamic_slice_in_dim(inputs, place * share_tokens, share_tokens, 0)
    rows_segments = lax.dynamic_slice_in_dim(segments, place * share_rows, share_rows, 0)
    split = w_query.shape[1]
    small = jnp.concatenate([b_query, b_value, b_hidden]).reshape(-1, 128)
    small_rows = small.shape[0]
    small = jnp.pad(small, ((0, -small_rows % 16), (0, 0)))
    first = jnp.concatenate([w_query, w_key, w_value, w_output.T], axis=1)
    (first, w_up, w_down), small = gather([first, w_hidden, w_project], small, groups, parts)
    w_in = first[:, :, : 3 * split].reshape(groups, width, 3, split).transpose(1, 2, 0, 3)
    w_in = w_in.reshape(width, 3 * groups * split)
    w_out = first[:, :, 3 * split :].transpose(0, 2, 1).reshape(groups * split, width)
    w_up = w_up.transpose(1, 0, 2).reshape(width, -1)
    w_down = w_down.reshape(-1, width)
    small = small[:, :small_rows].reshape(groups, -1).astype(wide)
    bias_query = small[:, :split].reshape(-1)
    bias_value = small[:, split : 2 * split].reshape(-1)
    bias_hidden = small[:, 2 * split :].reshape(-1)
    full = groups * split
    head_shape = (share_rows, seq_len, full // HD, HD)

    attn_gain = gain_attn.astype(wide)
    attn_shift = shift_attn.astype(wide)
    attn_bias = b_output.astype(wide)
    ffn_gain = gain_ffn.astype(wide)
    ffn_shift = shift_ffn.astype(wide)
    ffn_bias = b_project.astype(wide)
    grad_out = cotangent.astype(wide)

    projected = jnp.dot(tokens, w_in, preferred_element_type=wide)
    queries = (projected[:, :full] + bias_query).astype(low)
    keys_in = projected[:, full : 2 * full].astype(low)
    values = (projected[:, 2 * full :] + bias_value).astype(low)
    query_heads = queries.reshape(head_shape)
    key_heads = keys_in.reshape(head_shape)
    value_heads = values.reshape(head_shape)
    mixed_heads, logsum = lax.map(attend_forward, (query_heads, key_heads, value_heads, rows_segments))
    mixed = mixed_heads.reshape(share_tokens, full)
    hidden = tokens.astype(wide) + (jnp.dot(mixed, w_out, preferred_element_type=wide) + attn_bias)
    normed, scaled, inverse = norm_forward(hidden, attn_gain, attn_shift)
    normed_low = normed.astype(low)
    hidden_pre = jnp.dot(normed_low, w_up, preferred_element_type=wide) + bias_hidden
    active, gelu_pull = jax.vjp(gelu_exact, hidden_pre)
    active_low = active.astype(low)
    block_sum = normed + (jnp.dot(active_low, w_down, preferred_element_type=wide) + ffn_bias)
    output, scaled_out, inverse_out = norm_forward(block_sum, ffn_gain, ffn_shift)
    grad_sum = norm_backward(grad_out, scaled_out, inverse_out, ffn_gain)
    grad_ffn_gain = jnp.sum(grad_out * scaled_out, axis=0)
    grad_ffn_shift = jnp.sum(grad_out, axis=0)
    grad_sum_low = grad_sum.astype(low)
    grad_ffn_bias = jnp.sum(grad_sum_low.astype(wide), axis=0)
    grad_active = times_transposed(grad_sum_low, w_down)
    grad_w_down = cross_rows(grad_sum_low, active_low)
    grad_hidden_pre = gelu_pull(grad_active)[0].astype(low)
    grad_b_hidden = jnp.sum(grad_hidden_pre.astype(wide), axis=0)
    grad_w_up = cross_rows(normed_low, grad_hidden_pre)
    grad_normed = grad_sum + times_transposed(grad_hidden_pre, w_up)
    grad_hidden = norm_backward(grad_normed, scaled, inverse, attn_gain)
    grad_hidden_low = grad_hidden.astype(low)
    grad_attn_gain = jnp.sum(grad_normed * scaled, axis=0)
    grad_attn_shift = jnp.sum(grad_normed, axis=0)
    grad_attn_bias = jnp.sum(grad_hidden_low.astype(wide), axis=0)
    grad_w_out = cross_rows(grad_hidden_low, mixed)
    grad_mixed = times_transposed(grad_hidden_low, w_out).astype(low).reshape(head_shape)
    grad_q, grad_k, grad_v = lax.map(
        attend_backward, (query_heads, key_heads, value_heads, rows_segments, logsum, grad_mixed)
    )
    grad_q = grad_q.reshape(share_tokens, full)
    grad_k = grad_k.reshape(share_tokens, full)
    grad_v = grad_v.reshape(share_tokens, full)
    grad_projected = jnp.concatenate([grad_q, grad_k, grad_v], axis=1)
    grad_w_in = cross_rows(tokens, grad_projected)
    grad_b_query = jnp.sum(grad_q.astype(wide), axis=0)
    grad_b_value = jnp.sum(grad_v.astype(wide), axis=0)
    grad_input = grad_hidden + times_transposed(grad_projected, w_in)

    def parted(grad):
        return grad.astype(low).reshape(width, groups, -1).transpose(1, 0, 2)

    first = jnp.concatenate(
        [parted(grad_w_in[:, i * full : (i + 1) * full]) for i in range(3)] + [parted(grad_w_out)], axis=2
    )
    vectors = jnp.concatenate(
        [
            jnp.stack([grad_b_query, grad_b_value]).reshape(2 * groups, split),
            grad_b_hidden.reshape(-1, split),
            jnp.stack(
                [
                    grad_attn_gain,
                    grad_attn_shift,
                    grad_attn_bias,
                    grad_ffn_gain,
                    grad_ffn_shift,
                    grad_ffn_bias,
                ]
            ).reshape(-1, split),
        ],
        axis=0,
    )
    count = vectors.size // split
    vectors = vectors.reshape(-1, 128)
    (sum_first, sum_up, sum_down, vectors) = scatter(
        [first, parted(grad_w_up), parted(grad_w_down)], vectors, groups, parts
    )
    vectors = vectors.reshape(count, split)
    bias_qv = vectors[: 2 * groups].reshape(2, groups, split // HD, HD)
    rest = vectors[2 * groups :]
    hid = bias_hidden.shape[0] // split
    bias_h = rest[:hid].reshape(groups, -1, HD)
    vec = rest[hid:].reshape(6, -1)
    piece = HD // parts
    bias_qv = lax.dynamic_slice_in_dim(bias_qv, place, 1, 1)[:, 0]
    bias_qv = lax.dynamic_slice_in_dim(bias_qv, part * piece, piece, 2)
    bias_h = lax.dynamic_slice_in_dim(bias_h, place, 1, 0)[0]
    bias_h = lax.dynamic_slice_in_dim(bias_h, part * piece, piece, 1)
    piece = width // (parts * groups)
    vec = lax.dynamic_slice_in_dim(vec, (part * groups + place) * piece, piece, 1)
    return (
        output.astype(low),
        grad_input,
        sum_first[:, :split],
        sum_first[:, split : 2 * split],
        sum_first[:, 2 * split : 3 * split],
        sum_first[:, 3 * split :].T,
        sum_up,
        sum_down.T,
        bias_qv,
        bias_h,
        vec,
    )


def per_device(
    inputs,
    segments,
    w_query,
    w_key,
    w_value,
    b_query,
    b_value,
    w_output,
    b_output,
    gain_attn,
    shift_attn,
    w_hidden,
    b_hidden,
    w_project,
    b_project,
    gain_ffn,
    shift_ffn,
    cotangent,
):

    if (inputs.shape[1] // lax.axis_size("dp")) % 16:
        return per_device_small(
            inputs, segments, w_query, w_key, w_value, b_query, b_value, w_output, b_output, gain_attn, shift_attn,
            w_hidden, b_hidden, w_project, b_project, gain_ffn, shift_ffn, cotangent,
        )
    seq_len = segments.shape[1]
    share_tokens = cotangent.shape[0]
    share_rows = share_tokens // seq_len
    width = inputs.shape[1]
    groups, parts = lax.axis_size("tensor"), lax.axis_size("dp")
    place, part = lax.axis_index("tensor"), lax.axis_index("dp")
    low, wide = jnp.bfloat16, jnp.float32
    split = w_query.shape[1]
    nothing = jnp.zeros((split,), low)
    small = jnp.concatenate([b_query, nothing, b_value, nothing, b_hidden]).reshape(2, width)
    small = jnp.pad(small, ((0, 14), (0, 0)))
    nothing = jnp.zeros((width,), low)
    rows = [b_output, gain_attn, shift_attn, gain_ffn, shift_ffn, b_project, nothing, nothing]
    rows = jnp.concatenate(rows).reshape(8, width).astype(wide)
    rows_segments = lax.dynamic_slice_in_dim(segments, place * share_rows, share_rows, 0)
    first = jnp.concatenate([w_query, w_key, w_value, w_output.T], axis=1)
    saved, weights, sums = forward(
        [first, w_hidden, w_project], inputs, cotangent, small, rows, rows_segments, groups, parts
    )
    output = saved[0]
    grad_input, sum_first, sum_up, sum_down, vectors = backward(
        saved, weights, sums, inputs, rows, rows_segments, groups, parts
    )
    bias_qv = jnp.stack([vectors[:groups, :split], vectors[:groups, 2 * split : 3 * split]])
    bias_qv = bias_qv.reshape(2, groups, split // HD, HD)
    bias_h = vectors[groups : 2 * groups].reshape(groups, -1, HD)
    vec = vectors[2 * groups : 2 * groups + 6]
    piece = HD // parts
    bias_qv = lax.dynamic_slice_in_dim(bias_qv, place, 1, 1)[:, 0]
    bias_qv = lax.dynamic_slice_in_dim(bias_qv, part * piece, piece, 2)
    bias_h = lax.dynamic_slice_in_dim(bias_h, place, 1, 0)[0]
    bias_h = lax.dynamic_slice_in_dim(bias_h, part * piece, piece, 1)
    piece = width // (parts * groups)
    vec = lax.dynamic_slice_in_dim(vec, (part * groups + place) * piece, piece, 1)
    return (
        output.astype(low),
        grad_input,
        sum_first[:, :split],
        sum_first[:, split : 2 * split],
        sum_first[:, 2 * split : 3 * split],
        sum_first[:, 3 * split :].T,
        sum_up,
        sum_down.T,
        bias_qv,
        bias_h,
        vec,
    )


def solution(mesh):
    in_specs = (
        P("dp", None),
        P("dp", None),
        P(None, "tensor"),
        P(None, "tensor"),
        P(None, "tensor"),
        P("tensor"),
        P("tensor"),
        P("tensor", None),
        P(),
        P(),
        P(),
        P(None, "tensor"),
        P("tensor"),
        P("tensor", None),
        P(),
        P(),
        P(),
        P(("dp", "tensor"), None),
    )
    out_specs = (
        P(("dp", "tensor"), None),
        P(("dp", "tensor"), None),
        P("dp", "tensor"),
        P("dp", "tensor"),
        P("dp", "tensor"),
        P("tensor", "dp"),
        P("dp", "tensor"),
        P("tensor", "dp"),
        P(None, "tensor", "dp"),
        P("tensor", "dp"),
        P(None, ("dp", "tensor")),
    )
    return jax.shard_map(
        per_device, mesh=mesh, in_specs=in_specs, out_specs=out_specs, check_vma=False
    )
```

```python
import functools
import jax
import jax.numpy as jnp
from jax import lax
from jax.experimental import pallas as pl
from jax.experimental.pallas import tpu as pltpu
from jax.sharding import PartitionSpec as P

HD = 64
MESH = pl.DeviceIdType.MESH
LOW = jnp.bfloat16


class Place:
    def __init__(self, groups, parts):
        self.groups, self.parts = groups, parts
        self.t, self.d = lax.axis_index("tensor"), lax.axis_index("dp")
        self.count = parts.bit_length() - 1
        self.bits = [(self.d // (1 << i)) % 2 for i in range(self.count)]

    def partner(self, bit):
        return (self.d + (1 - 2 * self.bits[bit]) * (1 << bit), self.t)

    def along(self, step):
        return (self.d, (self.t + step) % self.groups)

    def enter(self):
        barrier = pltpu.get_barrier_semaphore()
        peers = [self.partner(b) for b in range(self.count)]
        peers += [self.along(j) for j in range(1, self.groups)]
        for peer in peers:
            pl.semaphore_signal(barrier, inc=1, device_id=peer, device_id_type=MESH)
        pl.semaphore_wait(barrier, len(peers))

    def pieces(self, open_bits, flipped=None):
        index = []
        for bit in reversed(range(self.count)):
            own = self.bits[bit]
            index.append(slice(None) if bit in open_bits else 1 - own if bit == flipped else own)
        return tuple(index)


def send(src, dst, sems, slot, peer):
    return pltpu.make_async_remote_copy(
        src_ref=src,
        dst_ref=dst,
        send_sem=sems[0].at[slot],
        recv_sem=sems[1].at[slot],
        device_id=peer,
        device_id_type=MESH,
    )


def orders(count):
    rest = list(range(1, count))
    return [rest, rest[::-1]]


def gather_kernel(groups, parts, arrays, *refs):
    shards, small = refs[:arrays], refs[arrays]
    outs, small_out = refs[arrays + 1 : 2 * arrays + 1], refs[2 * arrays + 1]
    held, small_held = refs[2 * arrays + 2 : 3 * arrays + 2], refs[3 * arrays + 2]
    load_sem, store_sem, z_send, z_recv, x_send, x_recv, s_send, s_recv = refs[3 * arrays + 3 :]
    me = Place(groups, parts)
    n = me.count
    half = shards[0].shape[-1] // 2
    bits_order = orders(n)
    me.enter()
    own = [me.t] + list(me.pieces(()))
    hops, doubles, tiny = {}, {}, []
    for j in range(1, groups):
        tiny.append(send(small, small_held.at[j - 1], (s_send, s_recv), j - 1, me.along(j)))
        tiny[-1].start()
    for a in range(arrays):
        for j in range(1, groups):
            u = a * (groups - 1) + j - 1
            hops[u] = send(
                shards[a].at[tuple(me.pieces(()))], held[a].at[tuple(own)], (z_send, z_recv), u, me.along(j)
            )
            hops[u].start()
    loads = []
    for a in range(arrays):
        loads.append(pltpu.make_async_copy(shards[a], held[a].at[me.t], load_sem.at[a]))
        loads[-1].start()

    units = arrays * (groups - 1)
    stores = []

    def advance(u, stage):
        a, j = divmod(u, groups - 1)
        source = (me.t + groups - 1 - j) % groups
        if stage == 0:
            hops[u].wait_recv()
        else:
            for h in range(2):
                if stage < n or h == 0:
                    doubles[u, stage - 1, h].wait_recv()
        if stage == n:
            out = pltpu.make_async_copy(held[a].at[source], outs[a].at[source], store_sem.at[u])
            out.start()
            stores.append(out)
            return
        for h in range(2):
            if stage == n - 1:
                if h == 1:
                    continue
                bit, done, cols = 0, set(range(1, n)), slice(None)
            else:
                bit, done = bits_order[h][stage], set(bits_order[h][:stage])
                cols = pl.ds(h * half, half)
            view = (source,) + me.pieces(done) + (slice(None), cols)
            slot = (u * n + stage) * 2 + h
            copy = send(held[a].at[view], held[a].at[view], (x_send, x_recv), slot, me.partner(bit))
            copy.start()
            doubles[u, stage, h] = copy

    for tick in range(units + n):
        for stage in range(n + 1):
            u = tick - stage
            if 0 <= u < units:
                advance(u, stage)
    for a in range(arrays):
        loads[a].wait()
        out = pltpu.make_async_copy(held[a].at[me.t], outs[a].at[me.t], store_sem.at[units + a])
        out.start()
        stores.append(out)
    small_out[me.t] = small[...]
    for j in range(1, groups):
        tiny[j - 1].wait()
        small_out[(me.t + groups - j) % groups] = small_held[j - 1]
    for copy in hops.values():
        copy.wait_send()
    for copy in doubles.values():
        copy.wait_send()
    for copy in stores:
        copy.wait()


def gather(shards, small, groups, parts):
    arrays, n = len(shards), parts.bit_length() - 1
    rows, cols = shards[0].shape[0] // parts, shards[0].shape[1]
    shape = (2,) * n + (rows, cols)
    units = arrays * (groups - 1)
    any_space = pl.BlockSpec(memory_space=pl.ANY)
    vmem = pl.BlockSpec(memory_space=pltpu.VMEM)
    *outs, small = pl.pallas_call(
        functools.partial(gather_kernel, groups, parts, arrays),
        out_shape=[jax.ShapeDtypeStruct((groups,) + shape, LOW)] * arrays
        + [jax.ShapeDtypeStruct((groups,) + small.shape, LOW)],
        in_specs=[any_space] * arrays + [vmem],
        out_specs=[any_space] * arrays + [vmem],
        scratch_shapes=[pltpu.VMEM((groups,) + shape, LOW)] * arrays
        + [
            pltpu.VMEM((groups - 1,) + small.shape, LOW),
            pltpu.SemaphoreType.DMA((arrays,)),
            pltpu.SemaphoreType.DMA((units + arrays,)),
            pltpu.SemaphoreType.DMA((units,)),
            pltpu.SemaphoreType.DMA((units,)),
            pltpu.SemaphoreType.DMA((units * n * 2,)),
            pltpu.SemaphoreType.DMA((units * n * 2,)),
            pltpu.SemaphoreType.DMA((groups - 1,)),
            pltpu.SemaphoreType.DMA((groups - 1,)),
        ],
        compiler_params=pltpu.CompilerParams(
            collective_id=0, has_side_effects=True, vmem_limit_bytes=60 << 20
        ),
        name="gather_weights",
    )(*[s.reshape(shape) for s in shards], small)
    return [o.reshape(groups, parts * rows, cols) for o in outs], small


def add_into(dst, src, lead):
    def one(i, carry):
        index = []
        for size in reversed(lead):
            index.append(i % size)
            i = i // size
        index = tuple(reversed(index))
        total = dst[index].astype(jnp.float32) + src[index].astype(jnp.float32)
        dst[index] = total.astype(LOW)
        return carry

    total = 1
    for size in lead:
        total *= size
    lax.fori_loop(0, total, one, 0)


def scatter_kernel(groups, parts, arrays, *refs):
    parted, vec = refs[:arrays], refs[arrays]
    outs, vec_out = refs[arrays + 1 : 2 * arrays + 1], refs[2 * arrays + 1]
    p = 2 * arrays + 2
    held = refs[p : p + arrays]
    n = parts.bit_length() - 1
    p += arrays
    landing = refs[p]
    halves = refs[p + 1 : p + n]
    final = refs[p + n]
    load_sem, x_send, x_recv, z_send, z_recv, vec_sum, vec_land, v_send, v_recv = refs[p + n + 1 :]
    me = Place(groups, parts)
    half = parted[0].shape[-1] // 2
    bits_order = orders(n)
    units = arrays * groups
    loads = []
    turn = [(u // groups, (me.t + 1 + u % groups) % groups) for u in range(units)]
    for u in range(units):
        a, target = turn[u]
        copy = pltpu.make_async_copy(parted[a].at[target], held[a].at[target], load_sem.at[u])
        copy.start()
        loads.append(copy)
    me.enter()
    copies, hops, tiny = {}, {}, {}

    def advance_vectors(stage):
        source = vec if stage == 0 else vec_sum.at[stage - 1]
        if stage:
            tiny[stage - 1].wait_recv()
            before = vec[...] if stage == 1 else vec_sum[stage - 2]
            vec_sum[stage - 1] = before + vec_land[stage - 1]
        peers = [me.partner(stage)] if stage < n else [me.along(j) for j in range(1, groups)]
        for k, peer in enumerate(peers):
            copy = send(source, vec_land.at[stage + k], (v_send, v_recv), stage + k, peer)
            copy.start()
            tiny[stage + k] = copy

    def advance(u, stage):
        a, target = turn[u]
        if stage == 0:
            loads[u].wait()
            copy = send(
                held[a].at[(target,) + me.pieces(set(range(1, n)), 0)],
                landing.at[u],
                (x_send, x_recv),
                u * 2 * n,
                me.partner(0),
            )
            copy.start()
            copies[u, 0, 0] = copy
            return
        for h in range(2):
            if stage == 1:
                if h == 1:
                    continue
                left, cols, source = set(range(1, n)), slice(None), landing.at[u]
            else:
                bits = bits_order[h]
                left, cols = set(bits[stage - 1 :]), pl.ds(h * half, half)
                source = halves[stage - 2].at[u, h]
            copies[u, stage - 1, h].wait_recv()
            view = (target,) + me.pieces(left) + (slice(None), cols)
            add_into(held[a].at[view], source, [2] * len(left))
        if stage == n:
            if u % groups < groups - 1:
                j = u % groups + 1
                slot = a * (groups - 1) + j - 1
                hops[slot] = send(
                    held[a].at[(target,) + me.pieces(())], final.at[slot], (z_send, z_recv), slot, me.along(j)
                )
                hops[slot].start()
            return
        for h in range(2):
            bits = bits_order[h]
            bit, left = bits[stage - 1], set(bits[stage:])
            view = (target,) + me.pieces(left, bit) + (slice(None), pl.ds(h * half, half))
            copy = send(
                held[a].at[view],
                halves[stage - 1].at[u, h],
                (x_send, x_recv),
                u * 2 * n + stage * 2 + h,
                me.partner(bit),
            )
            copy.start()
            copies[u, stage, h] = copy

    for tick in range(units + n):
        if tick <= n:
            advance_vectors(tick)
        for stage in reversed(range(n + 1)):
            u = tick - stage
            if 0 <= u < units:
                advance(u, stage)
    total = vec_sum[n - 1]
    for j in range(groups - 1):
        tiny[n + j].wait_recv()
        total = total + vec_land[n + j]
    vec_out[...] = total
    for a in range(arrays):
        total = held[a][(me.t,) + me.pieces(())].astype(jnp.float32)
        for j in range(groups - 1):
            slot = a * (groups - 1) + j
            hops[slot].wait_recv()
            total = total + final[slot].astype(jnp.float32)
        outs[a][...] = total
    for copy in tiny.values():
        copy.wait_send()
    for copy in copies.values():
        copy.wait_send()
    for copy in hops.values():
        copy.wait_send()


def scatter(parted, vec, groups, parts):
    arrays, n = len(parted), parts.bit_length() - 1
    rows, cols = parted[0].shape[1] // parts, parted[0].shape[2]
    shape = (groups,) + (2,) * n + (rows, cols)
    units = arrays * groups
    vmem = pl.BlockSpec(memory_space=pltpu.VMEM)
    return pl.pallas_call(
        functools.partial(scatter_kernel, groups, parts, arrays),
        out_shape=[jax.ShapeDtypeStruct((rows, cols), jnp.float32)] * arrays
        + [jax.ShapeDtypeStruct(vec.shape, jnp.float32)],
        in_specs=[pl.BlockSpec(memory_space=pl.ANY)] * arrays + [vmem],
        out_specs=[vmem] * (arrays + 1),
        scratch_shapes=[pltpu.VMEM(shape, LOW)] * arrays
        + [pltpu.VMEM((units,) + (2,) * (n - 1) + (rows, cols), LOW)]
        + [pltpu.VMEM((units, 2) + (2,) * (n - 1 - s) + (rows, cols // 2), LOW) for s in range(1, n)]
        + [
            pltpu.VMEM((arrays * (groups - 1), rows, cols), LOW),
            pltpu.SemaphoreType.DMA((units,)),
            pltpu.SemaphoreType.DMA((units * 2 * n,)),
            pltpu.SemaphoreType.DMA((units * 2 * n,)),
            pltpu.SemaphoreType.DMA((arrays * (groups - 1),)),
            pltpu.SemaphoreType.DMA((arrays * (groups - 1),)),
            pltpu.VMEM((n,) + vec.shape, jnp.float32),
            pltpu.VMEM((n + groups - 1,) + vec.shape, jnp.float32),
            pltpu.SemaphoreType.DMA((n + groups - 1,)),
            pltpu.SemaphoreType.DMA((n + groups - 1,)),
        ],
        compiler_params=pltpu.CompilerParams(
            collective_id=1, has_side_effects=True, vmem_limit_bytes=60 << 20
        ),
        name="scatter_gradients",
    )(*[g.reshape(shape) for g in parted], vec)


norm_epsilon = 1e-12
root_half = 0.7071067811865476


def norm_forward(values, norm_gain, norm_shift):
    average = jnp.mean(values, axis=-1, keepdims=True)
    centered = values - average
    variance = jnp.mean(centered * centered, axis=-1, keepdims=True)
    inverse = lax.rsqrt(variance + norm_epsilon)
    scaled = centered * inverse
    return (scaled * norm_gain + norm_shift, scaled, inverse)


def norm_backward(grad_out, scaled, inverse, norm_gain):
    weighted = grad_out * norm_gain
    mean_grad = jnp.mean(weighted, axis=-1, keepdims=True)
    mean_proj = jnp.mean(weighted * scaled, axis=-1, keepdims=True)
    return inverse * (weighted - mean_grad - scaled * mean_proj)


def gelu_exact(values):
    return 0.5 * values * (1.0 + lax.erf(values * root_half))


def cross_rows(left, right):
    return lax.dot_general(
        left, right, (((0,), (0,)), ((), ())), preferred_element_type=jnp.float32
    )


def times_transposed(left, right):
    return lax.dot_general(
        left, right, (((1,), (1,)), ((), ())), preferred_element_type=jnp.float32
    )


def masked_scores(queries, keys_in, segment_row):
    same_text = segment_row[:, None] == segment_row[None, :]
    scores = jnp.einsum("qhd,khd->hqk", queries, keys_in, preferred_element_type=jnp.float32)
    scores = scores * queries.shape[2] ** (-0.5)
    return jnp.where(same_text[None], scores, -1000000000.0)


def attend_forward(packed):
    queries, keys_in, values, segment_row = packed
    scores = masked_scores(queries, keys_in, segment_row)
    row_max = jnp.max(scores, axis=-1, keepdims=True)
    exponent = jnp.exp(scores - row_max)
    row_total = jnp.sum(exponent, axis=-1, keepdims=True)
    attn_probs = (exponent / row_total).astype(jnp.bfloat16)
    mixed_heads = jnp.einsum("hqk,khd->qhd", attn_probs, values, preferred_element_type=jnp.float32)
    return (mixed_heads.astype(jnp.bfloat16), row_max + jnp.log(row_total))


def attend_backward(packed):
    queries, keys_in, values, segment_row, logsum, grad_mixed = packed
    score_scale = queries.shape[2] ** (-0.5)
    scores = masked_scores(queries, keys_in, segment_row)
    attn_probs = jnp.exp(scores - logsum)
    grad_probs = jnp.einsum("qhd,khd->hqk", grad_mixed, values, preferred_element_type=jnp.float32)
    grad_values = jnp.einsum(
        "hqk,qhd->khd",
        attn_probs.astype(jnp.bfloat16),
        grad_mixed,
        preferred_element_type=jnp.float32,
    )
    inner_sum = jnp.sum(attn_probs * grad_probs, axis=-1, keepdims=True)
    grad_scores = (attn_probs * (grad_probs - inner_sum)).astype(jnp.bfloat16)
    grad_queries = (
        jnp.einsum("hqk,khd->qhd", grad_scores, keys_in, preferred_element_type=jnp.float32)
        * score_scale
    )
    grad_keys = (
        jnp.einsum("hqk,qhd->khd", grad_scores, queries, preferred_element_type=jnp.float32)
        * score_scale
    )
    return (
        grad_queries.astype(jnp.bfloat16),
        grad_keys.astype(jnp.bfloat16),
        grad_values.astype(jnp.bfloat16),
    )


def matmul_t(left, right):
    return lax.dot_general(left, right, (((1,), (1,)), ((), ())), preferred_element_type=jnp.float32)


TILE = 256
HOP = (10.0, 6.0, 5.0)
PASS = (8.0, 7.0)
SCORE = 1.4426950408889634


def row_tiles(count, size, body, hook=None):
    def step(i, carry):
        body(pl.ds(pl.multiple_of(i * size, size), size))
        if hook:
            hook(i)
        return carry

    lax.fori_loop(0, count // size, step, 0)


class Plan:
    def __init__(self):
        self.now, self.tasks, self.at = 0.0, [], {}

    def add(self, when, task):
        self.tasks.append((when, task))
        self.tasks.sort(key=lambda pair: pair[0])

    def point(self, name, spent, until=None):
        self.now += spent
        if until is not None:
            whens = [when for when, task in self.tasks if task == until]
            if whens:
                self.now = max(self.now, whens[0])
        self.at[name] = [task for when, task in self.tasks if when <= self.now]
        self.tasks = [pair for pair in self.tasks if pair[0] > self.now]


def at_point(plan, run, count, index, name, extra=None):
    for k in range(count):
        tasks = plan.at.get((name, k), [])
        if tasks:
            condition = index == k
            if extra is not None:
                condition = jnp.logical_and(condition, extra)

            @pl.when(condition)
            def _():
                for task in tasks:
                    run(*task)


def key_window(block, blocks, span):
    return max(0, block - 1) * span, min(blocks, block + 2) * span


def fold(values):
    return jnp.sum(values.reshape(-1, 8, values.shape[-1]), axis=0)


def make_mask(mask, segments, start):
    def step(r, carry):
        row = segments[pl.ds(start + r, 1), :].astype(jnp.float32)
        col = jnp.broadcast_to(row, (8, row.shape[1])).T[:, :1]
        mask[r] = jnp.where(col == row, 0.0, -1.0e9)
        return carry

    lax.fori_loop(0, mask.shape[0], step, 0)


def forward_kernel(groups, parts, *refs):
    (first, w_hidden, w_project, inputs, cot_in, segments) = refs[:6]
    biases, vectors = refs[6:9], refs[9:15]
    (out, dz_out, h_out, qkv_out, mixed_out, g_out, gp_out, lse_out, w0_out, w1_out, w2_out, sums) = refs[15:27]
    (held0, held1, held2, small_all, tok, mask, hacc, facc, yb, qkv, mixed, act, slope, lse, cot, small, rows) = refs[27:44]
    (load_sem, store_sem, z_send, z_recv, x_send, x_recv, s_send, s_recv) = refs[44:]
    me = Place(groups, parts)
    n = me.count
    wide, width = jnp.float32, tok.shape[1]
    count, seq = tok.shape[0], mask.shape[1]
    split = mixed.shape[2]
    heads = split // HD
    shards, held, weights = (first, w_hidden, w_project), (held0, held1, held2), (w0_out, w1_out, w2_out)
    half = width // 2
    bits_order = orders(n)
    loads, stores = [], []

    def load(src, dst):
        loads.append(pltpu.make_async_copy(src, dst, load_sem.at[len(loads)]))
        loads[-1].start()

    def store(src, dst, slot):
        return pltpu.make_async_copy(src, dst, store_sem.at[slot])

    load(first, held0.at[me.t])
    load(inputs.at[pl.ds(me.t * count, count)], tok)
    load(w_hidden, held1.at[me.t])
    load(w_project, held2.at[me.t])
    load(cot_in, cot)

    def line(ref):
        return ref[...].astype(wide).reshape(1, -1)

    gap = jnp.zeros((1, split), wide)
    lines = [jnp.concatenate([line(biases[0]), gap, line(biases[1]), gap], axis=1), line(biases[2])]
    lines.append(jnp.zeros((small.shape[0] - 2, width), wide))
    small[...] = jnp.concatenate(lines, axis=0).astype(LOW)
    for k, ref in enumerate(vectors):
        rows[k : k + 1, :] = line(ref)
    for k in (1, 2):
        sums[2 + k : 3 + k, :] = rows[k : k + 1, :]
    me.enter()
    mine = me.pieces(())
    turn = [(0, j) for j in range(1, groups)]
    turn += [(a, j) for j in range(1, groups) for a in (1, 2)]
    units = len(turn)
    hops, doubles, tiny = {}, {}, []
    for j in range(1, groups):
        tiny.append(send(small, small_all.at[me.t], (s_send, s_recv), j - 1, me.along(j)))
        tiny[-1].start()
    for u, (a, j) in enumerate(turn):
        hops[u] = send(shards[a].at[mine], held[a].at[(me.t,) + mine], (z_send, z_recv), u, me.along(j))
        hops[u].start()
    for u, (a, j) in enumerate(turn):
        source = (me.t + groups - j) % groups
        stores.append(store(held[a].at[source], weights[a].at[source], u))
        for stage in range(n):
            for h in range(2 if stage < n - 1 else 1):
                if stage == n - 1:
                    bit, done, cols = 0, set(range(1, n)), slice(None)
                else:
                    bit, done = bits_order[h][stage], set(bits_order[h][:stage])
                    cols = pl.ds(h * half, half)
                view = (source,) + me.pieces(done) + (slice(None), cols)
                slot = (u * n + stage) * 2 + h
                doubles[u, stage, h] = send(
                    held[a].at[view], held[a].at[view], (x_send, x_recv), slot, me.partner(bit)
                )

    def advance(u, stage):
        for h in range(2):
            if stage == 0:
                if h == 0:
                    hops[u].wait_recv()
            elif (u, stage - 1, h) in doubles:
                doubles[u, stage - 1, h].wait_recv()
        if stage == n:
            stores[u].start()
        for h in range(2):
            if (u, stage, h) in doubles:
                doubles[u, stage, h].start()

    plan = Plan()
    for u in range(units):
        for stage in range(n + 1):
            plan.add(HOP[0] + HOP[1] * u + HOP[2] * stage, (u, stage))
    for j in range(groups):
        plan.point(("start", j), 0.0, (turn.index((0, j)), n) if j else None)
        plan.point(("project", j), 1.8)
        plan.point(("attend", j), 1.7)
        plan.point(("combine", j), 1.7)
        plan.point(("combined", j), 1.0)
    plan.point(("norm", 0), 1.5)
    for j in range(groups):
        plan.point(("up", j), 0.0, (turn.index((1, j)), n) if j else None)
        plan.point(("upped", j), 1.8)
        plan.point(("down", j), 1.8, (turn.index((2, j)), n) if j else None)
        plan.point(("downed", j), 1.3)
        plan.point(("next", j), 1.3)

    def run(index, name, extra=None):
        at_point(plan, advance, groups, index, name, extra)

    def group(j):
        return (me.t + groups - j) % groups

    def weight(a, g):
        return held[a][g].reshape(width, width)

    def project(g):
        bias = small_all[g, 0:1, : 3 * split].astype(wide)

        def body(r):
            total = matmul_t(tok[r, :], weight(0, g)[: 3 * split])
            qkv[g, r, :] = (total + bias).astype(LOW)

        row_tiles(count, TILE, body)

    span = 128
    blocks = seq // span
    factor = SCORE * HD ** (-0.5)

    def attend(g, hook):
        def packed_row(p, carry):
            base = p * seq

            def at(lo, hi):
                return pl.ds(pl.multiple_of(base + lo, span), hi - lo)

            turned = qkv[g, at(0, seq), 2 * split :].T
            for b in range(blocks):
                lo, hi = key_window(b, blocks, span)
                here = (b * span, (b + 1) * span)
                bias = mask[p, lo:hi, here[0] : here[1]]
                scores, sums_e, mixes = [], [], []
                for h in range(heads):
                    q = qkv[g, at(*here), h * HD : (h + 1) * HD]
                    k = qkv[g, at(lo, hi), split + h * HD : split + (h + 1) * HD]
                    scores.append(matmul_t(k, q))
                for h in range(heads):
                    s = scores[h] * factor + bias
                    top = jnp.max(s, axis=0, keepdims=True)
                    e = jnp.exp2(s - top)
                    total = jnp.sum(e, axis=0, keepdims=True)
                    lse[g, p * blocks + b, h : h + 1, :] = top + jnp.log(total) * SCORE
                    sums_e.append((e.astype(LOW), total))
                for h in range(heads):
                    e, total = sums_e[h]
                    o = jnp.dot(turned[h * HD : (h + 1) * HD, lo:hi], e, preferred_element_type=wide)
                    mixes.append(o * (1.0 / total))
                mixed[g, at(*here), :] = jnp.concatenate(mixes, axis=0).T.astype(LOW)
            hook(p)
            return carry

        lax.fori_loop(0, count // seq, packed_row, 0)

    def combine(g):
        def body(r):
            hacc[r, :] = hacc[r, :] + jnp.dot(
                mixed[g, r, :], weight(0, g)[3 * split :], preferred_element_type=wide
            )

        row_tiles(count, TILE, body)

    def start_sum():
        def body(r):
            hacc[r, :] = tok[r, :].astype(wide) + rows[0:1]

        row_tiles(count, TILE, body)

    def first_norm():
        def body(r):
            y, _, _ = norm_forward(hacc[r, :], rows[1:2], rows[2:3])
            yb[r, :] = y.astype(LOW)
            facc[r, :] = y + rows[5:6]

        row_tiles(count, 64, body)

    def ffn_up(g, hook):
        bias = small_all[g, 1:2, :].astype(wide)

        def body(r):
            u = jnp.dot(yb[r, :], weight(1, g), preferred_element_type=wide) + bias
            below = 0.5 + 0.5 * lax.erf(u * root_half)
            act[g, r, :] = (u * below).astype(LOW)
            bell = jnp.exp2(u * u * (-0.5 * SCORE)) * 0.3989422804014327
            slope[g, r, :] = (below + u * bell).astype(LOW)

        row_tiles(count, TILE, body, hook)

    def ffn_down(g, hook):
        def body(r):
            facc[r, :] = facc[r, :] + jnp.dot(act[g, r, :], weight(2, g), preferred_element_type=wide)

        row_tiles(count, TILE, body, hook)

    def last_norm():
        def step(i, carry):
            r = pl.ds(pl.multiple_of(i * 64, 64), 64)
            y, scaled, inverse = norm_forward(facc[r, :], rows[3:4], rows[4:5])
            tok[r, :] = y.astype(LOW)
            grad = cot[r, :].astype(wide)
            dz = norm_backward(grad, scaled, inverse, rows[3:4])
            facc[r, :] = dz
            return (
                carry[0] + fold(grad * scaled),
                carry[1] + fold(grad),
                carry[2] + fold(dz.astype(LOW).astype(wide)),
            )

        zero = jnp.zeros((8, width), wide)
        found = lax.fori_loop(0, count // 64, step, (zero, zero, zero))
        for i in range(3):
            sums[i : i + 1, :] = jnp.sum(found[i], axis=0, keepdims=True)

    small_all[me.t] = small[...]
    make_mask(mask, segments, me.t * mask.shape[0])
    loads[0].wait()
    loads[1].wait()
    half_way = count // TILE // 2 - 1
    start_sum()

    def attend_stores(g, j):
        return [
            store(a.at[g], b.at[g], units + groups * i + j)
            for i, (a, b) in enumerate(((qkv, qkv_out), (mixed, mixed_out), (lse, lse_out)))
        ]

    def ffn_stores(g, j):
        return [
            store(a.at[g], b.at[g], units + groups * (3 + i) + j)
            for i, (a, b) in enumerate(((act, g_out), (slope, gp_out)))
        ]

    def attend_group(j, carry):
        @pl.when(j == 1)
        def _():
            for t in tiny:
                t.wait()

        g = group(j)
        run(j, "start")
        project(g)
        run(j, "project")
        attend(g, lambda p: run(j, "attend", p == 0))
        run(j, "combine")
        combine(g)
        for copy in attend_stores(g, j):
            copy.start()
        run(j, "combined")
        return carry

    def ffn_group(j, carry):
        g = group(j)
        run(j, "up")
        ffn_up(g, lambda i: run(j, "upped", i == half_way))
        run(j, "down")
        ffn_down(g, lambda i: run(j, "downed", i == half_way))
        for copy in ffn_stores(g, j):
            copy.start()
        run(j, "next")
        return carry

    lax.fori_loop(0, groups, attend_group, 0)
    for i in range(2, 5):
        loads[i].wait()
    first_norm()
    base = units + 5 * groups
    others = [store(hacc, h_out, base)]
    others[0].start()
    for task in plan.at["norm", 0]:
        advance(*task)
    lax.fori_loop(0, groups, ffn_group, 0)
    for _, task in plan.tasks:
        advance(*task)
    last_norm()
    others += [store(tok, out, base + 1), store(facc, dz_out, base + 2)]
    for a in range(3):
        others.append(store(held[a].at[me.t], weights[a].at[me.t], base + 3 + a))
    for copy in others[1:]:
        copy.start()
    stores += others
    for j in range(groups):
        stores += attend_stores(group(j), j) + ffn_stores(group(j), j)
    for copy in hops.values():
        copy.wait_send()
    for copy in doubles.values():
        copy.wait_send()
    for copy in stores:
        copy.wait()


def forward(shards, inputs, cotangent, biases, vectors, segments, groups, parts):
    n = parts.bit_length() - 1
    width, count = inputs.shape[1], cotangent.shape[0]
    split = width // groups
    shape = (2,) * n + (width // parts, width)
    seq = segments.shape[1]
    packed = count // seq
    units = 3 * (groups - 1)
    anywhere, vmem = pl.BlockSpec(memory_space=pl.ANY), pl.BlockSpec(memory_space=pltpu.VMEM)
    wide = jnp.float32

    def made(*dims):
        return lambda kind, dtype: kind(dims, dtype)

    tokens, grouped = made(count, width), made(groups, count, width)
    layout = [
        (tokens, LOW),
        (tokens, wide),
        (tokens, wide),
        (made(groups, count, 3 * split), LOW),
        (made(groups, count, split), LOW),
        (grouped, LOW),
        (grouped, LOW),
        (made(groups, packed * seq // 128, 8, 128), wide),
    ] + [(made(groups, *shape), LOW)] * 3 + [(made(8, width), wide)]
    dma = pltpu.SemaphoreType.DMA
    outs = pl.pallas_call(
        functools.partial(forward_kernel, groups, parts),
        out_shape=[f(jax.ShapeDtypeStruct, dtype) for f, dtype in layout],
        in_specs=[anywhere] * 5 + [vmem] * 10,
        out_specs=[anywhere] * (len(layout) - 1) + [vmem],
        scratch_shapes=[pltpu.VMEM((groups,) + shape, LOW)] * 3
        + [
            pltpu.VMEM((groups, 16, width), LOW),
            pltpu.VMEM((count, width), LOW),
            pltpu.VMEM((packed, seq, seq), wide),
            pltpu.VMEM((count, width), wide),
            pltpu.VMEM((count, width), wide),
            pltpu.VMEM((count, width), LOW),
            pltpu.VMEM((groups, count, 3 * split), LOW),
            pltpu.VMEM((groups, count, split), LOW),
            pltpu.VMEM((groups, count, width), LOW),
            pltpu.VMEM((groups, count, width), LOW),
            pltpu.VMEM((groups, packed * seq // 128, 8, 128), wide),
            pltpu.VMEM((count, width), LOW),
            pltpu.VMEM((16, width), LOW),
            pltpu.VMEM((8, width), wide),
            dma((5,)),
            dma((units + 5 * groups + 6,)),
            dma((units,)),
            dma((units,)),
            dma((units * n * 2,)),
            dma((units * n * 2,)),
            dma((groups - 1,)),
            dma((groups - 1,)),
        ],
        compiler_params=pltpu.CompilerParams(
            collective_id=2, has_side_effects=True, vmem_limit_bytes=63 << 20
        ),
        name="gather_and_forward",
    )(
        *[s.reshape(shape) for s in shards],
        inputs,
        cotangent,
        segments,
        *biases,
        *vectors,
    )
    weights = [w.reshape(groups, width, width) for w in outs[8:11]]
    return outs[:8], weights, outs[11]


def backward_kernel(groups, parts, *refs):
    (dz_in, h_in, qkv_in, mixed_in, act_in, slope_in, lse_in, w0_in, w1_in, w2_in, inputs) = refs[:11]
    segments, sums = refs[11:13]
    gi_out, out0, out1, out2, vec_out = refs[13:18]
    (held0, held1, held2, landing, final) = refs[18:23]
    (w_buf, d_buf, act, slope, grad, low, low_t, row_t, du, hid, mask, qkv, mixed, lse, dmix, dqkv) = refs[23:39]
    (vec, vec_sum, vec_land) = refs[39:42]
    (load_sem, x_send, x_recv, z_send, z_recv, v_send, v_recv) = refs[42:49]
    halves = refs[49:]
    me = Place(groups, parts)
    n = me.count
    wide, width = jnp.float32, du.shape[1]
    count, seq = du.shape[0], mask.shape[1]
    split = mixed.shape[2]
    heads = split // HD
    held = (held0, held1, held2)
    half = width // 2
    bits_order = orders(n)
    turn = [(a, i) for i in range(groups) for a in (2, 1)] + [(0, i) for i in range(groups)]
    slots = list(range(2 * groups)) + [2 * groups + 1 + 2 * i for i in range(groups)]
    units = len(turn)

    def load(slot, src, dst):
        return pltpu.make_async_copy(src, dst, load_sem.at[slot])

    def group(i):
        return (me.t + 1 + i) % groups

    def load_ffn(i):
        g, s = group(i), i % 2
        pairs = ((slope_in, slope), (w2_in, d_buf), (w1_in, w_buf), (act_in, act))
        return [load(4 + 4 * i + k, a.at[g], b.at[s]) for k, (a, b) in enumerate(pairs)]

    def load_heads(i):
        g, s = group(i), i % 2
        pairs = ((w0_in, w_buf.at[(groups + i) % 2]), (qkv_in, qkv.at[s]), (mixed_in, mixed.at[s]), (lse_in, lse.at[s]))
        return [load(4 + 4 * groups + 4 * i + k, a.at[g], b) for k, (a, b) in enumerate(pairs)]

    def start(copies):
        for copy in copies:
            copy.start()

    def finish_all(copies):
        for copy in copies:
            copy.wait()

    entry = [load(0, dz_in, grad), load(1, h_in, hid)]
    start(entry)
    start(load_ffn(0))
    me.enter()
    copies, hops, tiny = {}, {}, {}

    def advance_vectors(stage):
        source = vec if stage == 0 else vec_sum.at[stage - 1]
        if stage:
            tiny[stage - 1].wait_recv()
            before = vec[...] if stage == 1 else vec_sum[stage - 2]
            vec_sum[stage - 1] = before + vec_land[stage - 1]
        peers = [me.partner(stage)] if stage < n else [me.along(j) for j in range(1, groups)]
        for k, peer in enumerate(peers):
            copy = send(source, vec_land.at[stage + k], (v_send, v_recv), stage + k, peer)
            copy.start()
            tiny[stage + k] = copy

    for u, (a, i) in enumerate(turn):
        target = group(i)
        copies[u, 0, 0] = send(
            held[a].at[(target,) + me.pieces(set(range(1, n)), 0)],
            landing.at[u],
            (x_send, x_recv),
            u * 2 * n,
            me.partner(0),
        )
        for stage in range(1, n):
            for h in range(2):
                bits = bits_order[h]
                bit, left = bits[stage - 1], set(bits[stage:])
                copies[u, stage, h] = send(
                    held[a].at[(target,) + me.pieces(left, bit) + (slice(None), pl.ds(h * half, half))],
                    halves[stage - 1].at[u, h],
                    (x_send, x_recv),
                    u * 2 * n + stage * 2 + h,
                    me.partner(bit),
                )
        if i < groups - 1:
            slot = a * (groups - 1) + i
            hops[slot] = send(
                held[a].at[(target,) + me.pieces(())], final.at[slot], (z_send, z_recv), slot, me.along(i + 1)
            )

    def advance(u, stage):
        a, i = turn[u]
        target = group(i)
        for h in range(2):
            if (u, stage - 1, h) not in copies:
                continue
            if stage == 1:
                left, cols, source = set(range(1, n)), slice(None), landing.at[u]
            else:
                left, cols = set(bits_order[h][stage - 1 :]), pl.ds(h * half, half)
                source = halves[stage - 2].at[u, h]
            copies[u, stage - 1, h].wait_recv()
            view = (target,) + me.pieces(left) + (slice(None), cols)
            add_into(held[a].at[view], source, [2] * len(left))
        if stage == n and i < groups - 1:
            hops[a * (groups - 1) + i].start()
        for h in range(2):
            if (u, stage, h) in copies:
                copies[u, stage, h].start()

    plan = Plan()
    before = [-100.0] * (n + 1)

    def made(u):
        for stage in range(n + 1):
            when = plan.now + PASS[0] * stage
            if stage:
                when = max(when, before[stage] + PASS[1], before[stage - 1] + PASS[0])
            before[stage] = when
            plan.add(when, (u, stage))

    for i in range(groups):
        plan.now += 2.8
        made(2 * i)
        plan.point(("down", i), 0.0)
        plan.point(("back", i), 2.8)
        plan.point(("backed", i), 2.8)
        plan.now += 2.8
        made(2 * i + 1)
        plan.point(("up", i), 0.0)
    plan.point(("norm", 0), 3.0)
    plan.point(("norm", 1), 2.0)
    for i in range(groups):
        plan.point(("mix", i), 1.0)
        plan.point(("attend", i), 3.0)
        plan.point(("attended", i), 3.0)
        plan.now += 2.8
        made(2 * groups + i)
        plan.point(("first", i), 0.0)
        plan.point(("finish", i), 2.2)

    def run(index, name, extra=None):
        at_point(plan, advance, groups, index, name, extra)

    def put(a, g, cols, value):
        shape = held[a].shape[1:-1] + value.shape[1:]
        held[a][(g,) + (slice(None),) * (n + 1) + (cols,)] = value.astype(LOW).reshape(shape)

    def products(a, g, left, right):
        def step(i, carry):
            cols = pl.ds(pl.multiple_of(i * TILE, TILE), TILE)
            put(a, g, cols, jnp.dot(left[...], right[:, cols], preferred_element_type=wide))
            return carry

        lax.fori_loop(0, width // TILE, step, 0)

    def flip(dst, r, value):
        dst[:, r] = value.T

    vec[...] = jnp.zeros_like(vec)
    finish_all(entry)

    def prepare(i, carry):
        r = pl.ds(pl.multiple_of(i * 128, 128), 128)
        g = grad[r, :].astype(LOW)
        low[r, :] = g
        flip(low_t, r, g)
        y, _, _ = norm_forward(hid[r, :], sums[3:4], sums[4:5])
        flip(row_t, r, y.astype(LOW))
        return carry

    lax.fori_loop(0, count // 128, prepare, 0)
    make_mask(mask, segments, me.t * mask.shape[0])

    half_way = count // TILE // 2 - 1

    def ffn_group(i, outer):
        g, s = group(i), i % 2

        @pl.when(i + 1 < groups)
        def _():
            start(load_ffn(i + 1))

        @pl.when(i + 1 == groups)
        def _():
            start(load_heads(0))

        finish_all(load_ffn(i))
        products(2, g, low_t, act.at[s])
        run(i, "down")

        def back(k, carry):
            r = pl.ds(pl.multiple_of(k * TILE, TILE), TILE)
            part = matmul_t(low[r, :], d_buf[s])
            part = (part * slope[s, r, :].astype(wide)).astype(LOW)
            du[r, :] = part
            grad[r, :] = grad[r, :] + matmul_t(part, w_buf[s])
            run(i, "back", k == half_way)
            return carry + fold(part.astype(wide))

        total = lax.fori_loop(0, count // TILE, back, jnp.zeros((8, width), wide))
        vec[pl.ds(groups + g, 1), :] = jnp.sum(total, axis=0, keepdims=True)
        run(i, "backed")
        products(1, g, row_t, du)
        run(i, "up")
        return outer

    lax.fori_loop(0, groups, ffn_group, 0)
    tokens = load(2, inputs.at[pl.ds(me.t * count, count)], du)
    tokens.start()

    def norm(i, carry):
        r = pl.ds(pl.multiple_of(i * 64, 64), 64)
        _, scaled, inverse = norm_forward(hid[r, :], sums[3:4], sums[4:5])
        dy = grad[r, :]
        dh = norm_backward(dy, scaled, inverse, sums[3:4])
        dh_low = dh.astype(LOW)
        grad[r, :] = dh
        low[r, :] = dh_low
        return (carry[0] + fold(dy * scaled), carry[1] + fold(dy), carry[2] + fold(dh_low.astype(wide)))

    zero = jnp.zeros((8, width), wide)
    found = lax.fori_loop(0, count // 64, norm, (zero, zero, zero))
    for k in range(3):
        vec[2 * groups + k : 2 * groups + k + 1, :] = jnp.sum(found[k], axis=0, keepdims=True)
    vec[2 * groups + 3 : 2 * groups + 6, :] = sums[0:3, :]
    for task in plan.at["norm", 0]:
        advance(*task)
    tokens.wait()

    def turn_over(i, carry):
        r = pl.ds(pl.multiple_of(i * 128, 128), 128)
        flip(low_t, r, low[r, :])
        flip(row_t, r, du[r, :])
        return carry

    lax.fori_loop(0, count // 128, turn_over, 0)
    for task in plan.at["norm", 1]:
        advance(*task)

    span = 128
    blocks = seq // span
    scale = HD ** (-0.5)

    def heads_group(i, outer):
        g, s, ws = group(i), i % 2, (groups + i) % 2

        @pl.when(i + 1 < groups)
        def _():
            start(load_heads(i + 1))

        finish_all(load_heads(i))

        def mix(k, carry):
            r = pl.ds(pl.multiple_of(k * TILE, TILE), TILE)
            dmix[r, :] = matmul_t(low[r, :], w_buf[ws, 3 * split :, :]).astype(LOW)
            return carry

        lax.fori_loop(0, count // TILE, mix, 0)
        run(i, "mix")

        def packed_row(p, carry):
            base = p * seq

            def at(lo, hi):
                return pl.ds(pl.multiple_of(base + lo, span), hi - lo)

            turned = qkv[s, at(0, seq), split : 2 * split].T
            dks = [[None] * heads for _ in range(blocks)]
            dvs = [[None] * heads for _ in range(blocks)]
            dqs = []

            def gather_sum(total, lo, h, value):
                for c in range(value.shape[0] // span):
                    piece = value[c * span : (c + 1) * span]
                    old = total[lo // span + c][h]
                    total[lo // span + c][h] = piece if old is None else old + piece

            def write(b):
                parts_b = [dqs[b]] + [x * scale for x in dks[b]] + dvs[b]
                dqkv[at(b * span, (b + 1) * span), :] = jnp.concatenate(parts_b, axis=1).astype(LOW)

            for b in range(blocks):
                lo, hi = key_window(b, blocks, span)
                here = (b * span, (b + 1) * span)
                bias = mask[p, lo:hi, here[0] : here[1]]
                work, grads = [], []
                for h in range(heads):
                    q = qkv[s, at(*here), h * HD : (h + 1) * HD]
                    k = qkv[s, at(lo, hi), split + h * HD : split + (h + 1) * HD]
                    v = qkv[s, at(lo, hi), 2 * split + h * HD : 2 * split + (h + 1) * HD]
                    do = dmix[at(*here), h * HD : (h + 1) * HD]
                    work.append((q, do, matmul_t(k, q), matmul_t(v, do)))
                for h in range(heads):
                    q, do, score, dp = work[h]
                    prob = jnp.exp2(score * (SCORE * scale) + bias - lse[s, p * blocks + b, h : h + 1, :])
                    inner = jnp.sum(prob * dp, axis=0, keepdims=True)
                    grads.append((prob.astype(LOW), (prob * (dp - inner)).astype(LOW)))
                dq = []
                for h in range(heads):
                    q, do, _, _ = work[h]
                    prob, ds = grads[h]
                    gather_sum(dvs, lo, h, jnp.dot(prob, do, preferred_element_type=wide))
                    gather_sum(dks, lo, h, jnp.dot(ds, q, preferred_element_type=wide))
                    dq.append(jnp.dot(turned[h * HD : (h + 1) * HD, lo:hi], ds, preferred_element_type=wide))
                dqs.append(jnp.concatenate(dq, axis=0).T * scale)
                if b:
                    write(b - 1)
            write(blocks - 1)
            run(i, "attend", p == 0)
            return carry

        lax.fori_loop(0, count // seq, packed_row, 0)
        run(i, "attended")

        def first_cols(k, carry):
            cols = pl.ds(pl.multiple_of(k * TILE, TILE), TILE)
            put(0, g, cols, jnp.dot(row_t[...], dqkv[:, cols], preferred_element_type=wide))
            return carry

        edge = 3 * split // TILE * TILE
        lax.fori_loop(0, edge // TILE, first_cols, 0)
        tail = jnp.concatenate(
            [
                jnp.dot(row_t[...], dqkv[:, edge:], preferred_element_type=wide),
                jnp.dot(low_t[...], mixed[s], preferred_element_type=wide),
            ],
            axis=1,
        )
        put(0, g, slice(edge, width), tail)
        run(i, "first")

        def finish(k, carry):
            r = pl.ds(pl.multiple_of(k * TILE, TILE), TILE)
            part = dqkv[r, :]
            grad[r, :] = grad[r, :] + jnp.dot(part, w_buf[ws, : 3 * split, :], preferred_element_type=wide)
            return carry + fold(part.astype(wide))

        total = lax.fori_loop(0, count // TILE, finish, jnp.zeros((8, 3 * split), wide))
        vec[pl.ds(g, 1), : 3 * split] = jnp.sum(total, axis=0, keepdims=True)
        run(i, "finish")
        return outer

    lax.fori_loop(0, groups, heads_group, 0)
    result = load(3, grad, gi_out)
    result.start()
    rest = [task for _, task in plan.tasks]
    for stage in range(n + 1):
        advance_vectors(stage)
        for task in rest[:2] if stage < n else rest:
            advance(*task)
        rest = rest[2:]
    total = vec_sum[n - 1]
    for j in range(groups - 1):
        tiny[n + j].wait_recv()
        total = total + vec_land[n + j]
    vec_out[...] = total
    for a, out in ((2, out2), (1, out1), (0, out0)):
        total = held[a][(me.t,) + me.pieces(())].astype(wide)
        for j in range(groups - 1):
            slot = a * (groups - 1) + j
            hops[slot].wait_recv()
            total = total + final[slot].astype(wide)
        out[...] = total
    for copy in list(tiny.values()) + list(copies.values()) + list(hops.values()):
        copy.wait_send()
    result.wait()


def backward(saved, weights, sums, inputs, segments, groups, parts):
    n = parts.bit_length() - 1
    _, dz, hid, qkv, mixed, act, slope, lse = saved
    count, width = dz.shape
    split = width // groups
    piece = width // parts
    shape = (groups,) + (2,) * n + (piece, width)
    seq = segments.shape[1]
    packed = count // seq
    units = 3 * groups
    anywhere, vmem = pl.BlockSpec(memory_space=pl.ANY), pl.BlockSpec(memory_space=pltpu.VMEM)
    wide, dma = jnp.float32, pltpu.SemaphoreType.DMA
    lines = -(-(2 * groups + 6) // 8) * 8
    return pl.pallas_call(
        functools.partial(backward_kernel, groups, parts),
        out_shape=[jax.ShapeDtypeStruct((count, width), wide)]
        + [jax.ShapeDtypeStruct((piece, width), wide)] * 3
        + [jax.ShapeDtypeStruct((lines, width), wide)],
        in_specs=[anywhere] * 11 + [vmem] * 2,
        out_specs=[anywhere] + [vmem] * 4,
        scratch_shapes=[pltpu.VMEM(shape, LOW)] * 3
        + [
            pltpu.VMEM((units,) + (2,) * (n - 1) + (piece, width), LOW),
            pltpu.VMEM((3 * (groups - 1), piece, width), LOW),
            pltpu.VMEM((2, width, width), LOW),
            pltpu.VMEM((2, width, width), LOW),
            pltpu.VMEM((2, count, width), LOW),
            pltpu.VMEM((2, count, width), LOW),
            pltpu.VMEM((count, width), wide),
            pltpu.VMEM((count, width), LOW),
            pltpu.VMEM((width, count), LOW),
            pltpu.VMEM((width, count), LOW),
            pltpu.VMEM((count, width), LOW),
            pltpu.VMEM((count, width), wide),
            pltpu.VMEM((packed, seq, seq), wide),
            pltpu.VMEM((2, count, 3 * split), LOW),
            pltpu.VMEM((2, count, split), LOW),
            pltpu.VMEM((2, count // 128, 8, 128), wide),
            pltpu.VMEM((count, split), LOW),
            pltpu.VMEM((count, 3 * split), LOW),
            pltpu.VMEM((lines, width), wide),
            pltpu.VMEM((n, lines, width), wide),
            pltpu.VMEM((n + groups - 1, lines, width), wide),
            dma((8 * groups + 4,)),
            dma((units * 2 * n,)),
            dma((units * 2 * n,)),
            dma((3 * (groups - 1),)),
            dma((3 * (groups - 1),)),
            dma((n + groups - 1,)),
            dma((n + groups - 1,)),
        ]
        + [pltpu.VMEM((units, 2) + (2,) * (n - 1 - s) + (piece, width // 2), LOW) for s in range(1, n)],
        compiler_params=pltpu.CompilerParams(
            collective_id=3, has_side_effects=True, vmem_limit_bytes=67043328
        ),
        name="backward_and_scatter",
    )(dz, hid, qkv, mixed, act, slope, lse, *weights, inputs, segments, sums)


def pick(values, size, index):
    total = jnp.zeros((values.shape[0], size), values.dtype)
    for k in range(values.shape[1] // size):
        total = jnp.where(index == k, values[:, k * size : (k + 1) * size], total)
    return total


def outputs_kernel(groups, parts, *refs):
    out_in, gi_in, first, up, down, vec = refs[:6]
    out, gi, g_query, g_key, g_value, g_output, g_hidden, g_project, bias_qv, bias_h, vectors = refs[6:17]
    held_out, held_gi, load_sem, store_sem = refs[17:]
    t, d = lax.axis_index("tensor"), lax.axis_index("dp")
    count, width = held_gi.shape
    split, piece = width // groups, HD // parts
    size = count // 4
    loads, stores = [], []
    for k in range(4):
        r = pl.ds(k * size, size)
        for a, b, c in ((gi_in, held_gi, gi), (out_in, held_out, out)):
            loads.append(pltpu.make_async_copy(a.at[r], b.at[r], load_sem.at[len(loads)]))
            stores.append(pltpu.make_async_copy(b.at[r], c.at[r], store_sem.at[len(stores)]))
            loads[-1].start()
    for k, target in enumerate((g_query, g_key, g_value)):
        target[...] = first[:, k * split : (k + 1) * split]
    g_output[...] = first[:, 3 * split :].T
    g_hidden[...] = up[...]
    g_project[...] = down[...]
    for a, b in zip(loads, stores):
        a.wait()
        b.start()
    own, hidden = vec[pl.ds(t, 1), :], vec[pl.ds(groups + t, 1), :]
    heads = split // HD
    pieces = [own[:, k * HD : (k + 1) * HD] for k in range(heads)]
    pieces += [own[:, 2 * split + k * HD : 2 * split + (k + 1) * HD] for k in range(heads)]
    pieces += [hidden[:, k * HD : (k + 1) * HD] for k in range(width // HD)]
    found = pick(jnp.concatenate(pieces, axis=0), piece, d)
    for h in range(heads):
        bias_qv[h] = jnp.concatenate([found[h : h + 1], found[heads + h : heads + h + 1]], axis=0)
    bias_h[...] = found[2 * heads :].T
    vectors[...] = pick(vec[2 * groups : 2 * groups + 6, :], width // (parts * groups), d * groups + t)
    for b in stores:
        b.wait()


def finish_outputs(output, grad_input, first, up, down, vec, groups, parts):
    (count, width), (piece, _) = grad_input.shape, first.shape
    split, wide = width // groups, jnp.float32
    shapes = [(count, width)] + [(piece, split)] * 3 + [(split, piece), (piece, width), (piece, width)]
    shapes += [(split // HD, 2, HD // parts), (HD // parts, width // HD), (6, width // (parts * groups))]
    anywhere, vmem = pl.BlockSpec(memory_space=pl.ANY), pl.BlockSpec(memory_space=pltpu.VMEM)
    return pl.pallas_call(
        functools.partial(outputs_kernel, groups, parts),
        out_shape=[jax.ShapeDtypeStruct((count, width), LOW)] + [jax.ShapeDtypeStruct(s, wide) for s in shapes],
        in_specs=[anywhere] * 2 + [vmem] * 4,
        out_specs=[anywhere] * 2 + [vmem] * 9,
        scratch_shapes=[
            pltpu.VMEM((count, width), LOW),
            pltpu.VMEM((count, width), wide),
            pltpu.SemaphoreType.DMA((8,)),
            pltpu.SemaphoreType.DMA((8,)),
        ],
        name="outputs",
    )(output, grad_input, first, up, down, vec)


def per_device_small(
    inputs,
    segments,
    w_query,
    w_key,
    w_value,
    b_query,
    b_value,
    w_output,
    b_output,
    gain_attn,
    shift_attn,
    w_hidden,
    b_hidden,
    w_project,
    b_project,
    gain_ffn,
    shift_ffn,
    cotangent,
):
    seq_len = segments.shape[1]
    share_tokens = cotangent.shape[0]
    share_rows = share_tokens // seq_len
    width = inputs.shape[1]
    groups, parts = lax.axis_size("tensor"), lax.axis_size("dp")
    place, part = lax.axis_index("tensor"), lax.axis_index("dp")
    low = jnp.bfloat16
    wide = jnp.float32

    tokens = lax.dynamic_slice_in_dim(inputs, place * share_tokens, share_tokens, 0)
    rows_segments = lax.dynamic_slice_in_dim(segments, place * share_rows, share_rows, 0)
    split = w_query.shape[1]
    small = jnp.concatenate([b_query, b_value, b_hidden]).reshape(-1, 128)
    small_rows = small.shape[0]
    small = jnp.pad(small, ((0, -small_rows % 16), (0, 0)))
    first = jnp.concatenate([w_query, w_key, w_value, w_output.T], axis=1)
    (first, w_up, w_down), small = gather([first, w_hidden, w_project], small, groups, parts)
    w_in = first[:, :, : 3 * split].reshape(groups, width, 3, split).transpose(1, 2, 0, 3)
    w_in = w_in.reshape(width, 3 * groups * split)
    w_out = first[:, :, 3 * split :].transpose(0, 2, 1).reshape(groups * split, width)
    w_up = w_up.transpose(1, 0, 2).reshape(width, -1)
    w_down = w_down.reshape(-1, width)
    small = small[:, :small_rows].reshape(groups, -1).astype(wide)
    bias_query = small[:, :split].reshape(-1)
    bias_value = small[:, split : 2 * split].reshape(-1)
    bias_hidden = small[:, 2 * split :].reshape(-1)
    full = groups * split
    head_shape = (share_rows, seq_len, full // HD, HD)

    attn_gain = gain_attn.astype(wide)
    attn_shift = shift_attn.astype(wide)
    attn_bias = b_output.astype(wide)
    ffn_gain = gain_ffn.astype(wide)
    ffn_shift = shift_ffn.astype(wide)
    ffn_bias = b_project.astype(wide)
    grad_out = cotangent.astype(wide)

    projected = jnp.dot(tokens, w_in, preferred_element_type=wide)
    queries = (projected[:, :full] + bias_query).astype(low)
    keys_in = projected[:, full : 2 * full].astype(low)
    values = (projected[:, 2 * full :] + bias_value).astype(low)
    query_heads = queries.reshape(head_shape)
    key_heads = keys_in.reshape(head_shape)
    value_heads = values.reshape(head_shape)
    mixed_heads, logsum = lax.map(attend_forward, (query_heads, key_heads, value_heads, rows_segments))
    mixed = mixed_heads.reshape(share_tokens, full)
    hidden = tokens.astype(wide) + (jnp.dot(mixed, w_out, preferred_element_type=wide) + attn_bias)
    normed, scaled, inverse = norm_forward(hidden, attn_gain, attn_shift)
    normed_low = normed.astype(low)
    hidden_pre = jnp.dot(normed_low, w_up, preferred_element_type=wide) + bias_hidden
    active, gelu_pull = jax.vjp(gelu_exact, hidden_pre)
    active_low = active.astype(low)
    block_sum = normed + (jnp.dot(active_low, w_down, preferred_element_type=wide) + ffn_bias)
    output, scaled_out, inverse_out = norm_forward(block_sum, ffn_gain, ffn_shift)
    grad_sum = norm_backward(grad_out, scaled_out, inverse_out, ffn_gain)
    grad_ffn_gain = jnp.sum(grad_out * scaled_out, axis=0)
    grad_ffn_shift = jnp.sum(grad_out, axis=0)
    grad_sum_low = grad_sum.astype(low)
    grad_ffn_bias = jnp.sum(grad_sum_low.astype(wide), axis=0)
    grad_active = times_transposed(grad_sum_low, w_down)
    grad_w_down = cross_rows(grad_sum_low, active_low)
    grad_hidden_pre = gelu_pull(grad_active)[0].astype(low)
    grad_b_hidden = jnp.sum(grad_hidden_pre.astype(wide), axis=0)
    grad_w_up = cross_rows(normed_low, grad_hidden_pre)
    grad_normed = grad_sum + times_transposed(grad_hidden_pre, w_up)
    grad_hidden = norm_backward(grad_normed, scaled, inverse, attn_gain)
    grad_hidden_low = grad_hidden.astype(low)
    grad_attn_gain = jnp.sum(grad_normed * scaled, axis=0)
    grad_attn_shift = jnp.sum(grad_normed, axis=0)
    grad_attn_bias = jnp.sum(grad_hidden_low.astype(wide), axis=0)
    grad_w_out = cross_rows(grad_hidden_low, mixed)
    grad_mixed = times_transposed(grad_hidden_low, w_out).astype(low).reshape(head_shape)
    grad_q, grad_k, grad_v = lax.map(
        attend_backward, (query_heads, key_heads, value_heads, rows_segments, logsum, grad_mixed)
    )
    grad_q = grad_q.reshape(share_tokens, full)
    grad_k = grad_k.reshape(share_tokens, full)
    grad_v = grad_v.reshape(share_tokens, full)
    grad_projected = jnp.concatenate([grad_q, grad_k, grad_v], axis=1)
    grad_w_in = cross_rows(tokens, grad_projected)
    grad_b_query = jnp.sum(grad_q.astype(wide), axis=0)
    grad_b_value = jnp.sum(grad_v.astype(wide), axis=0)
    grad_input = grad_hidden + times_transposed(grad_projected, w_in)

    def parted(grad):
        return grad.astype(low).reshape(width, groups, -1).transpose(1, 0, 2)

    first = jnp.concatenate(
        [parted(grad_w_in[:, i * full : (i + 1) * full]) for i in range(3)] + [parted(grad_w_out)], axis=2
    )
    vectors = jnp.concatenate(
        [
            jnp.stack([grad_b_query, grad_b_value]).reshape(2 * groups, split),
            grad_b_hidden.reshape(-1, split),
            jnp.stack(
                [
                    grad_attn_gain,
                    grad_attn_shift,
                    grad_attn_bias,
                    grad_ffn_gain,
                    grad_ffn_shift,
                    grad_ffn_bias,
                ]
            ).reshape(-1, split),
        ],
        axis=0,
    )
    count = vectors.size // split
    vectors = vectors.reshape(-1, 128)
    (sum_first, sum_up, sum_down, vectors) = scatter(
        [first, parted(grad_w_up), parted(grad_w_down)], vectors, groups, parts
    )
    vectors = vectors.reshape(count, split)
    bias_qv = vectors[: 2 * groups].reshape(2, groups, split // HD, HD)
    rest = vectors[2 * groups :]
    hid = bias_hidden.shape[0] // split
    bias_h = rest[:hid].reshape(groups, -1, HD)
    vec = rest[hid:].reshape(6, -1)
    piece = HD // parts
    bias_qv = lax.dynamic_slice_in_dim(bias_qv, place, 1, 1)[:, 0]
    bias_qv = lax.dynamic_slice_in_dim(bias_qv, part * piece, piece, 2)
    bias_h = lax.dynamic_slice_in_dim(bias_h, place, 1, 0)[0]
    bias_h = lax.dynamic_slice_in_dim(bias_h, part * piece, piece, 1)
    piece = width // (parts * groups)
    vec = lax.dynamic_slice_in_dim(vec, (part * groups + place) * piece, piece, 1)
    return (
        output.astype(low),
        grad_input,
        sum_first[:, :split],
        sum_first[:, split : 2 * split],
        sum_first[:, 2 * split : 3 * split],
        sum_first[:, 3 * split :].T,
        sum_up,
        sum_down.T,
        bias_qv,
        bias_h,
        vec,
    )


def per_device(
    inputs,
    segments,
    w_query,
    w_key,
    w_value,
    b_query,
    b_value,
    w_output,
    b_output,
    gain_attn,
    shift_attn,
    w_hidden,
    b_hidden,
    w_project,
    b_project,
    gain_ffn,
    shift_ffn,
    cotangent,
):
    if (inputs.shape[1] // lax.axis_size("dp")) % 16:
        return per_device_small(
            inputs, segments, w_query, w_key, w_value, b_query, b_value, w_output, b_output, gain_attn, shift_attn,
            w_hidden, b_hidden, w_project, b_project, gain_ffn, shift_ffn, cotangent,
        )
    width, split = w_query.shape
    groups, parts = lax.axis_size("tensor"), lax.axis_size("dp")
    biases = [b_query, b_value, b_hidden]
    shared = [b_output, gain_attn, shift_attn, gain_ffn, shift_ffn, b_project]
    first = jnp.concatenate([w_query.T, w_key.T, w_value.T, w_output], axis=0)
    saved, weights, sums = forward(
        [first, w_hidden, w_project], inputs, cotangent, biases, shared, segments, groups, parts
    )
    grad_input, sum_first, sum_up, sum_down, vectors = backward(
        saved, weights, sums, inputs, segments, groups, parts
    )
    found = finish_outputs(saved[0], grad_input, sum_first, sum_up, sum_down, vectors, groups, parts)
    return (*found[:7], found[7].T, found[8].transpose(1, 0, 2), found[9].T, found[10])


def solution(mesh):
    in_specs = (
        P("dp", None),
        P("dp", None),
        P(None, "tensor"),
        P(None, "tensor"),
        P(None, "tensor"),
        P("tensor"),
        P("tensor"),
        P("tensor", None),
        P(),
        P(),
        P(),
        P(None, "tensor"),
        P("tensor"),
        P("tensor", None),
        P(),
        P(),
        P(),
        P(("dp", "tensor"), None),
    )
    out_specs = (
        P(("dp", "tensor"), None),
        P(("dp", "tensor"), None),
        P("dp", "tensor"),
        P("dp", "tensor"),
        P("dp", "tensor"),
        P("tensor", "dp"),
        P("dp", "tensor"),
        P("tensor", "dp"),
        P(None, "tensor", "dp"),
        P("tensor", "dp"),
        P(None, ("dp", "tensor")),
    )
    return jax.shard_map(
        per_device, mesh=mesh, in_specs=in_specs, out_specs=out_specs, check_vma=False
    )
```

```python
import functools
import jax
import jax.numpy as jnp
from jax import lax
from jax.experimental import pallas as pl
from jax.experimental.pallas import tpu as pltpu
from jax.sharding import PartitionSpec as P

HD = 64
MESH = pl.DeviceIdType.MESH
LOW = jnp.bfloat16


class Place:
    def __init__(self, groups, parts):
        self.groups, self.parts = groups, parts
        self.t, self.d = lax.axis_index("tensor"), lax.axis_index("dp")
        self.count = parts.bit_length() - 1
        self.bits = [(self.d // (1 << i)) % 2 for i in range(self.count)]

    def partner(self, bit):
        return (self.d + (1 - 2 * self.bits[bit]) * (1 << bit), self.t)

    def along(self, step):
        return (self.d, (self.t + step) % self.groups)

    def enter(self):
        barrier = pltpu.get_barrier_semaphore()
        peers = [self.partner(b) for b in range(self.count)]
        peers += [self.along(j) for j in range(1, self.groups)]
        for peer in peers:
            pl.semaphore_signal(barrier, inc=1, device_id=peer, device_id_type=MESH)
        pl.semaphore_wait(barrier, len(peers))

    def pieces(self, open_bits, flipped=None):
        index = []
        for bit in reversed(range(self.count)):
            own = self.bits[bit]
            index.append(slice(None) if bit in open_bits else 1 - own if bit == flipped else own)
        return tuple(index)


def send(src, dst, sems, slot, peer):
    return pltpu.make_async_remote_copy(
        src_ref=src,
        dst_ref=dst,
        send_sem=sems[0].at[slot],
        recv_sem=sems[1].at[slot],
        device_id=peer,
        device_id_type=MESH,
    )


def orders(count):
    rest = list(range(1, count))
    return [rest, rest[::-1]]


def gather_kernel(groups, parts, arrays, *refs):
    shards, small = refs[:arrays], refs[arrays]
    outs, small_out = refs[arrays + 1 : 2 * arrays + 1], refs[2 * arrays + 1]
    held, small_held = refs[2 * arrays + 2 : 3 * arrays + 2], refs[3 * arrays + 2]
    load_sem, store_sem, z_send, z_recv, x_send, x_recv, s_send, s_recv = refs[3 * arrays + 3 :]
    me = Place(groups, parts)
    n = me.count
    half = shards[0].shape[-1] // 2
    bits_order = orders(n)
    me.enter()
    own = [me.t] + list(me.pieces(()))
    hops, doubles, tiny = {}, {}, []
    for j in range(1, groups):
        tiny.append(send(small, small_held.at[j - 1], (s_send, s_recv), j - 1, me.along(j)))
        tiny[-1].start()
    for a in range(arrays):
        for j in range(1, groups):
            u = a * (groups - 1) + j - 1
            hops[u] = send(
                shards[a].at[tuple(me.pieces(()))], held[a].at[tuple(own)], (z_send, z_recv), u, me.along(j)
            )
            hops[u].start()
    loads = []
    for a in range(arrays):
        loads.append(pltpu.make_async_copy(shards[a], held[a].at[me.t], load_sem.at[a]))
        loads[-1].start()

    units = arrays * (groups - 1)
    stores = []

    def advance(u, stage):
        a, j = divmod(u, groups - 1)
        source = (me.t + groups - 1 - j) % groups
        if stage == 0:
            hops[u].wait_recv()
        else:
            for h in range(2):
                if stage < n or h == 0:
                    doubles[u, stage - 1, h].wait_recv()
        if stage == n:
            out = pltpu.make_async_copy(held[a].at[source], outs[a].at[source], store_sem.at[u])
            out.start()
            stores.append(out)
            return
        for h in range(2):
            if stage == n - 1:
                if h == 1:
                    continue
                bit, done, cols = 0, set(range(1, n)), slice(None)
            else:
                bit, done = bits_order[h][stage], set(bits_order[h][:stage])
                cols = pl.ds(h * half, half)
            view = (source,) + me.pieces(done) + (slice(None), cols)
            slot = (u * n + stage) * 2 + h
            copy = send(held[a].at[view], held[a].at[view], (x_send, x_recv), slot, me.partner(bit))
            copy.start()
            doubles[u, stage, h] = copy

    for tick in range(units + n):
        for stage in range(n + 1):
            u = tick - stage
            if 0 <= u < units:
                advance(u, stage)
    for a in range(arrays):
        loads[a].wait()
        out = pltpu.make_async_copy(held[a].at[me.t], outs[a].at[me.t], store_sem.at[units + a])
        out.start()
        stores.append(out)
    small_out[me.t] = small[...]
    for j in range(1, groups):
        tiny[j - 1].wait()
        small_out[(me.t + groups - j) % groups] = small_held[j - 1]
    for copy in hops.values():
        copy.wait_send()
    for copy in doubles.values():
        copy.wait_send()
    for copy in stores:
        copy.wait()


def gather(shards, small, groups, parts):
    arrays, n = len(shards), parts.bit_length() - 1
    rows, cols = shards[0].shape[0] // parts, shards[0].shape[1]
    shape = (2,) * n + (rows, cols)
    units = arrays * (groups - 1)
    any_space = pl.BlockSpec(memory_space=pl.ANY)
    vmem = pl.BlockSpec(memory_space=pltpu.VMEM)
    *outs, small = pl.pallas_call(
        functools.partial(gather_kernel, groups, parts, arrays),
        out_shape=[jax.ShapeDtypeStruct((groups,) + shape, LOW)] * arrays
        + [jax.ShapeDtypeStruct((groups,) + small.shape, LOW)],
        in_specs=[any_space] * arrays + [vmem],
        out_specs=[any_space] * arrays + [vmem],
        scratch_shapes=[pltpu.VMEM((groups,) + shape, LOW)] * arrays
        + [
            pltpu.VMEM((groups - 1,) + small.shape, LOW),
            pltpu.SemaphoreType.DMA((arrays,)),
            pltpu.SemaphoreType.DMA((units + arrays,)),
            pltpu.SemaphoreType.DMA((units,)),
            pltpu.SemaphoreType.DMA((units,)),
            pltpu.SemaphoreType.DMA((units * n * 2,)),
            pltpu.SemaphoreType.DMA((units * n * 2,)),
            pltpu.SemaphoreType.DMA((groups - 1,)),
            pltpu.SemaphoreType.DMA((groups - 1,)),
        ],
        compiler_params=pltpu.CompilerParams(
            collective_id=0, has_side_effects=True, vmem_limit_bytes=60 << 20
        ),
        name="gather_weights",
    )(*[s.reshape(shape) for s in shards], small)
    return [o.reshape(groups, parts * rows, cols) for o in outs], small


def add_into(dst, src, lead):
    def one(i, carry):
        index = []
        for size in reversed(lead):
            index.append(i % size)
            i = i // size
        index = tuple(reversed(index))
        total = dst[index].astype(jnp.float32) + src[index].astype(jnp.float32)
        dst[index] = total.astype(LOW)
        return carry

    total = 1
    for size in lead:
        total *= size
    lax.fori_loop(0, total, one, 0)


def scatter_kernel(groups, parts, arrays, *refs):
    parted, vec = refs[:arrays], refs[arrays]
    outs, vec_out = refs[arrays + 1 : 2 * arrays + 1], refs[2 * arrays + 1]
    p = 2 * arrays + 2
    held = refs[p : p + arrays]
    n = parts.bit_length() - 1
    p += arrays
    landing = refs[p]
    halves = refs[p + 1 : p + n]
    final = refs[p + n]
    load_sem, x_send, x_recv, z_send, z_recv, vec_sum, vec_land, v_send, v_recv = refs[p + n + 1 :]
    me = Place(groups, parts)
    half = parted[0].shape[-1] // 2
    bits_order = orders(n)
    units = arrays * groups
    loads = []
    turn = [(u // groups, (me.t + 1 + u % groups) % groups) for u in range(units)]
    for u in range(units):
        a, target = turn[u]
        copy = pltpu.make_async_copy(parted[a].at[target], held[a].at[target], load_sem.at[u])
        copy.start()
        loads.append(copy)
    me.enter()
    copies, hops, tiny = {}, {}, {}

    def advance_vectors(stage):
        source = vec if stage == 0 else vec_sum.at[stage - 1]
        if stage:
            tiny[stage - 1].wait_recv()
            before = vec[...] if stage == 1 else vec_sum[stage - 2]
            vec_sum[stage - 1] = before + vec_land[stage - 1]
        peers = [me.partner(stage)] if stage < n else [me.along(j) for j in range(1, groups)]
        for k, peer in enumerate(peers):
            copy = send(source, vec_land.at[stage + k], (v_send, v_recv), stage + k, peer)
            copy.start()
            tiny[stage + k] = copy

    def advance(u, stage):
        a, target = turn[u]
        if stage == 0:
            loads[u].wait()
            copy = send(
                held[a].at[(target,) + me.pieces(set(range(1, n)), 0)],
                landing.at[u],
                (x_send, x_recv),
                u * 2 * n,
                me.partner(0),
            )
            copy.start()
            copies[u, 0, 0] = copy
            return
        for h in range(2):
            if stage == 1:
                if h == 1:
                    continue
                left, cols, source = set(range(1, n)), slice(None), landing.at[u]
            else:
                bits = bits_order[h]
                left, cols = set(bits[stage - 1 :]), pl.ds(h * half, half)
                source = halves[stage - 2].at[u, h]
            copies[u, stage - 1, h].wait_recv()
            view = (target,) + me.pieces(left) + (slice(None), cols)
            add_into(held[a].at[view], source, [2] * len(left))
        if stage == n:
            if u % groups < groups - 1:
                j = u % groups + 1
                slot = a * (groups - 1) + j - 1
                hops[slot] = send(
                    held[a].at[(target,) + me.pieces(())], final.at[slot], (z_send, z_recv), slot, me.along(j)
                )
                hops[slot].start()
            return
        for h in range(2):
            bits = bits_order[h]
            bit, left = bits[stage - 1], set(bits[stage:])
            view = (target,) + me.pieces(left, bit) + (slice(None), pl.ds(h * half, half))
            copy = send(
                held[a].at[view],
                halves[stage - 1].at[u, h],
                (x_send, x_recv),
                u * 2 * n + stage * 2 + h,
                me.partner(bit),
            )
            copy.start()
            copies[u, stage, h] = copy

    for tick in range(units + n):
        if tick <= n:
            advance_vectors(tick)
        for stage in reversed(range(n + 1)):
            u = tick - stage
            if 0 <= u < units:
                advance(u, stage)
    total = vec_sum[n - 1]
    for j in range(groups - 1):
        tiny[n + j].wait_recv()
        total = total + vec_land[n + j]
    vec_out[...] = total
    for a in range(arrays):
        total = held[a][(me.t,) + me.pieces(())].astype(jnp.float32)
        for j in range(groups - 1):
            slot = a * (groups - 1) + j
            hops[slot].wait_recv()
            total = total + final[slot].astype(jnp.float32)
        outs[a][...] = total
    for copy in tiny.values():
        copy.wait_send()
    for copy in copies.values():
        copy.wait_send()
    for copy in hops.values():
        copy.wait_send()


def scatter(parted, vec, groups, parts):
    arrays, n = len(parted), parts.bit_length() - 1
    rows, cols = parted[0].shape[1] // parts, parted[0].shape[2]
    shape = (groups,) + (2,) * n + (rows, cols)
    units = arrays * groups
    vmem = pl.BlockSpec(memory_space=pltpu.VMEM)
    return pl.pallas_call(
        functools.partial(scatter_kernel, groups, parts, arrays),
        out_shape=[jax.ShapeDtypeStruct((rows, cols), jnp.float32)] * arrays
        + [jax.ShapeDtypeStruct(vec.shape, jnp.float32)],
        in_specs=[pl.BlockSpec(memory_space=pl.ANY)] * arrays + [vmem],
        out_specs=[vmem] * (arrays + 1),
        scratch_shapes=[pltpu.VMEM(shape, LOW)] * arrays
        + [pltpu.VMEM((units,) + (2,) * (n - 1) + (rows, cols), LOW)]
        + [pltpu.VMEM((units, 2) + (2,) * (n - 1 - s) + (rows, cols // 2), LOW) for s in range(1, n)]
        + [
            pltpu.VMEM((arrays * (groups - 1), rows, cols), LOW),
            pltpu.SemaphoreType.DMA((units,)),
            pltpu.SemaphoreType.DMA((units * 2 * n,)),
            pltpu.SemaphoreType.DMA((units * 2 * n,)),
            pltpu.SemaphoreType.DMA((arrays * (groups - 1),)),
            pltpu.SemaphoreType.DMA((arrays * (groups - 1),)),
            pltpu.VMEM((n,) + vec.shape, jnp.float32),
            pltpu.VMEM((n + groups - 1,) + vec.shape, jnp.float32),
            pltpu.SemaphoreType.DMA((n + groups - 1,)),
            pltpu.SemaphoreType.DMA((n + groups - 1,)),
        ],
        compiler_params=pltpu.CompilerParams(
            collective_id=1, has_side_effects=True, vmem_limit_bytes=60 << 20
        ),
        name="scatter_gradients",
    )(*[g.reshape(shape) for g in parted], vec)


norm_epsilon = 1e-12
root_half = 0.7071067811865476


def norm_forward(values, norm_gain, norm_shift):
    average = jnp.mean(values, axis=-1, keepdims=True)
    centered = values - average
    variance = jnp.mean(centered * centered, axis=-1, keepdims=True)
    inverse = lax.rsqrt(variance + norm_epsilon)
    scaled = centered * inverse
    return (scaled * norm_gain + norm_shift, scaled, inverse)


def norm_backward(grad_out, scaled, inverse, norm_gain):
    weighted = grad_out * norm_gain
    mean_grad = jnp.mean(weighted, axis=-1, keepdims=True)
    mean_proj = jnp.mean(weighted * scaled, axis=-1, keepdims=True)
    return inverse * (weighted - mean_grad - scaled * mean_proj)


def gelu_exact(values):
    return 0.5 * values * (1.0 + lax.erf(values * root_half))


def cross_rows(left, right):
    return lax.dot_general(
        left, right, (((0,), (0,)), ((), ())), preferred_element_type=jnp.float32
    )


def times_transposed(left, right):
    return lax.dot_general(
        left, right, (((1,), (1,)), ((), ())), preferred_element_type=jnp.float32
    )


def masked_scores(queries, keys_in, segment_row):
    same_text = segment_row[:, None] == segment_row[None, :]
    scores = jnp.einsum("qhd,khd->hqk", queries, keys_in, preferred_element_type=jnp.float32)
    scores = scores * queries.shape[2] ** (-0.5)
    return jnp.where(same_text[None], scores, -1000000000.0)


def attend_forward(packed):
    queries, keys_in, values, segment_row = packed
    scores = masked_scores(queries, keys_in, segment_row)
    row_max = jnp.max(scores, axis=-1, keepdims=True)
    exponent = jnp.exp(scores - row_max)
    row_total = jnp.sum(exponent, axis=-1, keepdims=True)
    attn_probs = (exponent / row_total).astype(jnp.bfloat16)
    mixed_heads = jnp.einsum("hqk,khd->qhd", attn_probs, values, preferred_element_type=jnp.float32)
    return (mixed_heads.astype(jnp.bfloat16), row_max + jnp.log(row_total))


def attend_backward(packed):
    queries, keys_in, values, segment_row, logsum, grad_mixed = packed
    score_scale = queries.shape[2] ** (-0.5)
    scores = masked_scores(queries, keys_in, segment_row)
    attn_probs = jnp.exp(scores - logsum)
    grad_probs = jnp.einsum("qhd,khd->hqk", grad_mixed, values, preferred_element_type=jnp.float32)
    grad_values = jnp.einsum(
        "hqk,qhd->khd",
        attn_probs.astype(jnp.bfloat16),
        grad_mixed,
        preferred_element_type=jnp.float32,
    )
    inner_sum = jnp.sum(attn_probs * grad_probs, axis=-1, keepdims=True)
    grad_scores = (attn_probs * (grad_probs - inner_sum)).astype(jnp.bfloat16)
    grad_queries = (
        jnp.einsum("hqk,khd->qhd", grad_scores, keys_in, preferred_element_type=jnp.float32)
        * score_scale
    )
    grad_keys = (
        jnp.einsum("hqk,qhd->khd", grad_scores, queries, preferred_element_type=jnp.float32)
        * score_scale
    )
    return (
        grad_queries.astype(jnp.bfloat16),
        grad_keys.astype(jnp.bfloat16),
        grad_values.astype(jnp.bfloat16),
    )


def matmul_t(left, right):
    return lax.dot_general(left, right, (((1,), (1,)), ((), ())), preferred_element_type=jnp.float32)


TILE = 256
HOP = (10.0, 6.0, 5.0)
PASS = (8.0, 7.0)
SCORE = 1.4426950408889634


def row_tiles(count, size, body, hook=None):
    def step(i, carry):
        body(pl.ds(pl.multiple_of(i * size, size), size))
        if hook:
            hook(i)
        return carry

    lax.fori_loop(0, count // size, step, 0)


class Plan:
    def __init__(self):
        self.now, self.tasks, self.at = 0.0, [], {}

    def add(self, when, task):
        self.tasks.append((when, task))
        self.tasks.sort(key=lambda pair: pair[0])

    def point(self, name, spent, until=None):
        self.now += spent
        if until is not None:
            whens = [when for when, task in self.tasks if task == until]
            if whens:
                self.now = max(self.now, whens[0])
        self.at[name] = [task for when, task in self.tasks if when <= self.now]
        self.tasks = [pair for pair in self.tasks if pair[0] > self.now]


def at_point(plan, run, count, index, name, extra=None):
    for k in range(count):
        tasks = plan.at.get((name, k), [])
        if tasks:
            condition = index == k
            if extra is not None:
                condition = jnp.logical_and(condition, extra)

            @pl.when(condition)
            def _():
                for task in tasks:
                    run(*task)


def key_window(block, blocks, span):
    return max(0, block - 1) * span, min(blocks, block + 2) * span


def fold(values):
    return jnp.sum(values.reshape(-1, 8, values.shape[-1]), axis=0)


def make_mask(mask, segments, start):
    def step(r, carry):
        row = segments[pl.ds(start + r, 1), :].astype(jnp.float32)
        col = jnp.broadcast_to(row, (8, row.shape[1])).T[:, :1]
        mask[r] = jnp.where(col == row, 0.0, -1.0e9)
        return carry

    lax.fori_loop(0, mask.shape[0], step, 0)


def forward_kernel(groups, parts, *refs):
    (first, w_hidden, w_project, inputs, cot_in, segments) = refs[:6]
    biases, vectors = refs[6:9], refs[9:15]
    (out, dz_out, h_out, qkv_out, mixed_out, g_out, gp_out, lse_out, w0_out, w1_out, w2_out, sums) = refs[15:27]
    (held0, held1, held2, small_all, tok, mask, hacc, facc, yb, qkv, mixed, act, slope, lse, cot, small, rows) = refs[27:44]
    (load_sem, store_sem, z_send, z_recv, x_send, x_recv, s_send, s_recv) = refs[44:]
    me = Place(groups, parts)
    n = me.count
    wide, width = jnp.float32, tok.shape[1]
    count, seq = tok.shape[0], mask.shape[1]
    split = mixed.shape[2]
    heads = split // HD
    shards, held, weights = (first, w_hidden, w_project), (held0, held1, held2), (w0_out, w1_out, w2_out)
    half = width // 2
    bits_order = orders(n)
    loads, stores = [], []

    def load(src, dst):
        loads.append(pltpu.make_async_copy(src, dst, load_sem.at[len(loads)]))
        loads[-1].start()

    def store(src, dst, slot):
        return pltpu.make_async_copy(src, dst, store_sem.at[slot])

    load(first, held0.at[me.t])
    load(inputs.at[pl.ds(me.t * count, count)], tok)
    load(w_hidden, held1.at[me.t])
    load(w_project, held2.at[me.t])
    load(cot_in, cot)

    def line(ref):
        return ref[...].astype(wide).reshape(1, -1)

    gap = jnp.zeros((1, split), wide)
    lines = [jnp.concatenate([line(biases[0]), gap, line(biases[1]), gap], axis=1), line(biases[2])]
    lines.append(jnp.zeros((small.shape[0] - 2, width), wide))
    small[...] = jnp.concatenate(lines, axis=0).astype(LOW)
    for k, ref in enumerate(vectors):
        rows[k : k + 1, :] = line(ref)
    for k in (1, 2):
        sums[2 + k : 3 + k, :] = rows[k : k + 1, :]
    me.enter()
    mine = me.pieces(())
    away = [0, 1] + list(range(groups - 1, 1, -1))
    turn = [(0, j) for j in away[1:]]
    turn += [(a, j) for j in away[1:] for a in (1, 2)]
    units = len(turn)
    hops, doubles, tiny = {}, {}, []
    for j in range(1, groups):
        tiny.append(send(small, small_all.at[me.t], (s_send, s_recv), j - 1, me.along(j)))
        tiny[-1].start()
    for u, (a, j) in enumerate(turn):
        hops[u] = send(shards[a].at[mine], held[a].at[(me.t,) + mine], (z_send, z_recv), u, me.along(j))
        hops[u].start()
    for u, (a, j) in enumerate(turn):
        source = (me.t + groups - j) % groups
        stores.append(store(held[a].at[source], weights[a].at[source], u))
        for stage in range(n):
            for h in range(2 if stage < n - 1 else 1):
                if stage == n - 1:
                    bit, done, cols = 0, set(range(1, n)), slice(None)
                else:
                    bit, done = bits_order[h][stage], set(bits_order[h][:stage])
                    cols = pl.ds(h * half, half)
                view = (source,) + me.pieces(done) + (slice(None), cols)
                slot = (u * n + stage) * 2 + h
                doubles[u, stage, h] = send(
                    held[a].at[view], held[a].at[view], (x_send, x_recv), slot, me.partner(bit)
                )

    def advance(u, stage):
        for h in range(2):
            if stage == 0:
                if h == 0:
                    hops[u].wait_recv()
            elif (u, stage - 1, h) in doubles:
                doubles[u, stage - 1, h].wait_recv()
        if stage == n:
            stores[u].start()
        for h in range(2):
            if (u, stage, h) in doubles:
                doubles[u, stage, h].start()

    plan = Plan()
    for u in range(units):
        for stage in range(n + 1):
            plan.add(HOP[0] + HOP[1] * u + HOP[2] * stage, (u, stage))
    for j in range(groups):
        plan.point(("start", j), 0.0, (turn.index((0, away[j])), n) if j else None)
        plan.point(("project", j), 1.8)
        plan.point(("attend", j), 1.7)
        plan.point(("combine", j), 1.7)
        plan.point(("combined", j), 1.0)
    plan.point(("norm", 0), 1.5)
    for j in range(groups):
        plan.point(("up", j), 0.0, (turn.index((1, away[j])), n) if j else None)
        plan.point(("upped", j), 1.8)
        plan.point(("down", j), 1.8, (turn.index((2, away[j])), n) if j else None)
        plan.point(("downed", j), 1.3)
        plan.point(("next", j), 1.3)

    def run(index, name, extra=None):
        at_point(plan, advance, groups, index, name, extra)

    def group(j):
        return (me.t + groups - jnp.where(j <= 1, j, groups + 1 - j)) % groups

    def weight(a, g):
        return held[a][g].reshape(width, width)

    def project(g):
        bias = small_all[g, 0:1, : 3 * split].astype(wide)

        def body(r):
            total = matmul_t(tok[r, :], weight(0, g)[: 3 * split])
            qkv[g, r, :] = (total + bias).astype(LOW)

        row_tiles(count, TILE, body)

    span = 128
    blocks = seq // span
    factor = SCORE * HD ** (-0.5)

    def attend(g, hook):
        def packed_row(p, carry):
            base = p * seq

            def at(lo, hi):
                return pl.ds(pl.multiple_of(base + lo, span), hi - lo)

            turned = qkv[g, at(0, seq), 2 * split :].T
            for b in range(blocks):
                lo, hi = key_window(b, blocks, span)
                here = (b * span, (b + 1) * span)
                bias = mask[p, lo:hi, here[0] : here[1]]
                scores, sums_e, mixes = [], [], []
                for h in range(heads):
                    q = qkv[g, at(*here), h * HD : (h + 1) * HD]
                    k = qkv[g, at(lo, hi), split + h * HD : split + (h + 1) * HD]
                    scores.append(matmul_t(k, q))
                for h in range(heads):
                    s = scores[h] * factor + bias
                    top = jnp.max(s, axis=0, keepdims=True)
                    e = jnp.exp2(s - top)
                    total = jnp.sum(e, axis=0, keepdims=True)
                    lse[g, p * blocks + b, h : h + 1, :] = top + jnp.log(total) * SCORE
                    sums_e.append((e.astype(LOW), total))
                for h in range(heads):
                    e, total = sums_e[h]
                    o = jnp.dot(turned[h * HD : (h + 1) * HD, lo:hi], e, preferred_element_type=wide)
                    mixes.append(o * (1.0 / total))
                mixed[g, at(*here), :] = jnp.concatenate(mixes, axis=0).T.astype(LOW)
            hook(p)
            return carry

        lax.fori_loop(0, count // seq, packed_row, 0)

    def combine(g):
        def body(r):
            hacc[r, :] = hacc[r, :] + jnp.dot(
                mixed[g, r, :], weight(0, g)[3 * split :], preferred_element_type=wide
            )

        row_tiles(count, TILE, body)

    def start_sum():
        def body(r):
            hacc[r, :] = tok[r, :].astype(wide) + rows[0:1]

        row_tiles(count, TILE, body)

    def first_norm():
        def body(r):
            y, _, _ = norm_forward(hacc[r, :], rows[1:2], rows[2:3])
            yb[r, :] = y.astype(LOW)
            facc[r, :] = y + rows[5:6]

        row_tiles(count, 64, body)

    def ffn_up(g, hook):
        bias = small_all[g, 1:2, :].astype(wide)

        def body(r):
            u = jnp.dot(yb[r, :], weight(1, g), preferred_element_type=wide) + bias
            below = 0.5 + 0.5 * lax.erf(u * root_half)
            act[g, r, :] = (u * below).astype(LOW)
            bell = jnp.exp2(u * u * (-0.5 * SCORE)) * 0.3989422804014327
            slope[g, r, :] = (below + u * bell).astype(LOW)

        row_tiles(count, TILE, body, hook)

    def ffn_down(g, hook):
        def body(r):
            facc[r, :] = facc[r, :] + jnp.dot(act[g, r, :], weight(2, g), preferred_element_type=wide)

        row_tiles(count, TILE, body, hook)

    def last_norm():
        def step(i, carry):
            r = pl.ds(pl.multiple_of(i * 64, 64), 64)
            y, scaled, inverse = norm_forward(facc[r, :], rows[3:4], rows[4:5])
            tok[r, :] = y.astype(LOW)
            grad = cot[r, :].astype(wide)
            dz = norm_backward(grad, scaled, inverse, rows[3:4])
            facc[r, :] = dz
            return (
                carry[0] + fold(grad * scaled),
                carry[1] + fold(grad),
                carry[2] + fold(dz.astype(LOW).astype(wide)),
            )

        zero = jnp.zeros((8, width), wide)
        found = lax.fori_loop(0, count // 64, step, (zero, zero, zero))
        for i in range(3):
            sums[i : i + 1, :] = jnp.sum(found[i], axis=0, keepdims=True)

    small_all[me.t] = small[...]
    make_mask(mask, segments, me.t * mask.shape[0])
    loads[0].wait()
    loads[1].wait()
    half_way = count // TILE // 2 - 1
    start_sum()

    def attend_stores(g, j):
        return [
            store(a.at[g], b.at[g], units + groups * i + j)
            for i, (a, b) in enumerate(((qkv, qkv_out), (mixed, mixed_out), (lse, lse_out)))
        ]

    def ffn_stores(g, j):
        return [
            store(a.at[g], b.at[g], units + groups * (3 + i) + j)
            for i, (a, b) in enumerate(((act, g_out), (slope, gp_out)))
        ]

    def attend_group(j, carry):
        @pl.when(j == 1)
        def _():
            for t in tiny:
                t.wait()

        g = group(j)
        run(j, "start")
        project(g)
        run(j, "project")
        attend(g, lambda p: run(j, "attend", p == 0))
        run(j, "combine")
        combine(g)
        for copy in attend_stores(g, j):
            copy.start()
        run(j, "combined")
        return carry

    def ffn_group(j, carry):
        g = group(j)
        run(j, "up")
        ffn_up(g, lambda i: run(j, "upped", i == half_way))
        run(j, "down")
        ffn_down(g, lambda i: run(j, "downed", i == half_way))
        for copy in ffn_stores(g, j):
            copy.start()
        run(j, "next")
        return carry

    lax.fori_loop(0, groups, attend_group, 0)
    for i in range(2, 5):
        loads[i].wait()
    first_norm()
    base = units + 5 * groups
    others = [store(hacc, h_out, base)]
    others[0].start()
    for task in plan.at["norm", 0]:
        advance(*task)
    lax.fori_loop(0, groups, ffn_group, 0)
    for _, task in plan.tasks:
        advance(*task)
    last_norm()
    others += [store(tok, out, base + 1), store(facc, dz_out, base + 2)]
    for a in range(3):
        others.append(store(held[a].at[me.t], weights[a].at[me.t], base + 3 + a))
    for copy in others[1:]:
        copy.start()
    stores += others
    for j in range(groups):
        stores += attend_stores(group(j), j) + ffn_stores(group(j), j)
    for copy in hops.values():
        copy.wait_send()
    for copy in doubles.values():
        copy.wait_send()
    for copy in stores:
        copy.wait()


def forward(shards, inputs, cotangent, biases, vectors, segments, groups, parts):
    n = parts.bit_length() - 1
    width, count = inputs.shape[1], cotangent.shape[0]
    split = width // groups
    shape = (2,) * n + (width // parts, width)
    seq = segments.shape[1]
    packed = count // seq
    units = 3 * (groups - 1)
    anywhere, vmem = pl.BlockSpec(memory_space=pl.ANY), pl.BlockSpec(memory_space=pltpu.VMEM)
    wide = jnp.float32

    def made(*dims):
        return lambda kind, dtype: kind(dims, dtype)

    tokens, grouped = made(count, width), made(groups, count, width)
    layout = [
        (tokens, LOW),
        (tokens, wide),
        (tokens, wide),
        (made(groups, count, 3 * split), LOW),
        (made(groups, count, split), LOW),
        (grouped, LOW),
        (grouped, LOW),
        (made(groups, packed * seq // 128, 8, 128), wide),
    ] + [(made(groups, *shape), LOW)] * 3 + [(made(8, width), wide)]
    dma = pltpu.SemaphoreType.DMA
    outs = pl.pallas_call(
        functools.partial(forward_kernel, groups, parts),
        out_shape=[f(jax.ShapeDtypeStruct, dtype) for f, dtype in layout],
        in_specs=[anywhere] * 5 + [vmem] * 10,
        out_specs=[anywhere] * (len(layout) - 1) + [vmem],
        scratch_shapes=[pltpu.VMEM((groups,) + shape, LOW)] * 3
        + [
            pltpu.VMEM((groups, 16, width), LOW),
            pltpu.VMEM((count, width), LOW),
            pltpu.VMEM((packed, seq, seq), wide),
            pltpu.VMEM((count, width), wide),
            pltpu.VMEM((count, width), wide),
            pltpu.VMEM((count, width), LOW),
            pltpu.VMEM((groups, count, 3 * split), LOW),
            pltpu.VMEM((groups, count, split), LOW),
            pltpu.VMEM((groups, count, width), LOW),
            pltpu.VMEM((groups, count, width), LOW),
            pltpu.VMEM((groups, packed * seq // 128, 8, 128), wide),
            pltpu.VMEM((count, width), LOW),
            pltpu.VMEM((16, width), LOW),
            pltpu.VMEM((8, width), wide),
            dma((5,)),
            dma((units + 5 * groups + 6,)),
            dma((units,)),
            dma((units,)),
            dma((units * n * 2,)),
            dma((units * n * 2,)),
            dma((groups - 1,)),
            dma((groups - 1,)),
        ],
        compiler_params=pltpu.CompilerParams(
            collective_id=2, has_side_effects=True, vmem_limit_bytes=63 << 20
        ),
        name="gather_and_forward",
    )(
        *[s.reshape(shape) for s in shards],
        inputs,
        cotangent,
        segments,
        *biases,
        *vectors,
    )
    weights = [w.reshape(groups, width, width) for w in outs[8:11]]
    return outs[:8], weights, outs[11]


def backward_kernel(groups, parts, *refs):
    (dz_in, h_in, qkv_in, mixed_in, act_in, slope_in, lse_in, w0_in, w1_in, w2_in, inputs) = refs[:11]
    segments, sums = refs[11:13]
    gi_out, out0, out1, out2, vec_out = refs[13:18]
    (held0, held1, held2, landing, final) = refs[18:23]
    (w_buf, d_buf, act, slope, grad, low, low_t, row_t, du, hid, mask, qkv, mixed, lse, dmix, dqkv) = refs[23:39]
    (vec, vec_sum, vec_land) = refs[39:42]
    (load_sem, x_send, x_recv, z_send, z_recv, v_send, v_recv) = refs[42:49]
    halves = refs[49:]
    me = Place(groups, parts)
    n = me.count
    wide, width = jnp.float32, du.shape[1]
    count, seq = du.shape[0], mask.shape[1]
    split = mixed.shape[2]
    heads = split // HD
    held = (held0, held1, held2)
    half = width // 2
    bits_order = orders(n)
    turn = [(a, i) for i in range(groups) for a in (2, 1)] + [(0, i) for i in range(groups)]
    slots = list(range(2 * groups)) + [2 * groups + 1 + 2 * i for i in range(groups)]
    units = len(turn)

    def load(slot, src, dst):
        return pltpu.make_async_copy(src, dst, load_sem.at[slot])

    def group(i):
        return (me.t + 1 + i) % groups

    def load_ffn(i):
        g, s = group(i), i % 2
        pairs = ((slope_in, slope), (w2_in, d_buf), (w1_in, w_buf), (act_in, act))
        return [load(4 + 4 * i + k, a.at[g], b.at[s]) for k, (a, b) in enumerate(pairs)]

    def load_heads(i):
        g, s = group(i), i % 2
        pairs = ((w0_in, w_buf.at[(groups + i) % 2]), (qkv_in, qkv.at[s]), (mixed_in, mixed.at[s]), (lse_in, lse.at[s]))
        return [load(4 + 4 * groups + 4 * i + k, a.at[g], b) for k, (a, b) in enumerate(pairs)]

    def start(copies):
        for copy in copies:
            copy.start()

    def finish_all(copies):
        for copy in copies:
            copy.wait()

    entry = [load(0, dz_in, grad), load(1, h_in, hid)]
    start(entry)
    start(load_ffn(0))
    me.enter()
    copies, hops, tiny = {}, {}, {}

    def advance_vectors(stage):
        source = vec if stage == 0 else vec_sum.at[stage - 1]
        if stage:
            tiny[stage - 1].wait_recv()
            before = vec[...] if stage == 1 else vec_sum[stage - 2]
            vec_sum[stage - 1] = before + vec_land[stage - 1]
        peers = [me.partner(stage)] if stage < n else [me.along(j) for j in range(1, groups)]
        for k, peer in enumerate(peers):
            copy = send(source, vec_land.at[stage + k], (v_send, v_recv), stage + k, peer)
            copy.start()
            tiny[stage + k] = copy

    for u, (a, i) in enumerate(turn):
        target = group(i)
        copies[u, 0, 0] = send(
            held[a].at[(target,) + me.pieces(set(range(1, n)), 0)],
            landing.at[u],
            (x_send, x_recv),
            u * 2 * n,
            me.partner(0),
        )
        for stage in range(1, n):
            for h in range(2):
                bits = bits_order[h]
                bit, left = bits[stage - 1], set(bits[stage:])
                copies[u, stage, h] = send(
                    held[a].at[(target,) + me.pieces(left, bit) + (slice(None), pl.ds(h * half, half))],
                    halves[stage - 1].at[u, h],
                    (x_send, x_recv),
                    u * 2 * n + stage * 2 + h,
                    me.partner(bit),
                )
        if i < groups - 1:
            slot = a * (groups - 1) + i
            hops[slot] = send(
                held[a].at[(target,) + me.pieces(())], final.at[slot], (z_send, z_recv), slot, me.along(i + 1)
            )

    def advance(u, stage):
        a, i = turn[u]
        target = group(i)
        for h in range(2):
            if (u, stage - 1, h) not in copies:
                continue
            if stage == 1:
                left, cols, source = set(range(1, n)), slice(None), landing.at[u]
            else:
                left, cols = set(bits_order[h][stage - 1 :]), pl.ds(h * half, half)
                source = halves[stage - 2].at[u, h]
            copies[u, stage - 1, h].wait_recv()
            view = (target,) + me.pieces(left) + (slice(None), cols)
            add_into(held[a].at[view], source, [2] * len(left))
        if stage == n and i < groups - 1:
            hops[a * (groups - 1) + i].start()
        for h in range(2):
            if (u, stage, h) in copies:
                copies[u, stage, h].start()

    plan = Plan()
    before = [-100.0] * (n + 1)

    def made(u):
        for stage in range(n + 1):
            when = plan.now + PASS[0] * stage
            if stage:
                when = max(when, before[stage] + PASS[1], before[stage - 1] + PASS[0])
            before[stage] = when
            plan.add(when, (u, stage))

    for i in range(groups):
        plan.now += 2.8
        made(2 * i)
        plan.point(("down", i), 0.0)
        plan.point(("back", i), 2.8)
        plan.point(("backed", i), 2.8)
        plan.now += 2.8
        made(2 * i + 1)
        plan.point(("up", i), 0.0)
    plan.point(("norm", 0), 3.0)
    plan.point(("norm", 1), 2.0)
    for i in range(groups):
        plan.point(("mix", i), 1.0)
        plan.point(("attend", i), 3.0)
        plan.point(("attended", i), 3.0)
        plan.now += 2.8
        made(2 * groups + i)
        plan.point(("first", i), 0.0)
        plan.point(("finish", i), 2.2)

    def run(index, name, extra=None):
        at_point(plan, advance, groups, index, name, extra)

    def put(a, g, cols, value):
        shape = held[a].shape[1:-1] + value.shape[1:]
        held[a][(g,) + (slice(None),) * (n + 1) + (cols,)] = value.astype(LOW).reshape(shape)

    def products(a, g, left, right):
        def step(i, carry):
            cols = pl.ds(pl.multiple_of(i * TILE, TILE), TILE)
            put(a, g, cols, jnp.dot(left[...], right[:, cols], preferred_element_type=wide))
            return carry

        lax.fori_loop(0, width // TILE, step, 0)

    def flip(dst, r, value):
        dst[:, r] = value.T

    vec[...] = jnp.zeros_like(vec)
    finish_all(entry)

    def prepare(i, carry):
        r = pl.ds(pl.multiple_of(i * 128, 128), 128)
        g = grad[r, :].astype(LOW)
        low[r, :] = g
        flip(low_t, r, g)
        y, _, _ = norm_forward(hid[r, :], sums[3:4], sums[4:5])
        flip(row_t, r, y.astype(LOW))
        return carry

    lax.fori_loop(0, count // 128, prepare, 0)
    make_mask(mask, segments, me.t * mask.shape[0])

    half_way = count // TILE // 2 - 1

    def ffn_group(i, outer):
        g, s = group(i), i % 2

        @pl.when(i + 1 < groups)
        def _():
            start(load_ffn(i + 1))

        @pl.when(i + 1 == groups)
        def _():
            start(load_heads(0))

        finish_all(load_ffn(i))
        products(2, g, low_t, act.at[s])
        run(i, "down")

        def back(k, carry):
            r = pl.ds(pl.multiple_of(k * TILE, TILE), TILE)
            part = matmul_t(low[r, :], d_buf[s])
            part = (part * slope[s, r, :].astype(wide)).astype(LOW)
            du[r, :] = part
            grad[r, :] = grad[r, :] + matmul_t(part, w_buf[s])
            run(i, "back", k == half_way)
            return carry + fold(part.astype(wide))

        total = lax.fori_loop(0, count // TILE, back, jnp.zeros((8, width), wide))
        vec[pl.ds(groups + g, 1), :] = jnp.sum(total, axis=0, keepdims=True)
        run(i, "backed")
        products(1, g, row_t, du)
        run(i, "up")
        return outer

    lax.fori_loop(0, groups, ffn_group, 0)
    tokens = load(2, inputs.at[pl.ds(me.t * count, count)], du)
    tokens.start()

    def norm(i, carry):
        r = pl.ds(pl.multiple_of(i * 64, 64), 64)
        _, scaled, inverse = norm_forward(hid[r, :], sums[3:4], sums[4:5])
        dy = grad[r, :]
        dh = norm_backward(dy, scaled, inverse, sums[3:4])
        dh_low = dh.astype(LOW)
        grad[r, :] = dh
        low[r, :] = dh_low
        return (carry[0] + fold(dy * scaled), carry[1] + fold(dy), carry[2] + fold(dh_low.astype(wide)))

    zero = jnp.zeros((8, width), wide)
    found = lax.fori_loop(0, count // 64, norm, (zero, zero, zero))
    for k in range(3):
        vec[2 * groups + k : 2 * groups + k + 1, :] = jnp.sum(found[k], axis=0, keepdims=True)
    vec[2 * groups + 3 : 2 * groups + 6, :] = sums[0:3, :]
    for task in plan.at["norm", 0]:
        advance(*task)
    tokens.wait()

    def turn_over(i, carry):
        r = pl.ds(pl.multiple_of(i * 128, 128), 128)
        flip(low_t, r, low[r, :])
        flip(row_t, r, du[r, :])
        return carry

    lax.fori_loop(0, count // 128, turn_over, 0)
    for task in plan.at["norm", 1]:
        advance(*task)

    span = 128
    blocks = seq // span
    scale = HD ** (-0.5)

    def heads_group(i, outer):
        g, s, ws = group(i), i % 2, (groups + i) % 2

        @pl.when(i + 1 < groups)
        def _():
            start(load_heads(i + 1))

        finish_all(load_heads(i))

        def mix(k, carry):
            r = pl.ds(pl.multiple_of(k * TILE, TILE), TILE)
            dmix[r, :] = matmul_t(low[r, :], w_buf[ws, 3 * split :, :]).astype(LOW)
            return carry

        lax.fori_loop(0, count // TILE, mix, 0)
        run(i, "mix")

        def packed_row(p, carry):
            base = p * seq

            def at(lo, hi):
                return pl.ds(pl.multiple_of(base + lo, span), hi - lo)

            turned = qkv[s, at(0, seq), split : 2 * split].T
            dks = [[None] * heads for _ in range(blocks)]
            dvs = [[None] * heads for _ in range(blocks)]
            dqs = []

            def gather_sum(total, lo, h, value):
                for c in range(value.shape[0] // span):
                    piece = value[c * span : (c + 1) * span]
                    old = total[lo // span + c][h]
                    total[lo // span + c][h] = piece if old is None else old + piece

            def write(b):
                parts_b = [dqs[b]] + [x * scale for x in dks[b]] + dvs[b]
                dqkv[at(b * span, (b + 1) * span), :] = jnp.concatenate(parts_b, axis=1).astype(LOW)

            for b in range(blocks):
                lo, hi = key_window(b, blocks, span)
                here = (b * span, (b + 1) * span)
                bias = mask[p, lo:hi, here[0] : here[1]]
                work, grads = [], []
                for h in range(heads):
                    q = qkv[s, at(*here), h * HD : (h + 1) * HD]
                    k = qkv[s, at(lo, hi), split + h * HD : split + (h + 1) * HD]
                    v = qkv[s, at(lo, hi), 2 * split + h * HD : 2 * split + (h + 1) * HD]
                    do = dmix[at(*here), h * HD : (h + 1) * HD]
                    work.append((q, do, matmul_t(k, q), matmul_t(v, do)))
                for h in range(heads):
                    q, do, score, dp = work[h]
                    prob = jnp.exp2(score * (SCORE * scale) + bias - lse[s, p * blocks + b, h : h + 1, :])
                    inner = jnp.sum(prob * dp, axis=0, keepdims=True)
                    grads.append((prob.astype(LOW), (prob * (dp - inner)).astype(LOW)))
                dq = []
                for h in range(heads):
                    q, do, _, _ = work[h]
                    prob, ds = grads[h]
                    gather_sum(dvs, lo, h, jnp.dot(prob, do, preferred_element_type=wide))
                    gather_sum(dks, lo, h, jnp.dot(ds, q, preferred_element_type=wide))
                    dq.append(jnp.dot(turned[h * HD : (h + 1) * HD, lo:hi], ds, preferred_element_type=wide))
                dqs.append(jnp.concatenate(dq, axis=0).T * scale)
                if b:
                    write(b - 1)
            write(blocks - 1)
            run(i, "attend", p == 0)
            return carry

        lax.fori_loop(0, count // seq, packed_row, 0)
        run(i, "attended")

        def first_cols(k, carry):
            cols = pl.ds(pl.multiple_of(k * TILE, TILE), TILE)
            put(0, g, cols, jnp.dot(row_t[...], dqkv[:, cols], preferred_element_type=wide))
            return carry

        edge = 3 * split // TILE * TILE
        lax.fori_loop(0, edge // TILE, first_cols, 0)
        tail = jnp.concatenate(
            [
                jnp.dot(row_t[...], dqkv[:, edge:], preferred_element_type=wide),
                jnp.dot(low_t[...], mixed[s], preferred_element_type=wide),
            ],
            axis=1,
        )
        put(0, g, slice(edge, width), tail)
        run(i, "first")

        def finish(k, carry):
            r = pl.ds(pl.multiple_of(k * TILE, TILE), TILE)
            part = dqkv[r, :]
            grad[r, :] = grad[r, :] + jnp.dot(part, w_buf[ws, : 3 * split, :], preferred_element_type=wide)
            return carry + fold(part.astype(wide))

        total = lax.fori_loop(0, count // TILE, finish, jnp.zeros((8, 3 * split), wide))
        vec[pl.ds(g, 1), : 3 * split] = jnp.sum(total, axis=0, keepdims=True)
        run(i, "finish")
        return outer

    lax.fori_loop(0, groups, heads_group, 0)
    result = load(3, grad, gi_out)
    result.start()
    rest = [task for _, task in plan.tasks]
    for stage in range(n + 1):
        advance_vectors(stage)
        for task in rest[:2] if stage < n else rest:
            advance(*task)
        rest = rest[2:]
    total = vec_sum[n - 1]
    for j in range(groups - 1):
        tiny[n + j].wait_recv()
        total = total + vec_land[n + j]
    vec_out[...] = total
    for a, out in ((2, out2), (1, out1), (0, out0)):
        total = held[a][(me.t,) + me.pieces(())].astype(wide)
        for j in range(groups - 1):
            slot = a * (groups - 1) + j
            hops[slot].wait_recv()
            total = total + final[slot].astype(wide)
        out[...] = total
    for copy in list(tiny.values()) + list(copies.values()) + list(hops.values()):
        copy.wait_send()
    result.wait()


def backward(saved, weights, sums, inputs, segments, groups, parts):
    n = parts.bit_length() - 1
    _, dz, hid, qkv, mixed, act, slope, lse = saved
    count, width = dz.shape
    split = width // groups
    piece = width // parts
    shape = (groups,) + (2,) * n + (piece, width)
    seq = segments.shape[1]
    packed = count // seq
    units = 3 * groups
    anywhere, vmem = pl.BlockSpec(memory_space=pl.ANY), pl.BlockSpec(memory_space=pltpu.VMEM)
    wide, dma = jnp.float32, pltpu.SemaphoreType.DMA
    lines = -(-(2 * groups + 6) // 8) * 8
    return pl.pallas_call(
        functools.partial(backward_kernel, groups, parts),
        out_shape=[jax.ShapeDtypeStruct((count, width), wide)]
        + [jax.ShapeDtypeStruct((piece, width), wide)] * 3
        + [jax.ShapeDtypeStruct((lines, width), wide)],
        in_specs=[anywhere] * 11 + [vmem] * 2,
        out_specs=[anywhere] + [vmem] * 4,
        scratch_shapes=[pltpu.VMEM(shape, LOW)] * 3
        + [
            pltpu.VMEM((units,) + (2,) * (n - 1) + (piece, width), LOW),
            pltpu.VMEM((3 * (groups - 1), piece, width), LOW),
            pltpu.VMEM((2, width, width), LOW),
            pltpu.VMEM((2, width, width), LOW),
            pltpu.VMEM((2, count, width), LOW),
            pltpu.VMEM((2, count, width), LOW),
            pltpu.VMEM((count, width), wide),
            pltpu.VMEM((count, width), LOW),
            pltpu.VMEM((width, count), LOW),
            pltpu.VMEM((width, count), LOW),
            pltpu.VMEM((count, width), LOW),
            pltpu.VMEM((count, width), wide),
            pltpu.VMEM((packed, seq, seq), wide),
            pltpu.VMEM((2, count, 3 * split), LOW),
            pltpu.VMEM((2, count, split), LOW),
            pltpu.VMEM((2, count // 128, 8, 128), wide),
            pltpu.VMEM((count, split), LOW),
            pltpu.VMEM((count, 3 * split), LOW),
            pltpu.VMEM((lines, width), wide),
            pltpu.VMEM((n, lines, width), wide),
            pltpu.VMEM((n + groups - 1, lines, width), wide),
            dma((8 * groups + 4,)),
            dma((units * 2 * n,)),
            dma((units * 2 * n,)),
            dma((3 * (groups - 1),)),
            dma((3 * (groups - 1),)),
            dma((n + groups - 1,)),
            dma((n + groups - 1,)),
        ]
        + [pltpu.VMEM((units, 2) + (2,) * (n - 1 - s) + (piece, width // 2), LOW) for s in range(1, n)],
        compiler_params=pltpu.CompilerParams(
            collective_id=3, has_side_effects=True, vmem_limit_bytes=67043328
        ),
        name="backward_and_scatter",
    )(dz, hid, qkv, mixed, act, slope, lse, *weights, inputs, segments, sums)


def pick(values, size, index):
    total = jnp.zeros((values.shape[0], size), values.dtype)
    for k in range(values.shape[1] // size):
        total = jnp.where(index == k, values[:, k * size : (k + 1) * size], total)
    return total


def outputs_kernel(groups, parts, *refs):
    out_in, gi_in, first, up, down, vec = refs[:6]
    out, gi, g_query, g_key, g_value, g_output, g_hidden, g_project, bias_qv, bias_h, vectors = refs[6:17]
    held_out, held_gi, load_sem, store_sem = refs[17:]
    t, d = lax.axis_index("tensor"), lax.axis_index("dp")
    count, width = held_gi.shape
    split, piece = width // groups, HD // parts
    size = count // 4
    loads, stores = [], []
    for k in range(4):
        r = pl.ds(k * size, size)
        for a, b, c in ((gi_in, held_gi, gi), (out_in, held_out, out)):
            loads.append(pltpu.make_async_copy(a.at[r], b.at[r], load_sem.at[len(loads)]))
            stores.append(pltpu.make_async_copy(b.at[r], c.at[r], store_sem.at[len(stores)]))
            loads[-1].start()
    for k, target in enumerate((g_query, g_key, g_value)):
        target[...] = first[:, k * split : (k + 1) * split]
    g_output[...] = first[:, 3 * split :].T
    g_hidden[...] = up[...]
    g_project[...] = down[...]
    for a, b in zip(loads, stores):
        a.wait()
        b.start()
    own, hidden = vec[pl.ds(t, 1), :], vec[pl.ds(groups + t, 1), :]
    heads = split // HD
    pieces = [own[:, k * HD : (k + 1) * HD] for k in range(heads)]
    pieces += [own[:, 2 * split + k * HD : 2 * split + (k + 1) * HD] for k in range(heads)]
    pieces += [hidden[:, k * HD : (k + 1) * HD] for k in range(width // HD)]
    found = pick(jnp.concatenate(pieces, axis=0), piece, d)
    for h in range(heads):
        bias_qv[h] = jnp.concatenate([found[h : h + 1], found[heads + h : heads + h + 1]], axis=0)
    bias_h[...] = found[2 * heads :].T
    vectors[...] = pick(vec[2 * groups : 2 * groups + 6, :], width // (parts * groups), d * groups + t)
    for b in stores:
        b.wait()


def finish_outputs(output, grad_input, first, up, down, vec, groups, parts):
    (count, width), (piece, _) = grad_input.shape, first.shape
    split, wide = width // groups, jnp.float32
    shapes = [(count, width)] + [(piece, split)] * 3 + [(split, piece), (piece, width), (piece, width)]
    shapes += [(split // HD, 2, HD // parts), (HD // parts, width // HD), (6, width // (parts * groups))]
    anywhere, vmem = pl.BlockSpec(memory_space=pl.ANY), pl.BlockSpec(memory_space=pltpu.VMEM)
    return pl.pallas_call(
        functools.partial(outputs_kernel, groups, parts),
        out_shape=[jax.ShapeDtypeStruct((count, width), LOW)] + [jax.ShapeDtypeStruct(s, wide) for s in shapes],
        in_specs=[anywhere] * 2 + [vmem] * 4,
        out_specs=[anywhere] * 2 + [vmem] * 9,
        scratch_shapes=[
            pltpu.VMEM((count, width), LOW),
            pltpu.VMEM((count, width), wide),
            pltpu.SemaphoreType.DMA((8,)),
            pltpu.SemaphoreType.DMA((8,)),
        ],
        name="outputs",
    )(output, grad_input, first, up, down, vec)


def per_device_small(
    inputs,
    segments,
    w_query,
    w_key,
    w_value,
    b_query,
    b_value,
    w_output,
    b_output,
    gain_attn,
    shift_attn,
    w_hidden,
    b_hidden,
    w_project,
    b_project,
    gain_ffn,
    shift_ffn,
    cotangent,
):
    seq_len = segments.shape[1]
    share_tokens = cotangent.shape[0]
    share_rows = share_tokens // seq_len
    width = inputs.shape[1]
    groups, parts = lax.axis_size("tensor"), lax.axis_size("dp")
    place, part = lax.axis_index("tensor"), lax.axis_index("dp")
    low = jnp.bfloat16
    wide = jnp.float32

    tokens = lax.dynamic_slice_in_dim(inputs, place * share_tokens, share_tokens, 0)
    rows_segments = lax.dynamic_slice_in_dim(segments, place * share_rows, share_rows, 0)
    split = w_query.shape[1]
    small = jnp.concatenate([b_query, b_value, b_hidden]).reshape(-1, 128)
    small_rows = small.shape[0]
    small = jnp.pad(small, ((0, -small_rows % 16), (0, 0)))
    first = jnp.concatenate([w_query, w_key, w_value, w_output.T], axis=1)
    (first, w_up, w_down), small = gather([first, w_hidden, w_project], small, groups, parts)
    w_in = first[:, :, : 3 * split].reshape(groups, width, 3, split).transpose(1, 2, 0, 3)
    w_in = w_in.reshape(width, 3 * groups * split)
    w_out = first[:, :, 3 * split :].transpose(0, 2, 1).reshape(groups * split, width)
    w_up = w_up.transpose(1, 0, 2).reshape(width, -1)
    w_down = w_down.reshape(-1, width)
    small = small[:, :small_rows].reshape(groups, -1).astype(wide)
    bias_query = small[:, :split].reshape(-1)
    bias_value = small[:, split : 2 * split].reshape(-1)
    bias_hidden = small[:, 2 * split :].reshape(-1)
    full = groups * split
    head_shape = (share_rows, seq_len, full // HD, HD)

    attn_gain = gain_attn.astype(wide)
    attn_shift = shift_attn.astype(wide)
    attn_bias = b_output.astype(wide)
    ffn_gain = gain_ffn.astype(wide)
    ffn_shift = shift_ffn.astype(wide)
    ffn_bias = b_project.astype(wide)
    grad_out = cotangent.astype(wide)

    projected = jnp.dot(tokens, w_in, preferred_element_type=wide)
    queries = (projected[:, :full] + bias_query).astype(low)
    keys_in = projected[:, full : 2 * full].astype(low)
    values = (projected[:, 2 * full :] + bias_value).astype(low)
    query_heads = queries.reshape(head_shape)
    key_heads = keys_in.reshape(head_shape)
    value_heads = values.reshape(head_shape)
    mixed_heads, logsum = lax.map(attend_forward, (query_heads, key_heads, value_heads, rows_segments))
    mixed = mixed_heads.reshape(share_tokens, full)
    hidden = tokens.astype(wide) + (jnp.dot(mixed, w_out, preferred_element_type=wide) + attn_bias)
    normed, scaled, inverse = norm_forward(hidden, attn_gain, attn_shift)
    normed_low = normed.astype(low)
    hidden_pre = jnp.dot(normed_low, w_up, preferred_element_type=wide) + bias_hidden
    active, gelu_pull = jax.vjp(gelu_exact, hidden_pre)
    active_low = active.astype(low)
    block_sum = normed + (jnp.dot(active_low, w_down, preferred_element_type=wide) + ffn_bias)
    output, scaled_out, inverse_out = norm_forward(block_sum, ffn_gain, ffn_shift)
    grad_sum = norm_backward(grad_out, scaled_out, inverse_out, ffn_gain)
    grad_ffn_gain = jnp.sum(grad_out * scaled_out, axis=0)
    grad_ffn_shift = jnp.sum(grad_out, axis=0)
    grad_sum_low = grad_sum.astype(low)
    grad_ffn_bias = jnp.sum(grad_sum_low.astype(wide), axis=0)
    grad_active = times_transposed(grad_sum_low, w_down)
    grad_w_down = cross_rows(grad_sum_low, active_low)
    grad_hidden_pre = gelu_pull(grad_active)[0].astype(low)
    grad_b_hidden = jnp.sum(grad_hidden_pre.astype(wide), axis=0)
    grad_w_up = cross_rows(normed_low, grad_hidden_pre)
    grad_normed = grad_sum + times_transposed(grad_hidden_pre, w_up)
    grad_hidden = norm_backward(grad_normed, scaled, inverse, attn_gain)
    grad_hidden_low = grad_hidden.astype(low)
    grad_attn_gain = jnp.sum(grad_normed * scaled, axis=0)
    grad_attn_shift = jnp.sum(grad_normed, axis=0)
    grad_attn_bias = jnp.sum(grad_hidden_low.astype(wide), axis=0)
    grad_w_out = cross_rows(grad_hidden_low, mixed)
    grad_mixed = times_transposed(grad_hidden_low, w_out).astype(low).reshape(head_shape)
    grad_q, grad_k, grad_v = lax.map(
        attend_backward, (query_heads, key_heads, value_heads, rows_segments, logsum, grad_mixed)
    )
    grad_q = grad_q.reshape(share_tokens, full)
    grad_k = grad_k.reshape(share_tokens, full)
    grad_v = grad_v.reshape(share_tokens, full)
    grad_projected = jnp.concatenate([grad_q, grad_k, grad_v], axis=1)
    grad_w_in = cross_rows(tokens, grad_projected)
    grad_b_query = jnp.sum(grad_q.astype(wide), axis=0)
    grad_b_value = jnp.sum(grad_v.astype(wide), axis=0)
    grad_input = grad_hidden + times_transposed(grad_projected, w_in)

    def parted(grad):
        return grad.astype(low).reshape(width, groups, -1).transpose(1, 0, 2)

    first = jnp.concatenate(
        [parted(grad_w_in[:, i * full : (i + 1) * full]) for i in range(3)] + [parted(grad_w_out)], axis=2
    )
    vectors = jnp.concatenate(
        [
            jnp.stack([grad_b_query, grad_b_value]).reshape(2 * groups, split),
            grad_b_hidden.reshape(-1, split),
            jnp.stack(
                [
                    grad_attn_gain,
                    grad_attn_shift,
                    grad_attn_bias,
                    grad_ffn_gain,
                    grad_ffn_shift,
                    grad_ffn_bias,
                ]
            ).reshape(-1, split),
        ],
        axis=0,
    )
    count = vectors.size // split
    vectors = vectors.reshape(-1, 128)
    (sum_first, sum_up, sum_down, vectors) = scatter(
        [first, parted(grad_w_up), parted(grad_w_down)], vectors, groups, parts
    )
    vectors = vectors.reshape(count, split)
    bias_qv = vectors[: 2 * groups].reshape(2, groups, split // HD, HD)
    rest = vectors[2 * groups :]
    hid = bias_hidden.shape[0] // split
    bias_h = rest[:hid].reshape(groups, -1, HD)
    vec = rest[hid:].reshape(6, -1)
    piece = HD // parts
    bias_qv = lax.dynamic_slice_in_dim(bias_qv, place, 1, 1)[:, 0]
    bias_qv = lax.dynamic_slice_in_dim(bias_qv, part * piece, piece, 2)
    bias_h = lax.dynamic_slice_in_dim(bias_h, place, 1, 0)[0]
    bias_h = lax.dynamic_slice_in_dim(bias_h, part * piece, piece, 1)
    piece = width // (parts * groups)
    vec = lax.dynamic_slice_in_dim(vec, (part * groups + place) * piece, piece, 1)
    return (
        output.astype(low),
        grad_input,
        sum_first[:, :split],
        sum_first[:, split : 2 * split],
        sum_first[:, 2 * split : 3 * split],
        sum_first[:, 3 * split :].T,
        sum_up,
        sum_down.T,
        bias_qv,
        bias_h,
        vec,
    )


def per_device(
    inputs,
    segments,
    w_query,
    w_key,
    w_value,
    b_query,
    b_value,
    w_output,
    b_output,
    gain_attn,
    shift_attn,
    w_hidden,
    b_hidden,
    w_project,
    b_project,
    gain_ffn,
    shift_ffn,
    cotangent,
):
    if (inputs.shape[1] // lax.axis_size("dp")) % 16:
        return per_device_small(
            inputs, segments, w_query, w_key, w_value, b_query, b_value, w_output, b_output, gain_attn, shift_attn,
            w_hidden, b_hidden, w_project, b_project, gain_ffn, shift_ffn, cotangent,
        )
    width, split = w_query.shape
    groups, parts = lax.axis_size("tensor"), lax.axis_size("dp")
    biases = [b_query, b_value, b_hidden]
    shared = [b_output, gain_attn, shift_attn, gain_ffn, shift_ffn, b_project]
    first = jnp.concatenate([w_query.T, w_key.T, w_value.T, w_output], axis=0)
    saved, weights, sums = forward(
        [first, w_hidden, w_project], inputs, cotangent, biases, shared, segments, groups, parts
    )
    grad_input, sum_first, sum_up, sum_down, vectors = backward(
        saved, weights, sums, inputs, segments, groups, parts
    )
    found = finish_outputs(saved[0], grad_input, sum_first, sum_up, sum_down, vectors, groups, parts)
    return (*found[:7], found[7].T, found[8].transpose(1, 0, 2), found[9].T, found[10])


def solution(mesh):
    in_specs = (
        P("dp", None),
        P("dp", None),
        P(None, "tensor"),
        P(None, "tensor"),
        P(None, "tensor"),
        P("tensor"),
        P("tensor"),
        P("tensor", None),
        P(),
        P(),
        P(),
        P(None, "tensor"),
        P("tensor"),
        P("tensor", None),
        P(),
        P(),
        P(),
        P(("dp", "tensor"), None),
    )
    out_specs = (
        P(("dp", "tensor"), None),
        P(("dp", "tensor"), None),
        P("dp", "tensor"),
        P("dp", "tensor"),
        P("dp", "tensor"),
        P("tensor", "dp"),
        P("dp", "tensor"),
        P("tensor", "dp"),
        P(None, "tensor", "dp"),
        P("tensor", "dp"),
        P(None, ("dp", "tensor")),
    )
    return jax.shard_map(
        per_device, mesh=mesh, in_specs=in_specs, out_specs=out_specs, check_vma=False
    )
```

```python
import functools
import jax
import jax.numpy as jnp
from jax import lax
from jax.experimental import pallas as pl
from jax.experimental.pallas import tpu as pltpu
from jax.sharding import PartitionSpec as P

HD = 64
MESH = pl.DeviceIdType.MESH
LOW = jnp.bfloat16


class Place:
    def __init__(self, groups, parts):
        self.groups, self.parts = groups, parts
        self.t, self.d = lax.axis_index("tensor"), lax.axis_index("dp")
        self.count = parts.bit_length() - 1
        self.bits = [(self.d // (1 << i)) % 2 for i in range(self.count)]

    def partner(self, bit):
        return (self.d + (1 - 2 * self.bits[bit]) * (1 << bit), self.t)

    def along(self, step):
        return (self.d, (self.t + step) % self.groups)

    def enter(self):
        barrier = pltpu.get_barrier_semaphore()
        peers = [self.partner(b) for b in range(self.count)]
        peers += [self.along(j) for j in range(1, self.groups)]
        for peer in peers:
            pl.semaphore_signal(barrier, inc=1, device_id=peer, device_id_type=MESH)
        pl.semaphore_wait(barrier, len(peers))

    def pieces(self, open_bits, flipped=None):
        index = []
        for bit in reversed(range(self.count)):
            own = self.bits[bit]
            index.append(slice(None) if bit in open_bits else 1 - own if bit == flipped else own)
        return tuple(index)


def send(src, dst, sems, slot, peer):
    return pltpu.make_async_remote_copy(
        src_ref=src,
        dst_ref=dst,
        send_sem=sems[0].at[slot],
        recv_sem=sems[1].at[slot],
        device_id=peer,
        device_id_type=MESH,
    )


def orders(count):
    rest = list(range(1, count))
    return [rest, rest[::-1]]


def gather_kernel(groups, parts, arrays, *refs):
    shards, small = refs[:arrays], refs[arrays]
    outs, small_out = refs[arrays + 1 : 2 * arrays + 1], refs[2 * arrays + 1]
    held, small_held = refs[2 * arrays + 2 : 3 * arrays + 2], refs[3 * arrays + 2]
    load_sem, store_sem, z_send, z_recv, x_send, x_recv, s_send, s_recv = refs[3 * arrays + 3 :]
    me = Place(groups, parts)
    n = me.count
    half = shards[0].shape[-1] // 2
    bits_order = orders(n)
    me.enter()
    own = [me.t] + list(me.pieces(()))
    hops, doubles, tiny = {}, {}, []
    for j in range(1, groups):
        tiny.append(send(small, small_held.at[j - 1], (s_send, s_recv), j - 1, me.along(j)))
        tiny[-1].start()
    for a in range(arrays):
        for j in range(1, groups):
            u = a * (groups - 1) + j - 1
            hops[u] = send(
                shards[a].at[tuple(me.pieces(()))], held[a].at[tuple(own)], (z_send, z_recv), u, me.along(j)
            )
            hops[u].start()
    loads = []
    for a in range(arrays):
        loads.append(pltpu.make_async_copy(shards[a], held[a].at[me.t], load_sem.at[a]))
        loads[-1].start()

    units = arrays * (groups - 1)
    stores = []

    def advance(u, stage):
        a, j = divmod(u, groups - 1)
        source = (me.t + groups - 1 - j) % groups
        if stage == 0:
            hops[u].wait_recv()
        else:
            for h in range(2):
                if stage < n or h == 0:
                    doubles[u, stage - 1, h].wait_recv()
        if stage == n:
            out = pltpu.make_async_copy(held[a].at[source], outs[a].at[source], store_sem.at[u])
            out.start()
            stores.append(out)
            return
        for h in range(2):
            if stage == n - 1:
                if h == 1:
                    continue
                bit, done, cols = 0, set(range(1, n)), slice(None)
            else:
                bit, done = bits_order[h][stage], set(bits_order[h][:stage])
                cols = pl.ds(h * half, half)
            view = (source,) + me.pieces(done) + (slice(None), cols)
            slot = (u * n + stage) * 2 + h
            copy = send(held[a].at[view], held[a].at[view], (x_send, x_recv), slot, me.partner(bit))
            copy.start()
            doubles[u, stage, h] = copy

    for tick in range(units + n):
        for stage in range(n + 1):
            u = tick - stage
            if 0 <= u < units:
                advance(u, stage)
    for a in range(arrays):
        loads[a].wait()
        out = pltpu.make_async_copy(held[a].at[me.t], outs[a].at[me.t], store_sem.at[units + a])
        out.start()
        stores.append(out)
    small_out[me.t] = small[...]
    for j in range(1, groups):
        tiny[j - 1].wait()
        small_out[(me.t + groups - j) % groups] = small_held[j - 1]
    for copy in hops.values():
        copy.wait_send()
    for copy in doubles.values():
        copy.wait_send()
    for copy in stores:
        copy.wait()


def gather(shards, small, groups, parts):
    arrays, n = len(shards), parts.bit_length() - 1
    rows, cols = shards[0].shape[0] // parts, shards[0].shape[1]
    shape = (2,) * n + (rows, cols)
    units = arrays * (groups - 1)
    any_space = pl.BlockSpec(memory_space=pl.ANY)
    vmem = pl.BlockSpec(memory_space=pltpu.VMEM)
    *outs, small = pl.pallas_call(
        functools.partial(gather_kernel, groups, parts, arrays),
        out_shape=[jax.ShapeDtypeStruct((groups,) + shape, LOW)] * arrays
        + [jax.ShapeDtypeStruct((groups,) + small.shape, LOW)],
        in_specs=[any_space] * arrays + [vmem],
        out_specs=[any_space] * arrays + [vmem],
        scratch_shapes=[pltpu.VMEM((groups,) + shape, LOW)] * arrays
        + [
            pltpu.VMEM((groups - 1,) + small.shape, LOW),
            pltpu.SemaphoreType.DMA((arrays,)),
            pltpu.SemaphoreType.DMA((units + arrays,)),
            pltpu.SemaphoreType.DMA((units,)),
            pltpu.SemaphoreType.DMA((units,)),
            pltpu.SemaphoreType.DMA((units * n * 2,)),
            pltpu.SemaphoreType.DMA((units * n * 2,)),
            pltpu.SemaphoreType.DMA((groups - 1,)),
            pltpu.SemaphoreType.DMA((groups - 1,)),
        ],
        compiler_params=pltpu.CompilerParams(
            collective_id=0, has_side_effects=True, vmem_limit_bytes=60 << 20
        ),
        name="gather_weights",
    )(*[s.reshape(shape) for s in shards], small)
    return [o.reshape(groups, parts * rows, cols) for o in outs], small


def add_into(dst, src, lead):
    def one(i, carry):
        index = []
        for size in reversed(lead):
            index.append(i % size)
            i = i // size
        index = tuple(reversed(index))
        total = dst[index].astype(jnp.float32) + src[index].astype(jnp.float32)
        dst[index] = total.astype(LOW)
        return carry

    total = 1
    for size in lead:
        total *= size
    lax.fori_loop(0, total, one, 0)


def scatter_kernel(groups, parts, arrays, *refs):
    parted, vec = refs[:arrays], refs[arrays]
    outs, vec_out = refs[arrays + 1 : 2 * arrays + 1], refs[2 * arrays + 1]
    p = 2 * arrays + 2
    held = refs[p : p + arrays]
    n = parts.bit_length() - 1
    p += arrays
    landing = refs[p]
    halves = refs[p + 1 : p + n]
    final = refs[p + n]
    load_sem, x_send, x_recv, z_send, z_recv, vec_sum, vec_land, v_send, v_recv = refs[p + n + 1 :]
    me = Place(groups, parts)
    half = parted[0].shape[-1] // 2
    bits_order = orders(n)
    units = arrays * groups
    loads = []
    turn = [(u // groups, (me.t + 1 + u % groups) % groups) for u in range(units)]
    for u in range(units):
        a, target = turn[u]
        copy = pltpu.make_async_copy(parted[a].at[target], held[a].at[target], load_sem.at[u])
        copy.start()
        loads.append(copy)
    me.enter()
    copies, hops, tiny = {}, {}, {}

    def advance_vectors(stage):
        source = vec if stage == 0 else vec_sum.at[stage - 1]
        if stage:
            tiny[stage - 1].wait_recv()
            before = vec[...] if stage == 1 else vec_sum[stage - 2]
            vec_sum[stage - 1] = before + vec_land[stage - 1]
        peers = [me.partner(stage)] if stage < n else [me.along(j) for j in range(1, groups)]
        for k, peer in enumerate(peers):
            copy = send(source, vec_land.at[stage + k], (v_send, v_recv), stage + k, peer)
            copy.start()
            tiny[stage + k] = copy

    def advance(u, stage):
        a, target = turn[u]
        if stage == 0:
            loads[u].wait()
            copy = send(
                held[a].at[(target,) + me.pieces(set(range(1, n)), 0)],
                landing.at[u],
                (x_send, x_recv),
                u * 2 * n,
                me.partner(0),
            )
            copy.start()
            copies[u, 0, 0] = copy
            return
        for h in range(2):
            if stage == 1:
                if h == 1:
                    continue
                left, cols, source = set(range(1, n)), slice(None), landing.at[u]
            else:
                bits = bits_order[h]
                left, cols = set(bits[stage - 1 :]), pl.ds(h * half, half)
                source = halves[stage - 2].at[u, h]
            copies[u, stage - 1, h].wait_recv()
            view = (target,) + me.pieces(left) + (slice(None), cols)
            add_into(held[a].at[view], source, [2] * len(left))
        if stage == n:
            if u % groups < groups - 1:
                j = u % groups + 1
                slot = a * (groups - 1) + j - 1
                hops[slot] = send(
                    held[a].at[(target,) + me.pieces(())], final.at[slot], (z_send, z_recv), slot, me.along(j)
                )
                hops[slot].start()
            return
        for h in range(2):
            bits = bits_order[h]
            bit, left = bits[stage - 1], set(bits[stage:])
            view = (target,) + me.pieces(left, bit) + (slice(None), pl.ds(h * half, half))
            copy = send(
                held[a].at[view],
                halves[stage - 1].at[u, h],
                (x_send, x_recv),
                u * 2 * n + stage * 2 + h,
                me.partner(bit),
            )
            copy.start()
            copies[u, stage, h] = copy

    for tick in range(units + n):
        if tick <= n:
            advance_vectors(tick)
        for stage in reversed(range(n + 1)):
            u = tick - stage
            if 0 <= u < units:
                advance(u, stage)
    total = vec_sum[n - 1]
    for j in range(groups - 1):
        tiny[n + j].wait_recv()
        total = total + vec_land[n + j]
    vec_out[...] = total
    for a in range(arrays):
        total = held[a][(me.t,) + me.pieces(())].astype(jnp.float32)
        for j in range(groups - 1):
            slot = a * (groups - 1) + j
            hops[slot].wait_recv()
            total = total + final[slot].astype(jnp.float32)
        outs[a][...] = total
    for copy in tiny.values():
        copy.wait_send()
    for copy in copies.values():
        copy.wait_send()
    for copy in hops.values():
        copy.wait_send()


def scatter(parted, vec, groups, parts):
    arrays, n = len(parted), parts.bit_length() - 1
    rows, cols = parted[0].shape[1] // parts, parted[0].shape[2]
    shape = (groups,) + (2,) * n + (rows, cols)
    units = arrays * groups
    vmem = pl.BlockSpec(memory_space=pltpu.VMEM)
    return pl.pallas_call(
        functools.partial(scatter_kernel, groups, parts, arrays),
        out_shape=[jax.ShapeDtypeStruct((rows, cols), jnp.float32)] * arrays
        + [jax.ShapeDtypeStruct(vec.shape, jnp.float32)],
        in_specs=[pl.BlockSpec(memory_space=pl.ANY)] * arrays + [vmem],
        out_specs=[vmem] * (arrays + 1),
        scratch_shapes=[pltpu.VMEM(shape, LOW)] * arrays
        + [pltpu.VMEM((units,) + (2,) * (n - 1) + (rows, cols), LOW)]
        + [pltpu.VMEM((units, 2) + (2,) * (n - 1 - s) + (rows, cols // 2), LOW) for s in range(1, n)]
        + [
            pltpu.VMEM((arrays * (groups - 1), rows, cols), LOW),
            pltpu.SemaphoreType.DMA((units,)),
            pltpu.SemaphoreType.DMA((units * 2 * n,)),
            pltpu.SemaphoreType.DMA((units * 2 * n,)),
            pltpu.SemaphoreType.DMA((arrays * (groups - 1),)),
            pltpu.SemaphoreType.DMA((arrays * (groups - 1),)),
            pltpu.VMEM((n,) + vec.shape, jnp.float32),
            pltpu.VMEM((n + groups - 1,) + vec.shape, jnp.float32),
            pltpu.SemaphoreType.DMA((n + groups - 1,)),
            pltpu.SemaphoreType.DMA((n + groups - 1,)),
        ],
        compiler_params=pltpu.CompilerParams(
            collective_id=1, has_side_effects=True, vmem_limit_bytes=60 << 20
        ),
        name="scatter_gradients",
    )(*[g.reshape(shape) for g in parted], vec)


norm_epsilon = 1e-12
root_half = 0.7071067811865476


def norm_forward(values, norm_gain, norm_shift):
    average = jnp.mean(values, axis=-1, keepdims=True)
    centered = values - average
    variance = jnp.mean(centered * centered, axis=-1, keepdims=True)
    inverse = lax.rsqrt(variance + norm_epsilon)
    scaled = centered * inverse
    return (scaled * norm_gain + norm_shift, scaled, inverse)


def norm_backward(grad_out, scaled, inverse, norm_gain):
    weighted = grad_out * norm_gain
    mean_grad = jnp.mean(weighted, axis=-1, keepdims=True)
    mean_proj = jnp.mean(weighted * scaled, axis=-1, keepdims=True)
    return inverse * (weighted - mean_grad - scaled * mean_proj)


def gelu_exact(values):
    return 0.5 * values * (1.0 + lax.erf(values * root_half))


def cross_rows(left, right):
    return lax.dot_general(
        left, right, (((0,), (0,)), ((), ())), preferred_element_type=jnp.float32
    )


def times_transposed(left, right):
    return lax.dot_general(
        left, right, (((1,), (1,)), ((), ())), preferred_element_type=jnp.float32
    )


def masked_scores(queries, keys_in, segment_row):
    same_text = segment_row[:, None] == segment_row[None, :]
    scores = jnp.einsum("qhd,khd->hqk", queries, keys_in, preferred_element_type=jnp.float32)
    scores = scores * queries.shape[2] ** (-0.5)
    return jnp.where(same_text[None], scores, -1000000000.0)


def attend_forward(packed):
    queries, keys_in, values, segment_row = packed
    scores = masked_scores(queries, keys_in, segment_row)
    row_max = jnp.max(scores, axis=-1, keepdims=True)
    exponent = jnp.exp(scores - row_max)
    row_total = jnp.sum(exponent, axis=-1, keepdims=True)
    attn_probs = (exponent / row_total).astype(jnp.bfloat16)
    mixed_heads = jnp.einsum("hqk,khd->qhd", attn_probs, values, preferred_element_type=jnp.float32)
    return (mixed_heads.astype(jnp.bfloat16), row_max + jnp.log(row_total))


def attend_backward(packed):
    queries, keys_in, values, segment_row, logsum, grad_mixed = packed
    score_scale = queries.shape[2] ** (-0.5)
    scores = masked_scores(queries, keys_in, segment_row)
    attn_probs = jnp.exp(scores - logsum)
    grad_probs = jnp.einsum("qhd,khd->hqk", grad_mixed, values, preferred_element_type=jnp.float32)
    grad_values = jnp.einsum(
        "hqk,qhd->khd",
        attn_probs.astype(jnp.bfloat16),
        grad_mixed,
        preferred_element_type=jnp.float32,
    )
    inner_sum = jnp.sum(attn_probs * grad_probs, axis=-1, keepdims=True)
    grad_scores = (attn_probs * (grad_probs - inner_sum)).astype(jnp.bfloat16)
    grad_queries = (
        jnp.einsum("hqk,khd->qhd", grad_scores, keys_in, preferred_element_type=jnp.float32)
        * score_scale
    )
    grad_keys = (
        jnp.einsum("hqk,qhd->khd", grad_scores, queries, preferred_element_type=jnp.float32)
        * score_scale
    )
    return (
        grad_queries.astype(jnp.bfloat16),
        grad_keys.astype(jnp.bfloat16),
        grad_values.astype(jnp.bfloat16),
    )


def matmul_t(left, right):
    return lax.dot_general(left, right, (((1,), (1,)), ((), ())), preferred_element_type=jnp.float32)


TILE = 256
HOP = (9.0, 6.0, 5.0)
PASS = (8.0, 7.0)
SCORE = 1.4426950408889634


def row_tiles(count, size, body, hook=None):
    def step(i, carry):
        body(pl.ds(pl.multiple_of(i * size, size), size))
        if hook:
            hook(i)
        return carry

    lax.fori_loop(0, count // size, step, 0)


class Plan:
    def __init__(self):
        self.now, self.tasks, self.at = 0.0, [], {}

    def add(self, when, task):
        self.tasks.append((when, task))
        self.tasks.sort(key=lambda pair: pair[0])

    def point(self, name, spent, until=None):
        self.now += spent
        if until is not None:
            whens = [when for when, task in self.tasks if task == until]
            if whens:
                self.now = max(self.now, whens[0])
        self.at[name] = [task for when, task in self.tasks if when <= self.now]
        self.tasks = [pair for pair in self.tasks if pair[0] > self.now]


def at_point(plan, run, count, index, name, extra=None):
    for k in range(count):
        tasks = plan.at.get((name, k), [])
        if tasks:
            condition = index == k
            if extra is not None:
                condition = jnp.logical_and(condition, extra)

            @pl.when(condition)
            def _():
                for task in tasks:
                    run(*task)


def key_window(block, blocks, span):
    return max(0, block - 1) * span, min(blocks, block + 2) * span


def fold(values):
    return jnp.sum(values.reshape(-1, 8, values.shape[-1]), axis=0)


def make_mask(mask, segments, start):
    def step(r, carry):
        row = segments[pl.ds(start + r, 1), :].astype(jnp.float32)
        col = jnp.broadcast_to(row, (8, row.shape[1])).T[:, :1]
        mask[r] = jnp.where(col == row, 0.0, -1.0e9)
        return carry

    lax.fori_loop(0, mask.shape[0], step, 0)


def forward_kernel(groups, parts, *refs):
    (first, w_hidden, w_project, inputs, cot_in, segments) = refs[:6]
    biases, vectors = refs[6:9], refs[9:15]
    (out, dz_out, h_out, qkv_out, mixed_out, g_out, gp_out, lse_out, w0_out, w1_out, w2_out, sums) = refs[15:27]
    (held0, held1, held2, small_all, tok, mask, hacc, facc, yb, qkv, mixed, act, slope, lse, cot, small, rows) = refs[27:44]
    (load_sem, store_sem, z_send, z_recv, x_send, x_recv, s_send, s_recv) = refs[44:]
    me = Place(groups, parts)
    n = me.count
    wide, width = jnp.float32, tok.shape[1]
    count, seq = tok.shape[0], mask.shape[1]
    split = mixed.shape[2]
    heads = split // HD
    shards, held, weights = (first, w_hidden, w_project), (held0, held1, held2), (w0_out, w1_out, w2_out)
    half = width // 2
    bits_order = orders(n)
    loads, stores = [], []

    def load(src, dst):
        loads.append(pltpu.make_async_copy(src, dst, load_sem.at[len(loads)]))
        loads[-1].start()

    def store(src, dst, slot):
        return pltpu.make_async_copy(src, dst, store_sem.at[slot])

    load(first, held0.at[me.t])
    load(inputs.at[pl.ds(me.t * count, count)], tok)
    load(w_hidden, held1.at[me.t])
    load(w_project, held2.at[me.t])
    load(cot_in, cot)

    def line(ref):
        return ref[...].astype(wide).reshape(1, -1)

    gap = jnp.zeros((1, split), wide)
    lines = [jnp.concatenate([line(biases[0]), gap, line(biases[1]), gap], axis=1), line(biases[2])]
    lines.append(jnp.zeros((small.shape[0] - 2, width), wide))
    small[...] = jnp.concatenate(lines, axis=0).astype(LOW)
    for k, ref in enumerate(vectors):
        rows[k : k + 1, :] = line(ref)
    for k in (1, 2):
        sums[2 + k : 3 + k, :] = rows[k : k + 1, :]
    me.enter()
    mine = me.pieces(())
    away = [0, 1] + list(range(groups - 1, 1, -1))
    turn = [(0, j) for j in away[1:]]
    turn += [(a, j) for j in away[1:] for a in (1, 2)]
    units = len(turn)
    hops, doubles, tiny = {}, {}, []
    for j in range(1, groups):
        tiny.append(send(small, small_all.at[me.t], (s_send, s_recv), j - 1, me.along(j)))
        tiny[-1].start()
    for u, (a, j) in enumerate(turn):
        hops[u] = send(shards[a].at[mine], held[a].at[(me.t,) + mine], (z_send, z_recv), u, me.along(j))
        hops[u].start()
    for u, (a, j) in enumerate(turn):
        source = (me.t + groups - j) % groups
        stores.append(store(held[a].at[source], weights[a].at[source], u))
        for stage in range(n):
            for h in range(2 if stage < n - 1 else 1):
                if stage == n - 1:
                    bit, done, cols = 0, set(range(1, n)), slice(None)
                else:
                    bit, done = bits_order[h][stage], set(bits_order[h][:stage])
                    cols = pl.ds(h * half, half)
                view = (source,) + me.pieces(done) + (slice(None), cols)
                slot = (u * n + stage) * 2 + h
                doubles[u, stage, h] = send(
                    held[a].at[view], held[a].at[view], (x_send, x_recv), slot, me.partner(bit)
                )

    def advance(u, stage):
        for h in range(2):
            if stage == 0:
                if h == 0:
                    hops[u].wait_recv()
            elif (u, stage - 1, h) in doubles:
                doubles[u, stage - 1, h].wait_recv()
        if stage == n:
            stores[u].start()
        for h in range(2):
            if (u, stage, h) in doubles:
                doubles[u, stage, h].start()

    plan = Plan()
    for u in range(units):
        for stage in range(n + 1):
            plan.add(HOP[0] + HOP[1] * u + HOP[2] * stage, (u, stage))
    for j in range(groups):
        plan.point(("start", j), 0.0, (turn.index((0, away[j])), n) if j else None)
        plan.point(("project", j), 1.8)
        plan.point(("attend", j), 1.7)
        plan.point(("combine", j), 1.7)
        plan.point(("combined", j), 1.0)
    plan.point(("norm", 0), 1.5)
    for j in range(groups):
        plan.point(("up", j), 0.0, (turn.index((1, away[j])), n) if j else None)
        plan.point(("upped", j), 1.8)
        plan.point(("down", j), 1.8, (turn.index((2, away[j])), n) if j else None)
        plan.point(("downed", j), 1.3)
        plan.point(("next", j), 1.3)

    def run(index, name, extra=None):
        at_point(plan, advance, groups, index, name, extra)

    def group(j):
        return (me.t + groups - jnp.where(j <= 1, j, groups + 1 - j)) % groups

    def weight(a, g):
        return held[a][g].reshape(width, width)

    def project(g):
        bias = small_all[g, 0:1, : 3 * split].astype(wide)

        def body(r):
            total = matmul_t(tok[r, :], weight(0, g)[: 3 * split])
            qkv[g, r, :] = (total + bias).astype(LOW)

        row_tiles(count, TILE, body)

    span = 128
    blocks = seq // span
    factor = SCORE * HD ** (-0.5)

    def attend(g, hook):
        def packed_row(p, carry):
            base = p * seq

            def at(lo, hi):
                return pl.ds(pl.multiple_of(base + lo, span), hi - lo)

            turned = qkv[g, at(0, seq), 2 * split :].T
            for b in range(blocks):
                lo, hi = key_window(b, blocks, span)
                here = (b * span, (b + 1) * span)
                bias = mask[p, lo:hi, here[0] : here[1]]
                scores, sums_e, mixes = [], [], []
                for h in range(heads):
                    q = qkv[g, at(*here), h * HD : (h + 1) * HD]
                    k = qkv[g, at(lo, hi), split + h * HD : split + (h + 1) * HD]
                    scores.append(matmul_t(k, q))
                for h in range(heads):
                    s = scores[h] * factor + bias
                    top = jnp.max(s, axis=0, keepdims=True)
                    e = jnp.exp2(s - top)
                    total = jnp.sum(e, axis=0, keepdims=True)
                    lse[g, p * blocks + b, h : h + 1, :] = top + jnp.log(total) * SCORE
                    sums_e.append((e.astype(LOW), total))
                for h in range(heads):
                    e, total = sums_e[h]
                    o = jnp.dot(turned[h * HD : (h + 1) * HD, lo:hi], e, preferred_element_type=wide)
                    mixes.append(o * (1.0 / total))
                mixed[g, at(*here), :] = jnp.concatenate(mixes, axis=0).T.astype(LOW)
            hook(p)
            return carry

        lax.fori_loop(0, count // seq, packed_row, 0)

    def combine(g):
        def body(r):
            hacc[r, :] = hacc[r, :] + jnp.dot(
                mixed[g, r, :], weight(0, g)[3 * split :], preferred_element_type=wide
            )

        row_tiles(count, TILE, body)

    def start_sum():
        def body(r):
            hacc[r, :] = tok[r, :].astype(wide) + rows[0:1]

        row_tiles(count, TILE, body)

    def first_norm():
        def body(r):
            y, _, _ = norm_forward(hacc[r, :], rows[1:2], rows[2:3])
            yb[r, :] = y.astype(LOW)
            facc[r, :] = y + rows[5:6]

        row_tiles(count, 64, body)

    def ffn_up(g, hook):
        bias = small_all[g, 1:2, :].astype(wide)

        def body(r):
            u = jnp.dot(yb[r, :], weight(1, g), preferred_element_type=wide) + bias
            below = 0.5 + 0.5 * lax.erf(u * root_half)
            act[g, r, :] = (u * below).astype(LOW)
            bell = jnp.exp2(u * u * (-0.5 * SCORE)) * 0.3989422804014327
            slope[g, r, :] = (below + u * bell).astype(LOW)

        row_tiles(count, TILE, body, hook)

    def ffn_down(g, hook):
        def body(r):
            facc[r, :] = facc[r, :] + jnp.dot(act[g, r, :], weight(2, g), preferred_element_type=wide)

        row_tiles(count, TILE, body, hook)

    def last_norm():
        def step(i, carry):
            r = pl.ds(pl.multiple_of(i * 64, 64), 64)
            y, scaled, inverse = norm_forward(facc[r, :], rows[3:4], rows[4:5])
            tok[r, :] = y.astype(LOW)
            grad = cot[r, :].astype(wide)
            dz = norm_backward(grad, scaled, inverse, rows[3:4])
            facc[r, :] = dz
            return (
                carry[0] + fold(grad * scaled),
                carry[1] + fold(grad),
                carry[2] + fold(dz.astype(LOW).astype(wide)),
            )

        zero = jnp.zeros((8, width), wide)
        found = lax.fori_loop(0, count // 64, step, (zero, zero, zero))
        for i in range(3):
            sums[i : i + 1, :] = jnp.sum(found[i], axis=0, keepdims=True)

    small_all[me.t] = small[...]
    make_mask(mask, segments, me.t * mask.shape[0])
    loads[0].wait()
    loads[1].wait()
    half_way = count // TILE // 2 - 1
    start_sum()

    def attend_stores(g, j):
        return [
            store(a.at[g], b.at[g], units + groups * i + j)
            for i, (a, b) in enumerate(((qkv, qkv_out), (mixed, mixed_out), (lse, lse_out)))
        ]

    def ffn_stores(g, j):
        return [
            store(a.at[g], b.at[g], units + groups * (3 + i) + j)
            for i, (a, b) in enumerate(((act, g_out), (slope, gp_out)))
        ]

    def attend_group(j, carry):
        @pl.when(j == 1)
        def _():
            for t in tiny:
                t.wait()

        g = group(j)
        run(j, "start")
        project(g)
        run(j, "project")
        attend(g, lambda p: run(j, "attend", p == 0))
        run(j, "combine")
        combine(g)
        for copy in attend_stores(g, j):
            copy.start()
        run(j, "combined")
        return carry

    def ffn_group(j, carry):
        g = group(j)
        run(j, "up")
        ffn_up(g, lambda i: run(j, "upped", i == half_way))
        run(j, "down")
        ffn_down(g, lambda i: run(j, "downed", i == half_way))
        for copy in ffn_stores(g, j):
            copy.start()
        run(j, "next")
        return carry

    lax.fori_loop(0, groups, attend_group, 0)
    for i in range(2, 5):
        loads[i].wait()
    first_norm()
    base = units + 5 * groups
    others = [store(hacc, h_out, base)]
    others[0].start()
    for task in plan.at["norm", 0]:
        advance(*task)
    lax.fori_loop(0, groups, ffn_group, 0)
    for _, task in plan.tasks:
        advance(*task)
    last_norm()
    others += [store(tok, out, base + 1), store(facc, dz_out, base + 2)]
    for a in range(3):
        others.append(store(held[a].at[me.t], weights[a].at[me.t], base + 3 + a))
    for copy in others[1:]:
        copy.start()
    stores += others
    for j in range(groups):
        stores += attend_stores(group(j), j) + ffn_stores(group(j), j)
    for copy in hops.values():
        copy.wait_send()
    for copy in doubles.values():
        copy.wait_send()
    for copy in stores:
        copy.wait()


def forward(shards, inputs, cotangent, biases, vectors, segments, groups, parts):
    n = parts.bit_length() - 1
    width, count = inputs.shape[1], cotangent.shape[0]
    split = width // groups
    shape = (2,) * n + (width // parts, width)
    seq = segments.shape[1]
    packed = count // seq
    units = 3 * (groups - 1)
    anywhere, vmem = pl.BlockSpec(memory_space=pl.ANY), pl.BlockSpec(memory_space=pltpu.VMEM)
    wide = jnp.float32

    def made(*dims):
        return lambda kind, dtype: kind(dims, dtype)

    tokens, grouped = made(count, width), made(groups, count, width)
    layout = [
        (tokens, LOW),
        (tokens, wide),
        (tokens, wide),
        (made(groups, count, 3 * split), LOW),
        (made(groups, count, split), LOW),
        (grouped, LOW),
        (grouped, LOW),
        (made(groups, packed * seq // 128, 8, 128), wide),
    ] + [(made(groups, *shape), LOW)] * 3 + [(made(8, width), wide)]
    dma = pltpu.SemaphoreType.DMA
    outs = pl.pallas_call(
        functools.partial(forward_kernel, groups, parts),
        out_shape=[f(jax.ShapeDtypeStruct, dtype) for f, dtype in layout],
        in_specs=[anywhere] * 5 + [vmem] * 10,
        out_specs=[anywhere] * (len(layout) - 1) + [vmem],
        scratch_shapes=[pltpu.VMEM((groups,) + shape, LOW)] * 3
        + [
            pltpu.VMEM((groups, 16, width), LOW),
            pltpu.VMEM((count, width), LOW),
            pltpu.VMEM((packed, seq, seq), wide),
            pltpu.VMEM((count, width), wide),
            pltpu.VMEM((count, width), wide),
            pltpu.VMEM((count, width), LOW),
            pltpu.VMEM((groups, count, 3 * split), LOW),
            pltpu.VMEM((groups, count, split), LOW),
            pltpu.VMEM((groups, count, width), LOW),
            pltpu.VMEM((groups, count, width), LOW),
            pltpu.VMEM((groups, packed * seq // 128, 8, 128), wide),
            pltpu.VMEM((count, width), LOW),
            pltpu.VMEM((16, width), LOW),
            pltpu.VMEM((8, width), wide),
            dma((5,)),
            dma((units + 5 * groups + 6,)),
            dma((units,)),
            dma((units,)),
            dma((units * n * 2,)),
            dma((units * n * 2,)),
            dma((groups - 1,)),
            dma((groups - 1,)),
        ],
        compiler_params=pltpu.CompilerParams(
            collective_id=2, has_side_effects=True, vmem_limit_bytes=63 << 20
        ),
        name="gather_and_forward",
    )(
        *[s.reshape(shape) for s in shards],
        inputs,
        cotangent,
        segments,
        *biases,
        *vectors,
    )
    weights = [w.reshape(groups, width, width) for w in outs[8:11]]
    return outs[:8], weights, outs[11]


def backward_kernel(groups, parts, *refs):
    (dz_in, h_in, qkv_in, mixed_in, act_in, slope_in, lse_in, w0_in, w1_in, w2_in, inputs) = refs[:11]
    segments, sums = refs[11:13]
    gi_out, out0, out1, out2, vec_out = refs[13:18]
    (held0, held1, held2, landing, final) = refs[18:23]
    (w_buf, d_buf, act, slope, grad, low, low_t, row_t, du, hid, mask, qkv, mixed, lse, dmix, dqkv) = refs[23:39]
    (vec, vec_sum, vec_land) = refs[39:42]
    (load_sem, x_send, x_recv, z_send, z_recv, v_send, v_recv) = refs[42:49]
    halves = refs[49:]
    me = Place(groups, parts)
    n = me.count
    wide, width = jnp.float32, du.shape[1]
    count, seq = du.shape[0], mask.shape[1]
    split = mixed.shape[2]
    heads = split // HD
    held = (held0, held1, held2)
    half = width // 2
    bits_order = orders(n)
    turn = [(a, i) for i in range(groups) for a in (2, 1)] + [(0, i) for i in range(groups)]
    slots = list(range(2 * groups)) + [2 * groups + 1 + 2 * i for i in range(groups)]
    units = len(turn)

    def load(slot, src, dst):
        return pltpu.make_async_copy(src, dst, load_sem.at[slot])

    def group(i):
        return (me.t + 1 + i) % groups

    def load_ffn(i):
        g, s = group(i), i % 2
        pairs = ((slope_in, slope), (w2_in, d_buf), (w1_in, w_buf), (act_in, act))
        return [load(4 + 4 * i + k, a.at[g], b.at[s]) for k, (a, b) in enumerate(pairs)]

    def load_heads(i):
        g, s = group(i), i % 2
        pairs = ((w0_in, w_buf.at[(groups + i) % 2]), (qkv_in, qkv.at[s]), (mixed_in, mixed.at[s]), (lse_in, lse.at[s]))
        return [load(4 + 4 * groups + 4 * i + k, a.at[g], b) for k, (a, b) in enumerate(pairs)]

    def start(copies):
        for copy in copies:
            copy.start()

    def finish_all(copies):
        for copy in copies:
            copy.wait()

    entry = [load(0, dz_in, grad), load(1, h_in, hid)]
    start(entry)
    start(load_ffn(0))
    me.enter()
    copies, hops, tiny = {}, {}, {}

    def advance_vectors(stage):
        source = vec if stage == 0 else vec_sum.at[stage - 1]
        if stage:
            tiny[stage - 1].wait_recv()
            before = vec[...] if stage == 1 else vec_sum[stage - 2]
            vec_sum[stage - 1] = before + vec_land[stage - 1]
        peers = [me.partner(stage)] if stage < n else [me.along(j) for j in range(1, groups)]
        for k, peer in enumerate(peers):
            copy = send(source, vec_land.at[stage + k], (v_send, v_recv), stage + k, peer)
            copy.start()
            tiny[stage + k] = copy

    for u, (a, i) in enumerate(turn):
        target = group(i)
        copies[u, 0, 0] = send(
            held[a].at[(target,) + me.pieces(set(range(1, n)), 0)],
            landing.at[u],
            (x_send, x_recv),
            u * 2 * n,
            me.partner(0),
        )
        for stage in range(1, n):
            for h in range(2):
                bits = bits_order[h]
                bit, left = bits[stage - 1], set(bits[stage:])
                copies[u, stage, h] = send(
                    held[a].at[(target,) + me.pieces(left, bit) + (slice(None), pl.ds(h * half, half))],
                    halves[stage - 1].at[u, h],
                    (x_send, x_recv),
                    u * 2 * n + stage * 2 + h,
                    me.partner(bit),
                )
        if i < groups - 1:
            slot = a * (groups - 1) + i
            hops[slot] = send(
                held[a].at[(target,) + me.pieces(())], final.at[slot], (z_send, z_recv), slot, me.along(i + 1)
            )

    def advance(u, stage):
        a, i = turn[u]
        target = group(i)
        for h in range(2):
            if (u, stage - 1, h) not in copies:
                continue
            if stage == 1:
                left, cols, source = set(range(1, n)), slice(None), landing.at[u]
            else:
                left, cols = set(bits_order[h][stage - 1 :]), pl.ds(h * half, half)
                source = halves[stage - 2].at[u, h]
            copies[u, stage - 1, h].wait_recv()
            view = (target,) + me.pieces(left) + (slice(None), cols)
            add_into(held[a].at[view], source, [2] * len(left))
        if stage == n and i < groups - 1:
            hops[a * (groups - 1) + i].start()
        for h in range(2):
            if (u, stage, h) in copies:
                copies[u, stage, h].start()

    plan = Plan()
    before = [-100.0] * (n + 1)

    def made(u):
        for stage in range(n + 1):
            when = plan.now + PASS[0] * stage
            if stage:
                when = max(when, before[stage] + PASS[1], before[stage - 1] + PASS[0])
            before[stage] = when
            plan.add(when, (u, stage))

    for i in range(groups):
        plan.now += 2.8
        made(2 * i)
        plan.point(("down", i), 0.0)
        plan.point(("back", i), 2.8)
        plan.point(("backed", i), 2.8)
        plan.now += 2.8
        made(2 * i + 1)
        plan.point(("up", i), 0.0)
    plan.point(("norm", 0), 3.0)
    plan.point(("norm", 1), 2.0)
    for i in range(groups):
        plan.point(("mix", i), 1.0)
        plan.point(("attend", i), 3.0)
        plan.point(("attended", i), 3.0)
        plan.now += 2.8
        made(2 * groups + i)
        plan.point(("first", i), 0.0)
        plan.point(("finish", i), 2.2)

    def run(index, name, extra=None):
        at_point(plan, advance, groups, index, name, extra)

    def put(a, g, cols, value):
        shape = held[a].shape[1:-1] + value.shape[1:]
        held[a][(g,) + (slice(None),) * (n + 1) + (cols,)] = value.astype(LOW).reshape(shape)

    def products(a, g, left, right):
        def step(i, carry):
            cols = pl.ds(pl.multiple_of(i * TILE, TILE), TILE)
            put(a, g, cols, jnp.dot(left[...], right[:, cols], preferred_element_type=wide))
            return carry

        lax.fori_loop(0, width // TILE, step, 0)

    def flip(dst, r, value):
        dst[:, r] = value.T

    vec[...] = jnp.zeros_like(vec)
    finish_all(entry)

    def prepare(i, carry):
        r = pl.ds(pl.multiple_of(i * 128, 128), 128)
        g = grad[r, :].astype(LOW)
        low[r, :] = g
        flip(low_t, r, g)
        y, _, _ = norm_forward(hid[r, :], sums[3:4], sums[4:5])
        flip(row_t, r, y.astype(LOW))
        return carry

    lax.fori_loop(0, count // 128, prepare, 0)
    make_mask(mask, segments, me.t * mask.shape[0])

    half_way = count // TILE // 2 - 1

    def ffn_group(i, outer):
        g, s = group(i), i % 2

        @pl.when(i + 1 < groups)
        def _():
            start(load_ffn(i + 1))

        @pl.when(i + 1 == groups)
        def _():
            start(load_heads(0))

        finish_all(load_ffn(i))
        products(2, g, low_t, act.at[s])
        run(i, "down")

        def back(k, carry):
            r = pl.ds(pl.multiple_of(k * TILE, TILE), TILE)
            part = matmul_t(low[r, :], d_buf[s])
            part = (part * slope[s, r, :].astype(wide)).astype(LOW)
            du[r, :] = part
            grad[r, :] = grad[r, :] + matmul_t(part, w_buf[s])
            run(i, "back", k == half_way)
            return carry + fold(part.astype(wide))

        total = lax.fori_loop(0, count // TILE, back, jnp.zeros((8, width), wide))
        vec[pl.ds(groups + g, 1), :] = jnp.sum(total, axis=0, keepdims=True)
        run(i, "backed")
        products(1, g, row_t, du)
        run(i, "up")
        return outer

    lax.fori_loop(0, groups, ffn_group, 0)
    tokens = load(2, inputs.at[pl.ds(me.t * count, count)], du)
    tokens.start()

    def norm(i, carry):
        r = pl.ds(pl.multiple_of(i * 64, 64), 64)
        _, scaled, inverse = norm_forward(hid[r, :], sums[3:4], sums[4:5])
        dy = grad[r, :]
        dh = norm_backward(dy, scaled, inverse, sums[3:4])
        dh_low = dh.astype(LOW)
        grad[r, :] = dh
        low[r, :] = dh_low
        return (carry[0] + fold(dy * scaled), carry[1] + fold(dy), carry[2] + fold(dh_low.astype(wide)))

    zero = jnp.zeros((8, width), wide)
    found = lax.fori_loop(0, count // 64, norm, (zero, zero, zero))
    for k in range(3):
        vec[2 * groups + k : 2 * groups + k + 1, :] = jnp.sum(found[k], axis=0, keepdims=True)
    vec[2 * groups + 3 : 2 * groups + 6, :] = sums[0:3, :]
    for task in plan.at["norm", 0]:
        advance(*task)
    tokens.wait()

    def turn_over(i, carry):
        r = pl.ds(pl.multiple_of(i * 128, 128), 128)
        flip(low_t, r, low[r, :])
        flip(row_t, r, du[r, :])
        return carry

    lax.fori_loop(0, count // 128, turn_over, 0)
    for task in plan.at["norm", 1]:
        advance(*task)

    span = 128
    blocks = seq // span
    scale = HD ** (-0.5)

    def heads_group(i, outer):
        g, s, ws = group(i), i % 2, (groups + i) % 2

        @pl.when(i + 1 < groups)
        def _():
            start(load_heads(i + 1))

        finish_all(load_heads(i))

        def mix(k, carry):
            r = pl.ds(pl.multiple_of(k * TILE, TILE), TILE)
            dmix[r, :] = matmul_t(low[r, :], w_buf[ws, 3 * split :, :]).astype(LOW)
            return carry

        lax.fori_loop(0, count // TILE, mix, 0)
        run(i, "mix")

        def packed_row(p, carry):
            base = p * seq

            def at(lo, hi):
                return pl.ds(pl.multiple_of(base + lo, span), hi - lo)

            turned = qkv[s, at(0, seq), split : 2 * split].T
            dks = [[None] * heads for _ in range(blocks)]
            dvs = [[None] * heads for _ in range(blocks)]
            dqs = []

            def gather_sum(total, lo, h, value):
                for c in range(value.shape[0] // span):
                    piece = value[c * span : (c + 1) * span]
                    old = total[lo // span + c][h]
                    total[lo // span + c][h] = piece if old is None else old + piece

            def write(b):
                parts_b = [dqs[b]] + [x * scale for x in dks[b]] + dvs[b]
                dqkv[at(b * span, (b + 1) * span), :] = jnp.concatenate(parts_b, axis=1).astype(LOW)

            for b in range(blocks):
                lo, hi = key_window(b, blocks, span)
                here = (b * span, (b + 1) * span)
                bias = mask[p, lo:hi, here[0] : here[1]]
                work, grads = [], []
                for h in range(heads):
                    q = qkv[s, at(*here), h * HD : (h + 1) * HD]
                    k = qkv[s, at(lo, hi), split + h * HD : split + (h + 1) * HD]
                    v = qkv[s, at(lo, hi), 2 * split + h * HD : 2 * split + (h + 1) * HD]
                    do = dmix[at(*here), h * HD : (h + 1) * HD]
                    work.append((q, do, matmul_t(k, q), matmul_t(v, do)))
                for h in range(heads):
                    q, do, score, dp = work[h]
                    prob = jnp.exp2(score * (SCORE * scale) + bias - lse[s, p * blocks + b, h : h + 1, :])
                    inner = jnp.sum(prob * dp, axis=0, keepdims=True)
                    grads.append((prob.astype(LOW), (prob * (dp - inner)).astype(LOW)))
                dq = []
                for h in range(heads):
                    q, do, _, _ = work[h]
                    prob, ds = grads[h]
                    gather_sum(dvs, lo, h, jnp.dot(prob, do, preferred_element_type=wide))
                    gather_sum(dks, lo, h, jnp.dot(ds, q, preferred_element_type=wide))
                    dq.append(jnp.dot(turned[h * HD : (h + 1) * HD, lo:hi], ds, preferred_element_type=wide))
                dqs.append(jnp.concatenate(dq, axis=0).T * scale)
                if b:
                    write(b - 1)
            write(blocks - 1)
            run(i, "attend", p == 0)
            return carry

        lax.fori_loop(0, count // seq, packed_row, 0)
        run(i, "attended")

        def first_cols(k, carry):
            cols = pl.ds(pl.multiple_of(k * TILE, TILE), TILE)
            put(0, g, cols, jnp.dot(row_t[...], dqkv[:, cols], preferred_element_type=wide))
            return carry

        edge = 3 * split // TILE * TILE
        lax.fori_loop(0, edge // TILE, first_cols, 0)
        tail = jnp.concatenate(
            [
                jnp.dot(row_t[...], dqkv[:, edge:], preferred_element_type=wide),
                jnp.dot(low_t[...], mixed[s], preferred_element_type=wide),
            ],
            axis=1,
        )
        put(0, g, slice(edge, width), tail)
        run(i, "first")

        def finish(k, carry):
            r = pl.ds(pl.multiple_of(k * TILE, TILE), TILE)
            part = dqkv[r, :]
            grad[r, :] = grad[r, :] + jnp.dot(part, w_buf[ws, : 3 * split, :], preferred_element_type=wide)
            return carry + fold(part.astype(wide))

        total = lax.fori_loop(0, count // TILE, finish, jnp.zeros((8, 3 * split), wide))
        vec[pl.ds(g, 1), : 3 * split] = jnp.sum(total, axis=0, keepdims=True)
        run(i, "finish")
        return outer

    lax.fori_loop(0, groups, heads_group, 0)
    result = load(3, grad, gi_out)
    result.start()
    rest = [task for _, task in plan.tasks]
    for stage in range(n + 1):
        advance_vectors(stage)
        for task in rest[:2] if stage < n else rest:
            advance(*task)
        rest = rest[2:]
    total = vec_sum[n - 1]
    for j in range(groups - 1):
        tiny[n + j].wait_recv()
        total = total + vec_land[n + j]
    vec_out[...] = total
    for a, out in ((2, out2), (1, out1), (0, out0)):
        total = held[a][(me.t,) + me.pieces(())].astype(wide)
        for j in range(groups - 1):
            slot = a * (groups - 1) + j
            hops[slot].wait_recv()
            total = total + final[slot].astype(wide)
        out[...] = total
    for copy in list(tiny.values()) + list(copies.values()) + list(hops.values()):
        copy.wait_send()
    result.wait()


def backward(saved, weights, sums, inputs, segments, groups, parts):
    n = parts.bit_length() - 1
    _, dz, hid, qkv, mixed, act, slope, lse = saved
    count, width = dz.shape
    split = width // groups
    piece = width // parts
    shape = (groups,) + (2,) * n + (piece, width)
    seq = segments.shape[1]
    packed = count // seq
    units = 3 * groups
    anywhere, vmem = pl.BlockSpec(memory_space=pl.ANY), pl.BlockSpec(memory_space=pltpu.VMEM)
    wide, dma = jnp.float32, pltpu.SemaphoreType.DMA
    lines = -(-(2 * groups + 6) // 8) * 8
    return pl.pallas_call(
        functools.partial(backward_kernel, groups, parts),
        out_shape=[jax.ShapeDtypeStruct((count, width), wide)]
        + [jax.ShapeDtypeStruct((piece, width), wide)] * 3
        + [jax.ShapeDtypeStruct((lines, width), wide)],
        in_specs=[anywhere] * 11 + [vmem] * 2,
        out_specs=[anywhere] + [vmem] * 4,
        scratch_shapes=[pltpu.VMEM(shape, LOW)] * 3
        + [
            pltpu.VMEM((units,) + (2,) * (n - 1) + (piece, width), LOW),
            pltpu.VMEM((3 * (groups - 1), piece, width), LOW),
            pltpu.VMEM((2, width, width), LOW),
            pltpu.VMEM((2, width, width), LOW),
            pltpu.VMEM((2, count, width), LOW),
            pltpu.VMEM((2, count, width), LOW),
            pltpu.VMEM((count, width), wide),
            pltpu.VMEM((count, width), LOW),
            pltpu.VMEM((width, count), LOW),
            pltpu.VMEM((width, count), LOW),
            pltpu.VMEM((count, width), LOW),
            pltpu.VMEM((count, width), wide),
            pltpu.VMEM((packed, seq, seq), wide),
            pltpu.VMEM((2, count, 3 * split), LOW),
            pltpu.VMEM((2, count, split), LOW),
            pltpu.VMEM((2, count // 128, 8, 128), wide),
            pltpu.VMEM((count, split), LOW),
            pltpu.VMEM((count, 3 * split), LOW),
            pltpu.VMEM((lines, width), wide),
            pltpu.VMEM((n, lines, width), wide),
            pltpu.VMEM((n + groups - 1, lines, width), wide),
            dma((8 * groups + 4,)),
            dma((units * 2 * n,)),
            dma((units * 2 * n,)),
            dma((3 * (groups - 1),)),
            dma((3 * (groups - 1),)),
            dma((n + groups - 1,)),
            dma((n + groups - 1,)),
        ]
        + [pltpu.VMEM((units, 2) + (2,) * (n - 1 - s) + (piece, width // 2), LOW) for s in range(1, n)],
        compiler_params=pltpu.CompilerParams(
            collective_id=3, has_side_effects=True, vmem_limit_bytes=67043328
        ),
        name="backward_and_scatter",
    )(dz, hid, qkv, mixed, act, slope, lse, *weights, inputs, segments, sums)


def pick(values, size, index):
    total = jnp.zeros((values.shape[0], size), values.dtype)
    for k in range(values.shape[1] // size):
        total = jnp.where(index == k, values[:, k * size : (k + 1) * size], total)
    return total


def outputs_kernel(groups, parts, *refs):
    out_in, gi_in, first, up, down, vec = refs[:6]
    out, gi, g_query, g_key, g_value, g_output, g_hidden, g_project, bias_qv, bias_h, vectors = refs[6:17]
    held_out, held_gi, load_sem, store_sem = refs[17:]
    t, d = lax.axis_index("tensor"), lax.axis_index("dp")
    count, width = held_gi.shape
    split, piece = width // groups, HD // parts
    size = count // 4
    loads, stores = [], []
    for k in range(4):
        r = pl.ds(k * size, size)
        for a, b, c in ((gi_in, held_gi, gi), (out_in, held_out, out)):
            loads.append(pltpu.make_async_copy(a.at[r], b.at[r], load_sem.at[len(loads)]))
            stores.append(pltpu.make_async_copy(b.at[r], c.at[r], store_sem.at[len(stores)]))
            loads[-1].start()
    for k, target in enumerate((g_query, g_key, g_value)):
        target[...] = first[:, k * split : (k + 1) * split]
    g_output[...] = first[:, 3 * split :].T
    g_hidden[...] = up[...]
    g_project[...] = down[...]
    for a, b in zip(loads, stores):
        a.wait()
        b.start()
    own, hidden = vec[pl.ds(t, 1), :], vec[pl.ds(groups + t, 1), :]
    heads = split // HD
    pieces = [own[:, k * HD : (k + 1) * HD] for k in range(heads)]
    pieces += [own[:, 2 * split + k * HD : 2 * split + (k + 1) * HD] for k in range(heads)]
    pieces += [hidden[:, k * HD : (k + 1) * HD] for k in range(width // HD)]
    found = pick(jnp.concatenate(pieces, axis=0), piece, d)
    for h in range(heads):
        bias_qv[h] = jnp.concatenate([found[h : h + 1], found[heads + h : heads + h + 1]], axis=0)
    bias_h[...] = found[2 * heads :].T
    vectors[...] = pick(vec[2 * groups : 2 * groups + 6, :], width // (parts * groups), d * groups + t)
    for b in stores:
        b.wait()


def finish_outputs(output, grad_input, first, up, down, vec, groups, parts):
    (count, width), (piece, _) = grad_input.shape, first.shape
    split, wide = width // groups, jnp.float32
    shapes = [(count, width)] + [(piece, split)] * 3 + [(split, piece), (piece, width), (piece, width)]
    shapes += [(split // HD, 2, HD // parts), (HD // parts, width // HD), (6, width // (parts * groups))]
    anywhere, vmem = pl.BlockSpec(memory_space=pl.ANY), pl.BlockSpec(memory_space=pltpu.VMEM)
    return pl.pallas_call(
        functools.partial(outputs_kernel, groups, parts),
        out_shape=[jax.ShapeDtypeStruct((count, width), LOW)] + [jax.ShapeDtypeStruct(s, wide) for s in shapes],
        in_specs=[anywhere] * 2 + [vmem] * 4,
        out_specs=[anywhere] * 2 + [vmem] * 9,
        scratch_shapes=[
            pltpu.VMEM((count, width), LOW),
            pltpu.VMEM((count, width), wide),
            pltpu.SemaphoreType.DMA((8,)),
            pltpu.SemaphoreType.DMA((8,)),
        ],
        name="outputs",
    )(output, grad_input, first, up, down, vec)


def per_device_small(
    inputs,
    segments,
    w_query,
    w_key,
    w_value,
    b_query,
    b_value,
    w_output,
    b_output,
    gain_attn,
    shift_attn,
    w_hidden,
    b_hidden,
    w_project,
    b_project,
    gain_ffn,
    shift_ffn,
    cotangent,
):
    seq_len = segments.shape[1]
    share_tokens = cotangent.shape[0]
    share_rows = share_tokens // seq_len
    width = inputs.shape[1]
    groups, parts = lax.axis_size("tensor"), lax.axis_size("dp")
    place, part = lax.axis_index("tensor"), lax.axis_index("dp")
    low = jnp.bfloat16
    wide = jnp.float32

    tokens = lax.dynamic_slice_in_dim(inputs, place * share_tokens, share_tokens, 0)
    rows_segments = lax.dynamic_slice_in_dim(segments, place * share_rows, share_rows, 0)
    split = w_query.shape[1]
    small = jnp.concatenate([b_query, b_value, b_hidden]).reshape(-1, 128)
    small_rows = small.shape[0]
    small = jnp.pad(small, ((0, -small_rows % 16), (0, 0)))
    first = jnp.concatenate([w_query, w_key, w_value, w_output.T], axis=1)
    (first, w_up, w_down), small = gather([first, w_hidden, w_project], small, groups, parts)
    w_in = first[:, :, : 3 * split].reshape(groups, width, 3, split).transpose(1, 2, 0, 3)
    w_in = w_in.reshape(width, 3 * groups * split)
    w_out = first[:, :, 3 * split :].transpose(0, 2, 1).reshape(groups * split, width)
    w_up = w_up.transpose(1, 0, 2).reshape(width, -1)
    w_down = w_down.reshape(-1, width)
    small = small[:, :small_rows].reshape(groups, -1).astype(wide)
    bias_query = small[:, :split].reshape(-1)
    bias_value = small[:, split : 2 * split].reshape(-1)
    bias_hidden = small[:, 2 * split :].reshape(-1)
    full = groups * split
    head_shape = (share_rows, seq_len, full // HD, HD)

    attn_gain = gain_attn.astype(wide)
    attn_shift = shift_attn.astype(wide)
    attn_bias = b_output.astype(wide)
    ffn_gain = gain_ffn.astype(wide)
    ffn_shift = shift_ffn.astype(wide)
    ffn_bias = b_project.astype(wide)
    grad_out = cotangent.astype(wide)

    projected = jnp.dot(tokens, w_in, preferred_element_type=wide)
    queries = (projected[:, :full] + bias_query).astype(low)
    keys_in = projected[:, full : 2 * full].astype(low)
    values = (projected[:, 2 * full :] + bias_value).astype(low)
    query_heads = queries.reshape(head_shape)
    key_heads = keys_in.reshape(head_shape)
    value_heads = values.reshape(head_shape)
    mixed_heads, logsum = lax.map(attend_forward, (query_heads, key_heads, value_heads, rows_segments))
    mixed = mixed_heads.reshape(share_tokens, full)
    hidden = tokens.astype(wide) + (jnp.dot(mixed, w_out, preferred_element_type=wide) + attn_bias)
    normed, scaled, inverse = norm_forward(hidden, attn_gain, attn_shift)
    normed_low = normed.astype(low)
    hidden_pre = jnp.dot(normed_low, w_up, preferred_element_type=wide) + bias_hidden
    active, gelu_pull = jax.vjp(gelu_exact, hidden_pre)
    active_low = active.astype(low)
    block_sum = normed + (jnp.dot(active_low, w_down, preferred_element_type=wide) + ffn_bias)
    output, scaled_out, inverse_out = norm_forward(block_sum, ffn_gain, ffn_shift)
    grad_sum = norm_backward(grad_out, scaled_out, inverse_out, ffn_gain)
    grad_ffn_gain = jnp.sum(grad_out * scaled_out, axis=0)
    grad_ffn_shift = jnp.sum(grad_out, axis=0)
    grad_sum_low = grad_sum.astype(low)
    grad_ffn_bias = jnp.sum(grad_sum_low.astype(wide), axis=0)
    grad_active = times_transposed(grad_sum_low, w_down)
    grad_w_down = cross_rows(grad_sum_low, active_low)
    grad_hidden_pre = gelu_pull(grad_active)[0].astype(low)
    grad_b_hidden = jnp.sum(grad_hidden_pre.astype(wide), axis=0)
    grad_w_up = cross_rows(normed_low, grad_hidden_pre)
    grad_normed = grad_sum + times_transposed(grad_hidden_pre, w_up)
    grad_hidden = norm_backward(grad_normed, scaled, inverse, attn_gain)
    grad_hidden_low = grad_hidden.astype(low)
    grad_attn_gain = jnp.sum(grad_normed * scaled, axis=0)
    grad_attn_shift = jnp.sum(grad_normed, axis=0)
    grad_attn_bias = jnp.sum(grad_hidden_low.astype(wide), axis=0)
    grad_w_out = cross_rows(grad_hidden_low, mixed)
    grad_mixed = times_transposed(grad_hidden_low, w_out).astype(low).reshape(head_shape)
    grad_q, grad_k, grad_v = lax.map(
        attend_backward, (query_heads, key_heads, value_heads, rows_segments, logsum, grad_mixed)
    )
    grad_q = grad_q.reshape(share_tokens, full)
    grad_k = grad_k.reshape(share_tokens, full)
    grad_v = grad_v.reshape(share_tokens, full)
    grad_projected = jnp.concatenate([grad_q, grad_k, grad_v], axis=1)
    grad_w_in = cross_rows(tokens, grad_projected)
    grad_b_query = jnp.sum(grad_q.astype(wide), axis=0)
    grad_b_value = jnp.sum(grad_v.astype(wide), axis=0)
    grad_input = grad_hidden + times_transposed(grad_projected, w_in)

    def parted(grad):
        return grad.astype(low).reshape(width, groups, -1).transpose(1, 0, 2)

    first = jnp.concatenate(
        [parted(grad_w_in[:, i * full : (i + 1) * full]) for i in range(3)] + [parted(grad_w_out)], axis=2
    )
    vectors = jnp.concatenate(
        [
            jnp.stack([grad_b_query, grad_b_value]).reshape(2 * groups, split),
            grad_b_hidden.reshape(-1, split),
            jnp.stack(
                [
                    grad_attn_gain,
                    grad_attn_shift,
                    grad_attn_bias,
                    grad_ffn_gain,
                    grad_ffn_shift,
                    grad_ffn_bias,
                ]
            ).reshape(-1, split),
        ],
        axis=0,
    )
    count = vectors.size // split
    vectors = vectors.reshape(-1, 128)
    (sum_first, sum_up, sum_down, vectors) = scatter(
        [first, parted(grad_w_up), parted(grad_w_down)], vectors, groups, parts
    )
    vectors = vectors.reshape(count, split)
    bias_qv = vectors[: 2 * groups].reshape(2, groups, split // HD, HD)
    rest = vectors[2 * groups :]
    hid = bias_hidden.shape[0] // split
    bias_h = rest[:hid].reshape(groups, -1, HD)
    vec = rest[hid:].reshape(6, -1)
    piece = HD // parts
    bias_qv = lax.dynamic_slice_in_dim(bias_qv, place, 1, 1)[:, 0]
    bias_qv = lax.dynamic_slice_in_dim(bias_qv, part * piece, piece, 2)
    bias_h = lax.dynamic_slice_in_dim(bias_h, place, 1, 0)[0]
    bias_h = lax.dynamic_slice_in_dim(bias_h, part * piece, piece, 1)
    piece = width // (parts * groups)
    vec = lax.dynamic_slice_in_dim(vec, (part * groups + place) * piece, piece, 1)
    return (
        output.astype(low),
        grad_input,
        sum_first[:, :split],
        sum_first[:, split : 2 * split],
        sum_first[:, 2 * split : 3 * split],
        sum_first[:, 3 * split :].T,
        sum_up,
        sum_down.T,
        bias_qv,
        bias_h,
        vec,
    )


def per_device(
    inputs,
    segments,
    w_query,
    w_key,
    w_value,
    b_query,
    b_value,
    w_output,
    b_output,
    gain_attn,
    shift_attn,
    w_hidden,
    b_hidden,
    w_project,
    b_project,
    gain_ffn,
    shift_ffn,
    cotangent,
):
    if (inputs.shape[1] // lax.axis_size("dp")) % 16:
        return per_device_small(
            inputs, segments, w_query, w_key, w_value, b_query, b_value, w_output, b_output, gain_attn, shift_attn,
            w_hidden, b_hidden, w_project, b_project, gain_ffn, shift_ffn, cotangent,
        )
    width, split = w_query.shape
    groups, parts = lax.axis_size("tensor"), lax.axis_size("dp")
    biases = [b_query, b_value, b_hidden]
    shared = [b_output, gain_attn, shift_attn, gain_ffn, shift_ffn, b_project]
    first = jnp.concatenate([w_query.T, w_key.T, w_value.T, w_output], axis=0)
    saved, weights, sums = forward(
        [first, w_hidden, w_project], inputs, cotangent, biases, shared, segments, groups, parts
    )
    grad_input, sum_first, sum_up, sum_down, vectors = backward(
        saved, weights, sums, inputs, segments, groups, parts
    )
    found = finish_outputs(saved[0], grad_input, sum_first, sum_up, sum_down, vectors, groups, parts)
    return (*found[:7], found[7].T, found[8].transpose(1, 0, 2), found[9].T, found[10])


def solution(mesh):
    in_specs = (
        P("dp", None),
        P("dp", None),
        P(None, "tensor"),
        P(None, "tensor"),
        P(None, "tensor"),
        P("tensor"),
        P("tensor"),
        P("tensor", None),
        P(),
        P(),
        P(),
        P(None, "tensor"),
        P("tensor"),
        P("tensor", None),
        P(),
        P(),
        P(),
        P(("dp", "tensor"), None),
    )
    out_specs = (
        P(("dp", "tensor"), None),
        P(("dp", "tensor"), None),
        P("dp", "tensor"),
        P("dp", "tensor"),
        P("dp", "tensor"),
        P("tensor", "dp"),
        P("dp", "tensor"),
        P("tensor", "dp"),
        P(None, "tensor", "dp"),
        P("tensor", "dp"),
        P(None, ("dp", "tensor")),
    )
    return jax.shard_map(
        per_device, mesh=mesh, in_specs=in_specs, out_specs=out_specs, check_vma=False
    )
```
